128 devices in a mesh: phase: 8 (over y_hi, z), row: 16 (over x, y_lo, core).
Axes of the slice: x: 4, y: 4 (y_hi: 2, y_lo: 2; y = y_hi * 2 + y_lo), z: 4, core: 2. Of those that a mesh axis runs over, the one named last changes fastest.
Arguments:
- frames: float32 [2, 64, 256, 256], P(None, 'phase', 'row'), may hold values from -50 to 50
- auxiliary: float32 [2, 64, 256, 256], P(None, 'phase', 'row'), may hold values from -6 to 6
- scaled_dual: float32 [2, 64, 256, 256], P(None, 'phase', 'row'), may hold values from -3 to 3
- coil_maps: float32 [16, 2, 256, 256], P(None, None, 'row'), may hold values from -5 to 5
- measured: float32 [16, 2, 64, 256, 256], P(None, None, 'phase', 'row'), may hold values from -6 to 6
- sampling: int32 [64, 256], P('phase'), may hold values 0 or 1
Outputs:
- new_frames: float32 [2, 64, 256, 256], P(None, 'phase', 'row')
- new_aux: float32 [2, 64, 256, 256], P(None, 'phase', 'row')
- new_dual: float32 [2, 64, 256, 256], P(None, 'phase', 'row')
- residual_norms: float32 [2], replicated
The draws below stay inside these ranges and needn't reach their ends.
All inputs are finite; a program needn't handle non-finite values. No bound on the sum of `sampling` on one device may be relied on, other than what follows from the above.
Results may differ from the reference program's by a relative error of at most 0.003.
Values sent between devices are 32-bit elements; how exact they have to be, the bound alone decides.
No kernel may reach another device: no remote copies, remote signals or barrier semaphores. Data moves between devices by JAX's collectives and lax.ppermute only.
A program may use at most 256 MiB of HBM per device.

```python
import math
import jax
import jax.numpy as jnp
from jax import lax

NX = 256
NY = 256
COILS = 16
CG_STEPS = 2
PHASES = 64


def rough_scales(key, count, ramp, spread):
    position = jnp.arange(count, dtype=jnp.int32).astype(jnp.float32) / count
    jitter = jax.random.uniform(key, (count,), jnp.float32, 0.0, spread)
    return jnp.exp(ramp * position + jitter)


def draw_frames(key, part):
    subkeys = jax.random.split(jax.random.fold_in(key, 11), 4)
    shape = (2, PHASES, NX, NY)
    noise = jax.random.truncated_normal(subkeys[0], -4.0, 4.0, shape, jnp.float32)
    phase_scale = rough_scales(subkeys[1], PHASES, math.log(3.0), 0.3)
    row_scale = rough_scales(subkeys[2], NX, math.log(3.0), math.log(2.0))
    col_scale = rough_scales(subkeys[3], NY, 0.0, math.log(4.0))
    return noise * phase_scale[:, None, None] * row_scale[:, None] * col_scale / 8.0


def draw_coil_maps(key, part):
    subkeys = jax.random.split(jax.random.fold_in(key, 23), 3)
    shape = (COILS, 2, NX, NY)
    noise = jax.random.truncated_normal(subkeys[0], -4.0, 4.0, shape, jnp.float32)
    row_scale = rough_scales(subkeys[1], NX, math.log(3.0), math.log(2.0))
    col_scale = rough_scales(subkeys[2], NY, 0.0, math.log(4.0))
    return noise * 0.3 * row_scale[:, None] * col_scale / 6.0


def set_ends(values, stream_key, least, high):
    spot = [jax.random.randint(jax.random.fold_in(stream_key, axis), (), 0, length) for axis, length in enumerate(values.shape)]
    main_axis = values.shape.index(max(values.shape))
    next_to = spot[:main_axis] + [(spot[main_axis] + 1) % values.shape[main_axis]] + spot[main_axis + 1:]
    return values.at[tuple(spot)].set(least).at[tuple(next_to)].set(high)


def block_scale(own_key, extent, cuts, low, high):
    def one(axis_at, shards_of):
        steps = jax.random.uniform(jax.random.fold_in(jax.random.fold_in(own_key, 6), axis_at), (shards_of,), jnp.float32, low / len(cuts), high / len(cuts))
        return jnp.repeat(jnp.exp(steps), extent[axis_at] // shards_of).reshape((-1,) + (1,) * (len(extent) - axis_at - 1))

    level = one(*cuts[0])
    for cut in cuts[1:]:
        level = level * one(*cut)
    return level


def scatter_about(rng, shape, scale, bound, cuts=(), kind=jnp.bfloat16):
    factor_of = block_scale(rng, shape, cuts, -0.22, 0.18) if cuts else 1.0
    drawn = jax.random.normal(rng, shape, jnp.float32) * scale * factor_of
    return jnp.minimum(jnp.maximum(drawn, -bound), bound).astype(kind)


def setup_inputs(seed: int = 0) -> dict:
    arg_keys = jax.random.split(jax.random.key(seed), 7)
    frames = draw_frames(jax.random.fold_in(arg_keys[6], 71), 0)
    auxiliary = scatter_about(arg_keys[1], (2, PHASES, NX, NY), 1.0, 6.0, ((1, 8), (2, 16)), jnp.float32)
    scaled_dual = scatter_about(arg_keys[2], (2, PHASES, NX, NY), 0.5, 3.0, ((1, 8), (2, 16)), jnp.float32)
    coil_maps = draw_coil_maps(jax.random.fold_in(arg_keys[6], 71), 0)
    measured = scatter_about(arg_keys[4], (COILS, 2, PHASES, NX, NY), 1.0, 6.0, ((2, 8), (3, 16)), jnp.float32)
    sampling = set_ends((jax.random.randint(arg_keys[5], (PHASES, NX), 0, 2) < 1).astype(jnp.int32), jax.random.fold_in(arg_keys[5], 1), 0, 1)
    return {"frames": frames, "auxiliary": auxiliary, "scaled_dual": scaled_dual, "coil_maps": coil_maps, "measured": measured, "sampling": sampling}


EXACT = lax.Precision.HIGHEST
PENALTY = 0.5
DAMPING = 0.1
THRESHOLD = 1.0

def tables(count):
    indices = jnp.arange(count, dtype=jnp.int32)
    angles = (indices[:, None] * indices[None, :] % count).astype(jnp.float32) * (2.0 * math.pi / count)
    return (jnp.cos(angles) / math.sqrt(count), jnp.sin(angles) / math.sqrt(count))

def apply_rows(table, values):
    return jnp.einsum('kx,...xy->...ky', table, values, precision=EXACT)

def forward(real_part, imag_part, cosine, sine_table):
    return (apply_rows(cosine, real_part) + apply_rows(sine_table, imag_part), apply_rows(cosine, imag_part) - apply_rows(sine_table, real_part))

def inverse(real_part, imag_part, cosine, sine_table):
    return (apply_rows(cosine, real_part) - apply_rows(sine_table, imag_part), apply_rows(cosine, imag_part) + apply_rows(sine_table, real_part))

def gram_part(values, coil_maps, weight, cosine, sine_table):

    def coil_term(summed, maps):
        real_part = maps[0] * values[0] - maps[1] * values[1]
        imag_part = maps[0] * values[1] + maps[1] * values[0]
        spec_real, spec_imag = forward(real_part, imag_part, cosine, sine_table)
        back_real, back_imag = inverse(spec_real * weight, spec_imag * weight, cosine, sine_table)
        term_real = maps[0] * back_real + maps[1] * back_imag
        term_imag = maps[0] * back_imag - maps[1] * back_real
        return (summed + jnp.stack([term_real, term_imag]), None)
    summed, unused = lax.scan(coil_term, jnp.zeros_like(values), coil_maps)
    return summed

def adjoint_data(measured, coil_maps, weight, cosine, sine_table):

    def coil_term(summed, pair):
        maps, sample = pair
        back_real, back_imag = inverse(sample[0] * weight, sample[1] * weight, cosine, sine_table)
        term_real = maps[0] * back_real + maps[1] * back_imag
        term_imag = maps[0] * back_imag - maps[1] * back_real
        return (summed + jnp.stack([term_real, term_imag]), None)
    start = jnp.zeros(measured.shape[1:], jnp.float32)
    summed, unused = lax.scan(coil_term, start, (coil_maps, measured))
    return summed

def forward_diff(values):
    return jnp.roll(values, -1, axis=1) - values

def backward_diff(values):
    return jnp.roll(values, 1, axis=1) - values

def reference(frames, auxiliary, scaled_dual, coil_maps, measured, sampling):
    cosine, sine_table = tables(NX)
    weight = sampling.astype(jnp.float32)[:, :, None]

    def apply_normal(values):
        return gram_part(values, coil_maps, weight, cosine, sine_table) + PENALTY * backward_diff(forward_diff(values)) + DAMPING * values
    rhs = adjoint_data(measured, coil_maps, weight, cosine, sine_table) + PENALTY * backward_diff(auxiliary - scaled_dual)
    estimate = frames
    residual = rhs - apply_normal(frames)
    direction = residual
    energy = jnp.sum(residual * residual)
    for iteration in range(CG_STEPS):
        image_dir = apply_normal(direction)
        step_size = energy / jnp.sum(direction * image_dir)
        estimate = estimate + step_size * direction
        residual = residual - step_size * image_dir
        if iteration + 1 < CG_STEPS:
            fresh = jnp.sum(residual * residual)
            direction = residual + fresh / energy * direction
            energy = fresh
    shifted = forward_diff(estimate) + scaled_dual
    magnitude = jnp.sqrt(shifted[0] * shifted[0] + shifted[1] * shifted[1])
    factor = jnp.maximum(magnitude - THRESHOLD, 0.0) / jnp.maximum(magnitude, THRESHOLD)
    new_aux = shifted * factor[None]
    new_dual = shifted - new_aux
    primal_gap = new_dual - scaled_dual
    dual_gap = new_aux - auxiliary
    residual_norms = jnp.stack([jnp.sqrt(jnp.sum(primal_gap * primal_gap)), PENALTY * jnp.sqrt(jnp.sum(dual_gap * dual_gap))])
    return (estimate, new_aux, new_dual, residual_norms)
```

```python
import functools
import math

import jax
import jax.numpy as jnp
import numpy as np
from jax import lax
from jax.experimental import pallas as pl
from jax.experimental.pallas import tpu as pltpu
from jax.sharding import PartitionSpec as P

PENALTY = 0.5
DAMPING = 0.1
THRESHOLD = 1.0

COILS = 16
PHASES = 8
ROWS = 16
SIZE = 256
LANES = 128
GROUP = 16
ROW_SHARDS = 16
PHASE_SHARDS = 8
ALL = ROW_SHARDS * PHASE_SHARDS

F32 = jnp.float32
BF16 = jnp.bfloat16


def lane_bit(rows, bit):
    lane = lax.broadcasted_iota(jnp.int32, (rows, LANES), 1)
    return (lane & (GROUP << bit)) != 0


def lane_group(rows):
    return lax.broadcasted_iota(jnp.int32, (rows, LANES), 1) // GROUP


def roll(value, groups):
    groups %= 8
    if groups == 0:
        return value
    return pltpu.roll(value, groups * GROUP, 1)


def gather_coils(halves):
    rows = halves[0][0].shape[0]
    lane = lax.broadcasted_iota(jnp.int32, (rows, LANES), 1)
    turned = []
    for c, (low, high) in enumerate(halves):
        if c >= 8:
            low, high = high, low
        shift = c % 8
        if shift:
            low, high = roll(low, shift), roll(high, shift)
            wrapped = lane < shift * GROUP
            low, high = jnp.where(wrapped, high, low), jnp.where(wrapped, low, high)
        turned.append((low, high))
    for bit in range(3):
        mask = lane_bit(rows, bit)
        turned = [
            tuple(jnp.where(mask, turned[(i + (1 << bit)) % 16][h], turned[i][h]) for h in range(2))
            for i in range(16)
        ]
    turned = [(turned[i][0], turned[(i + 8) % 16][1]) for i in range(16)]
    return [turned[(-j) % 16] for j in range(16)]


def transpose_groups(values):
    rows = values[0].shape[0]
    turned = [roll(value, a) for a, value in enumerate(values)]
    for bit in range(3):
        mask = lane_bit(rows, bit)
        turned = [jnp.where(mask, turned[(i + (1 << bit)) % 8], turned[i]) for i in range(8)]
    return [roll(turned[(-b) % 8], -b) for b in range(8)]


def pick_groups(values):
    rows = values[0].shape[0]
    for bit in range(3):
        mask = lane_bit(rows, bit)
        values = [jnp.where(mask, values[i + 1], values[i]) for i in range(0, len(values), 2)]
    return values[0]


def sum_groups(value):
    value = value + pltpu.roll(value, 4 * GROUP, 1)
    value = value + pltpu.roll(value, 2 * GROUP, 1)
    return value + pltpu.roll(value, GROUP, 1)


def spread_group(value, group):
    return sum_groups(jnp.where(lane_group(value.shape[0]) == group, value, 0.0))


def split(value):
    high = value.astype(BF16)
    return high, (value - high.astype(F32)).astype(BF16)


def dot(a, b):
    return jnp.dot(a, b, preferred_element_type=F32)


def dot3(table, value):
    return dot(table[0], value[0]) + (dot(table[0], value[1]) + dot(table[1], value[0]))


def wide(value):
    return jnp.concatenate([value, value], 1)


def combine(maps_real, maps_imag, real, imag):
    out_real = maps_real * real + maps_imag * imag
    out_imag = maps_real * imag - maps_imag * real
    return (
        sum_groups(out_real[:, :LANES] + out_real[:, LANES:]),
        sum_groups(out_imag[:, :LANES] + out_imag[:, LANES:]),
    )


def coil_images(maps_real, maps_imag, real, imag):
    real, imag = wide(real), wide(imag)
    return maps_real * real - maps_imag * imag, maps_real * imag + maps_imag * real


def pack_measured_kernel(in_ref, out_ref):
    for row in range(0, in_ref.shape[2], 8):
        halves = [
            (in_ref[c, 0, row : row + 8, :LANES], in_ref[c, 0, row : row + 8, LANES:])
            for c in range(COILS)
        ]
        for j, (low, high) in enumerate(gather_coils(halves)):
            out_ref[j, row : row + 8, :LANES] = low
            out_ref[j, row : row + 8, LANES:] = high


def pack_measured(measured, part):
    lines = measured.shape[2]
    step = 32
    return pl.pallas_call(
        pack_measured_kernel,
        grid=(lines // step,),
        in_specs=[pl.BlockSpec((COILS, 1, step, SIZE), lambda i: (0, part, i, 0))],
        out_specs=pl.BlockSpec((ROW_SHARDS, step, SIZE), lambda i: (0, i, 0)),
        out_shape=jax.ShapeDtypeStruct((ROW_SHARDS, lines, SIZE), F32),
        name=f"pack_measured_{part}",
    )(measured)


def pack_image_kernel(maps_ref, frames_ref, aux_ref, dual_ref, before_ref, after_ref, out_ref):
    for part in range(2):
        for row in range(0, ROWS, 8):
            at = slice(row, row + 8)
            halves = [
                (maps_ref[c, part, at, :LANES], maps_ref[c, part, at, LANES:]) for c in range(COILS)
            ]
            for j, (low, high) in enumerate(gather_coils(halves)):
                out_ref[j, part, at, :LANES] = low
                out_ref[j, part, at, LANES:] = high
            for half in range(2):
                cols = slice(half * LANES, (half + 1) * LANES)
                frames = [frames_ref[part, t, at, cols] for t in range(PHASES)]
                following = frames[1:] + [after_ref[part, 0, at, cols]]
                gap = [
                    aux_ref[part, t, at, cols] - dual_ref[part, t, at, cols] - following[t] + frames[t]
                    for t in range(PHASES)
                ]
                gap_before = [before_ref[part, 0, at, cols] - frames[0]] + gap[:-1]
                local = [
                    PENALTY * (gap_before[t] - gap[t]) - DAMPING * frames[t] for t in range(PHASES)
                ]
                to = slice(part * LANES, (part + 1) * LANES)
                for which, values in ((2, frames), (3, local)):
                    for jj, value in enumerate(transpose_groups(values)):
                        out_ref[half * 8 + jj, which, at, to] = value


def gram_table_kernel(weight_ref, tables_ref, out_ref):
    weight = weight_ref[0]
    cos_high, cos_low, sin_high, sin_low = (tables_ref[i] for i in range(4))

    def scaled(table):
        return (table.astype(F32) * weight).astype(BF16)

    cos_w = scaled(cos_high), scaled(cos_low)
    sin_w = scaled(sin_high), scaled(sin_low)
    cos, sin = (cos_high, cos_low), (sin_high, sin_low)
    real = dot3(cos_w, cos) + dot3(sin_w, sin)
    imag = dot3(sin_w, cos) - dot3(cos_w, sin)
    out_ref[0, 0], out_ref[0, 2] = split(real)
    out_ref[0, 1], out_ref[0, 3] = split(imag)


def gram_tables(weight, tables):
    return pl.pallas_call(
        gram_table_kernel,
        grid=(PHASES,),
        in_specs=[
            pl.BlockSpec((1, 1, SIZE), lambda t: (t, 0, 0)),
            pl.BlockSpec((4, SIZE, SIZE), lambda t: (0, 0, 0)),
        ],
        out_specs=pl.BlockSpec((1, 4, SIZE, SIZE), lambda t: (t, 0, 0, 0)),
        out_shape=jax.ShapeDtypeStruct((PHASES, 4, SIZE, SIZE), BF16),
        name="gram_tables",
    )(weight, tables)


def maps_of(image_ref):
    return image_ref[:, 0].reshape(SIZE, SIZE), image_ref[:, 1].reshape(SIZE, SIZE)


def gram(gram_ref, maps, real, imag):
    real, imag = (split(v) for v in coil_images(*maps, real, imag))
    table_real = gram_ref[0, 0], gram_ref[0, 2]
    table_imag = gram_ref[0, 1], gram_ref[0, 3]
    back_real = dot3(table_real, real) - dot3(table_imag, imag)
    back_imag = dot3(table_real, imag) + dot3(table_imag, real)
    return combine(*maps, back_real, back_imag)


def start_kernel(gram_ref, image_ref, out_ref):
    t = pl.program_id(0)
    frames = image_ref[:, 2].reshape(SIZE, SIZE)
    local = image_ref[:, 3].reshape(SIZE, SIZE)
    real, imag = spread_group(frames[:, :LANES], t), spread_group(frames[:, LANES:], t)
    gram_real, gram_imag = gram(gram_ref, maps_of(image_ref), real, imag)
    out_ref[0, 0] = spread_group(local[:, :LANES], t) - gram_real
    out_ref[1, 0] = spread_group(local[:, LANES:], t) - gram_imag


GRAM_SPEC = pl.BlockSpec((1, 4, SIZE, SIZE), lambda t: (t, 0, 0, 0))
IMAGE_SPEC = pl.BlockSpec((ROW_SHARDS, 4, ROWS, SIZE), lambda t: (0, 0, 0, 0))
MAPS_SPEC = pl.BlockSpec((ROW_SHARDS, 2, ROWS, SIZE), lambda t: (0, 0, 0, 0))
VECTOR_SPEC = pl.BlockSpec((2, 1, SIZE, LANES), lambda t: (0, t, 0, 0))
VECTOR = jax.ShapeDtypeStruct((2, PHASES, SIZE, LANES), F32)


def start(grams, image):
    return pl.pallas_call(
        start_kernel,
        grid=(PHASES,),
        in_specs=[GRAM_SPEC, IMAGE_SPEC],
        out_specs=VECTOR_SPEC,
        out_shape=VECTOR,
        name="start",
    )(grams, image)


def adjoint_kernel(part, weight_ref, tables_ref, image_ref, lines_ref, in_ref, out_ref):
    weight = weight_ref[0]
    lines = split(lines_ref[...].reshape(SIZE, SIZE))

    def scaled(i):
        return (tables_ref[i].astype(F32) * weight).astype(BF16)

    by_cos = dot3((scaled(0), scaled(1)), lines)
    by_sin = dot3((scaled(2), scaled(3)), lines)
    maps = maps_of(image_ref)
    if part == 0:
        real, imag = combine(*maps, by_cos, by_sin)
    else:
        real, imag = combine(*maps, -by_sin, by_cos)
    out_ref[0, 0] = in_ref[0, 0] + real
    out_ref[1, 0] = in_ref[1, 0] + imag


def adjoint(part, weight, tables, image, lines, so_far):
    return pl.pallas_call(
        functools.partial(adjoint_kernel, part),
        grid=(PHASES,),
        in_specs=[
            pl.BlockSpec((1, 1, SIZE), lambda t: (t, 0, 0)),
            pl.BlockSpec((4, SIZE, SIZE), lambda t: (0, 0, 0)),
            MAPS_SPEC,
            pl.BlockSpec((ROW_SHARDS, ROWS, SIZE), lambda t: (0, t, 0)),
            VECTOR_SPEC,
        ],
        out_specs=VECTOR_SPEC,
        out_shape=VECTOR,
        name=f"adjoint_{part}",
    )(weight, tables, image, lines, so_far)


def gram_kernel(gram_ref, image_ref, in_ref, out_ref):
    real, imag = gram(gram_ref, maps_of(image_ref), in_ref[0, 0], in_ref[1, 0])
    out_ref[0, 0] = real
    out_ref[1, 0] = imag


def gram_apply(grams, image, vector):
    return pl.pallas_call(
        gram_kernel,
        grid=(PHASES,),
        in_specs=[GRAM_SPEC, MAPS_SPEC, VECTOR_SPEC],
        out_specs=VECTOR_SPEC,
        out_shape=VECTOR,
        name="gram_apply",
    )(grams, image, vector)


def fold(value):
    return jnp.sum(value.reshape(-1, 8, LANES), 0)


def normal_kernel(first_ref, gram_ref, before_ref, after_ref, image_ref, edge_ref, back_ref, sums_ref):
    @pl.when(pl.program_id(0) == 0)
    def _():
        sums_ref[...] = jnp.zeros_like(sums_ref)

    rows = first_ref.shape[2]
    rr = rw = ww = dd = 0.0
    for part in range(2):
        values = [first_ref[part, t] for t in range(PHASES)]
        around = [before_ref[part]] + values + [after_ref[part]]
        images = [
            gram_ref[part, t]
            + PENALTY * ((around[t + 1] - around[t]) - (around[t + 2] - around[t + 1]))
            + DAMPING * values[t]
            for t in range(PHASES)
        ]
        for t in range(PHASES):
            image_ref[part, t] = images[t]
            rr += fold(values[t] * values[t])
            rw += fold(values[t] * images[t])
            ww += fold(images[t] * images[t])
            if t:
                step = images[t] - images[t - 1]
                dd += fold(step * step)
        edge_ref[part] = images[0]
        for which, vectors in ((0, values), (1, images)):
            back = pick_groups(vectors)
            for j in range(rows // ROWS):
                back_ref[j, 2 * which + part] = back[j * ROWS : (j + 1) * ROWS]
    for i, value in enumerate((rr, rw, ww, dd)):
        sums_ref[i] += value


def normal(first, grams_first, before, after):
    rows = 64
    whole = pl.BlockSpec((2, PHASES, rows, LANES), lambda i: (0, 0, i, 0))
    edge = pl.BlockSpec((2, rows, LANES), lambda i: (0, i, 0))
    return pl.pallas_call(
        normal_kernel,
        grid=(SIZE // rows,),
        in_specs=[whole, whole, edge, edge],
        out_specs=[
            whole,
            edge,
            pl.BlockSpec((rows // ROWS, 4, ROWS, LANES), lambda i: (i, 0, 0, 0)),
            pl.BlockSpec((4, 8, LANES), lambda i: (0, 0, 0)),
        ],
        out_shape=[
            VECTOR,
            jax.ShapeDtypeStruct((2, SIZE, LANES), F32),
            jax.ShapeDtypeStruct((ROW_SHARDS, 4, ROWS, LANES), F32),
            jax.ShapeDtypeStruct((4, 8, LANES), F32),
        ],
        name="normal",
    )(first, grams_first, before, after)


def curvature_kernel(gram_ref, image_ref, in_ref, out_ref):
    @pl.when(pl.program_id(0) == 0)
    def _():
        out_ref[...] = jnp.zeros_like(out_ref)

    real, imag = coil_images(*maps_of(image_ref), in_ref[0, 0], in_ref[1, 0])
    real_high, imag_high = real.astype(BF16), imag.astype(BF16)
    table_real, table_imag = gram_ref[0, 0], gram_ref[0, 1]
    back_real = dot(table_real, real_high) - dot(table_imag, imag_high)
    back_imag = dot(table_real, imag_high) + dot(table_imag, real_high)
    total = real * back_real + imag * back_imag
    out_ref[...] += fold(total[:, :LANES]) + fold(total[:, LANES:])


def curvature(grams, image, vector):
    return pl.pallas_call(
        curvature_kernel,
        grid=(PHASES,),
        in_specs=[pl.BlockSpec((1, 2, SIZE, SIZE), lambda t: (t, 0, 0, 0)), MAPS_SPEC, VECTOR_SPEC],
        out_specs=pl.BlockSpec((8, LANES), lambda t: (0, 0)),
        out_shape=jax.ShapeDtypeStruct((8, LANES), F32),
        name="curvature",
    )(grams, image, vector)


def lane_row(values):
    lane = lax.broadcasted_iota(jnp.int32, (1, LANES), 1)
    row = jnp.zeros((1, LANES), F32)
    for i, value in enumerate(values):
        row = jnp.where(lane == i, value, row)
    return row


def whole_sum(value):
    return jnp.sum(jnp.sum(value, 0, keepdims=True), 1, keepdims=True)


def share_kernel(sums_ref, curve_ref, last_ref, after_ref, out_ref):
    rr, rw, ww, dd = (whole_sum(sums_ref[i]) * 0.125 for i in range(4))
    edge = 0.0
    for part in range(2):
        step = after_ref[part] - last_ref[part, 0]
        edge = edge + fold(step * step)
    dd = dd + whole_sum(edge) * 0.125
    curve = whole_sum(curve_ref[...]) + PENALTY * dd + DAMPING * ww
    row = lane_row((rr, rw, ww, curve))
    out_ref[...] = jnp.broadcast_to(row[None], out_ref.shape)


def share(sums, curve, vector, after):
    return pl.pallas_call(
        share_kernel,
        grid=(1,),
        in_specs=[
            pl.BlockSpec((4, 8, LANES), lambda i: (0, 0, 0)),
            pl.BlockSpec((8, LANES), lambda i: (0, 0)),
            pl.BlockSpec((2, 1, SIZE, LANES), lambda i: (0, PHASES - 1, 0, 0)),
            pl.BlockSpec((2, SIZE, LANES), lambda i: (0, 0, 0)),
        ],
        out_specs=pl.BlockSpec((ALL, 1, LANES), lambda i: (0, 0, 0)),
        out_shape=jax.ShapeDtypeStruct((ALL, 1, LANES), F32),
        name="share",
    )(sums, curve, vector, after)


def unpack_kernel(in_ref, out_ref, edge_ref):
    for which in range(4):
        for row in range(0, ROWS, 8):
            at = slice(row, row + 8)
            for half in range(2):
                values = [in_ref[half * 8 + jj, which, at] for jj in range(8)]
                cols = slice(half * LANES, (half + 1) * LANES)
                for t, value in enumerate(transpose_groups(values)):
                    out_ref[which, t, at, cols] = value
                    if t == 0:
                        edge_ref[which, at, cols] = value


def unpack(back):
    return pl.pallas_call(
        unpack_kernel,
        out_shape=[
            jax.ShapeDtypeStruct((4, PHASES, ROWS, SIZE), F32),
            jax.ShapeDtypeStruct((4, ROWS, SIZE), F32),
        ],
        name="unpack",
    )(back)


def finish_kernel(
    shared_ref, frames_ref, aux_ref, dual_ref, steps_ref, edge_ref, after_ref,
    x_ref, new_aux_ref, new_dual_ref, out_ref,
):
    row = jnp.sum(shared_ref[...], 0)
    rr, rw, ww, curve = (row[:, i : i + 1] for i in range(4))
    alpha = rr / rw
    fresh = rr - 2.0 * alpha * rw + alpha * alpha * ww
    beta = fresh / rr
    gamma = 1.0 + beta
    bend = gamma * gamma * rw - 2.0 * gamma * alpha * ww + alpha * alpha * curve
    second = fresh / bend
    by_first = alpha + second * gamma
    by_image = -second * alpha
    primal = dual_sum = 0.0
    for row in range(0, ROWS, 8):
        at = slice(row, row + 8)
        parts = []
        for part in range(2):
            values = [
                frames_ref[part, t, at]
                + by_first * steps_ref[part, t, at]
                + by_image * steps_ref[2 + part, t, at]
                for t in range(PHASES)
            ]
            for t in range(PHASES):
                x_ref[part, t, at] = values[t]
            after = (
                after_ref[part, 0, at]
                + by_first * edge_ref[part, at]
                + by_image * edge_ref[2 + part, at]
            )
            parts.append(values + [after])
        for t in range(PHASES):
            dual = [dual_ref[part, t, at] for part in range(2)]
            shifted = [parts[part][t + 1] - parts[part][t] + dual[part] for part in range(2)]
            magnitude = jnp.sqrt(shifted[0] * shifted[0] + shifted[1] * shifted[1])
            factor = jnp.maximum(magnitude - THRESHOLD, 0.0) / jnp.maximum(magnitude, THRESHOLD)
            for part in range(2):
                new_aux = shifted[part] * factor
                new_dual = shifted[part] - new_aux
                new_aux_ref[part, t, at] = new_aux
                new_dual_ref[part, t, at] = new_dual
                gap = new_dual - dual[part]
                primal += gap * gap
                gap = new_aux - aux_ref[part, t, at]
                dual_sum += gap * gap
    sums = lane_row((whole_sum(primal), whole_sum(dual_sum)))
    out_ref[...] = jnp.broadcast_to(sums[None], out_ref.shape)


def finish(shared, frames, auxiliary, scaled_dual, steps, edge, after):
    image = jax.ShapeDtypeStruct((2, PHASES, ROWS, SIZE), F32)
    return pl.pallas_call(
        finish_kernel,
        out_shape=[image, image, image, jax.ShapeDtypeStruct((ALL, 1, LANES), F32)],
        name="finish",
    )(shared, frames, auxiliary, scaled_dual, steps, edge, after)


def norms_kernel(in_ref, out_ref):
    root = jnp.sqrt(jnp.sum(in_ref[...], 0))
    lane = lax.broadcasted_iota(jnp.int32, (1, LANES), 1)
    out_ref[...] = jnp.where(lane == 1, PENALTY, 1.0) * root


def norms(shared):
    return pl.pallas_call(
        norms_kernel, out_shape=jax.ShapeDtypeStruct((1, LANES), F32), name="norms"
    )(shared)


def tables():
    index = np.arange(SIZE)
    angle = (index[:, None] * index[None, :] % SIZE) * (2.0 * math.pi / SIZE)
    out = []
    for table in (np.cos(angle), np.sin(angle)):
        table = (table / math.sqrt(SIZE)).astype(np.float32)
        high = table.astype(BF16)
        out += [high, (table - high.astype(np.float32)).astype(BF16)]
    return np.stack(out)


def shift(value, steps):
    pairs = [(i, (i + steps) % PHASE_SHARDS) for i in range(PHASE_SHARDS)]
    return lax.ppermute(value, "phase", pairs)


def exchange(value, axes):
    return lax.all_to_all(value, axes, 0, 0, tiled=True)


def local(frames, auxiliary, scaled_dual, coil_maps, measured, sampling):
    table = jnp.asarray(tables())
    weight = sampling.astype(F32)[:, None, :]
    lines = measured.reshape(COILS, 2, PHASES * ROWS, SIZE)

    last = slice(PHASES - 1, PHASES)
    before = shift(auxiliary[:, last] - scaled_dual[:, last] + frames[:, last], 1)
    after = shift(frames[:, :1], -1)
    packed_real = exchange(pack_measured(lines, 0), "row")
    packed_image = pl.pallas_call(
        pack_image_kernel,
        out_shape=jax.ShapeDtypeStruct((ROW_SHARDS, 4, ROWS, SIZE), F32),
        name="pack_image",
    )(coil_maps, frames, auxiliary, scaled_dual, before, after)
    image = exchange(packed_image, "row")
    packed_imag = exchange(pack_measured(lines, 1), "row")

    grams = gram_tables(weight, table)
    residual = start(grams, image)
    residual = adjoint(0, weight, table, image, packed_real, residual)
    residual = adjoint(1, weight, table, image, packed_imag, residual)

    residual_before = shift(residual[:, PHASES - 1], 1)
    residual_after = shift(residual[:, 0], -1)
    grams_residual = gram_apply(grams, image, residual)
    product, product_first, back, sums = normal(
        residual, grams_residual, residual_before, residual_after
    )
    product_after = shift(product_first, -1)
    steps, steps_first = unpack(exchange(back, "row"))
    steps_after = shift(steps_first, -1)
    curve = curvature(grams, image, product)
    shared = exchange(share(sums, curve, product, product_after), ("phase", "row"))
    new_frames, new_aux, new_dual, gaps = finish(
        shared, frames, auxiliary, scaled_dual, steps, steps_after, after
    )
    residual_norms = norms(exchange(gaps, ("phase", "row")))[0, :2]
    return new_frames, new_aux, new_dual, residual_norms


def solution(mesh):
    image = P(None, "phase", "row", None)
    in_specs = (
        image,
        image,
        image,
        P(None, None, "row", None),
        P(None, None, "phase", "row", None),
        P("phase", None),
    )
    return jax.shard_map(
        local, mesh=mesh, in_specs=in_specs, out_specs=(image, image, image, P()), check_vma=False
    )
```

```python
import functools
import math

import jax
import jax.numpy as jnp
import numpy as np
from jax import lax
from jax.experimental import pallas as pl
from jax.experimental.pallas import tpu as pltpu
from jax.sharding import PartitionSpec as P

PENALTY = 0.5
DAMPING = 0.1
THRESHOLD = 1.0

COILS = 16
PHASES = 8
ROWS = 16
SIZE = 256
LANES = 128
GROUP = 16
FOLD = 32
LINES = PHASES * ROWS
MAIN = 88
EXTRA = LINES - MAIN
IMAGE = 4 * ROWS
ROW_SHARDS = 16
PHASE_SHARDS = 8
ALL = ROW_SHARDS * PHASE_SHARDS

F32 = jnp.float32
BF16 = jnp.bfloat16


def lane_bit(rows, bit):
    lane = lax.broadcasted_iota(jnp.int32, (rows, LANES), 1)
    return (lane & (GROUP << bit)) != 0


def lane_group(rows):
    return lax.broadcasted_iota(jnp.int32, (rows, LANES), 1) // GROUP


def roll(value, groups):
    groups %= 8
    if groups == 0:
        return value
    return pltpu.roll(value, groups * GROUP, 1)


def gather_coils(halves):
    rows = halves[0][0].shape[0]
    lane = lax.broadcasted_iota(jnp.int32, (rows, LANES), 1)
    turned = []
    for c, (low, high) in enumerate(halves):
        if c >= 8:
            low, high = high, low
        shift = c % 8
        if shift:
            low, high = roll(low, shift), roll(high, shift)
            wrapped = lane < shift * GROUP
            low, high = jnp.where(wrapped, high, low), jnp.where(wrapped, low, high)
        turned.append((low, high))
    for bit in range(3):
        mask = lane_bit(rows, bit)
        turned = [
            tuple(jnp.where(mask, turned[(i + (1 << bit)) % 16][h], turned[i][h]) for h in range(2))
            for i in range(16)
        ]
    turned = [(turned[i][0], turned[(i + 8) % 16][1]) for i in range(16)]
    return [turned[(-j) % 16] for j in range(16)]


def transpose_groups(values):
    rows = values[0].shape[0]
    turned = [roll(value, a) for a, value in enumerate(values)]
    for bit in range(3):
        mask = lane_bit(rows, bit)
        turned = [jnp.where(mask, turned[(i + (1 << bit)) % 8], turned[i]) for i in range(8)]
    return [roll(turned[(-b) % 8], -b) for b in range(8)]


def spread_half(value, half):
    rows = value.shape[0]
    turned = pltpu.roll(value, 4 * GROUP, 1)
    low = ~lane_bit(rows, 2)
    values = [jnp.where(low == (half == 0), value, turned)]
    for bit in (1, 0):
        low = ~lane_bit(rows, bit)
        spread = []
        for value in values:
            turned = pltpu.roll(value, GROUP << bit, 1)
            spread += [jnp.where(low, value, turned), jnp.where(low, turned, value)]
        values = spread
    return values


def sum_four(values):
    rows = values[0].shape[0]
    for bit in range(2):
        low = ~lane_bit(rows, bit)
        values = [
            jnp.where(low, a, b) + pltpu.roll(jnp.where(low, b, a), GROUP << bit, 1)
            for a, b in zip(values[::2], values[1::2])
        ]
    return values[0] + pltpu.roll(values[0], 4 * GROUP, 1)


def fold_phase(value, phase):
    group = lane_group(FOLD)
    out = None
    for i in range(8):
        piece = roll(value[i * FOLD : (i + 1) * FOLD], i - phase)
        out = piece if out is None else jnp.where(group == i, piece, out)
    return out


def unfold_phase(value, phase, i):
    return roll(value, phase - i)


def split(value):
    high = value.astype(BF16)
    return high, (value - high.astype(F32)).astype(BF16)


def dot(a, b):
    return jnp.dot(a, b, preferred_element_type=F32)


def dot3(table, value):
    return dot(table[0], value[0]) + (dot(table[0], value[1]) + dot(table[1], value[0]))


def wide(value):
    return jnp.concatenate([value, value], 1)


def images_of(maps_ref, at, real, imag):
    maps_real, maps_imag = maps_at(maps_ref, at)
    real, imag = wide(real), wide(imag)
    return maps_real * real - maps_imag * imag, maps_real * imag + maps_imag * real


def maps_at(maps_ref, at):
    return maps_ref[0, at], maps_ref[1, at]


def combine(maps_real, maps_imag, real, imag):
    out_real = maps_real * real + maps_imag * imag
    out_imag = maps_real * imag - maps_imag * real
    return out_real[:, :LANES] + out_real[:, LANES:], out_imag[:, :LANES] + out_imag[:, LANES:]


def chunks(step):
    return [slice(row, row + step) for row in range(0, SIZE, step)]


def store_split(ref, which, at, value):
    ref[which, at], ref[which + 1, at] = split(value)


def expand(vector_ref, maps_ref, pieces):
    half = pl.program_id(0)
    for at in chunks(32):
        real = spread_half(vector_ref[0, at], half)
        imag = spread_half(vector_ref[1, at], half)
        for t in range(4):
            image_real, image_imag = images_of(maps_ref, at, real[t], imag[t])
            store_split(pieces[t], 0, at, image_real)
            store_split(pieces[t], 2, at, image_imag)


def reduce(maps_ref, backs, finish):
    for at in chunks(32):
        maps = maps_at(maps_ref, at)
        terms = [combine(*maps, backs[t][0, at], backs[t][1, at]) for t in range(4)]
        finish(at, sum_four([term[0] for term in terms]), sum_four([term[1] for term in terms]))


def gram_products(gram_ref, pieces, backs):
    for t in range(4):
        real_high, real_low, imag_high, imag_low = (pieces[t][i] for i in range(4))
        table_real, table_imag, low_real, low_imag = (gram_ref[t, i] for i in range(4))
        backs[t][0] = (
            dot(table_real, real_high) + dot(table_real, real_low) + dot(low_real, real_high)
        ) - (dot(table_imag, imag_high) + dot(table_imag, imag_low) + dot(low_imag, imag_high))
        backs[t][1] = (
            dot(table_real, imag_high) + dot(table_real, imag_low) + dot(low_real, imag_high)
        ) + (dot(table_imag, real_high) + dot(table_imag, real_low) + dot(low_imag, real_high))


def in_step(rows):
    return lane_bit(rows, 2) == (pl.program_id(0) == 1)


def split_three(value):
    high = value.astype(BF16)
    value = value - high.astype(F32)
    middle = value.astype(BF16)
    return high, middle, (value - middle.astype(F32)).astype(BF16)


def compact(weight_ref, in_ref, lines_ref, base):
    count = lines_ref.shape[1]
    weight = jnp.broadcast_to(weight_ref[...], (8, LINES))
    row = lax.broadcasted_iota(jnp.int32, (LINES, LINES), 0)
    col = lax.broadcasted_iota(jnp.int32, (LINES, LINES), 1)
    upto = jnp.where(row <= col, 1.0, 0.0).astype(BF16)
    number = dot(weight.astype(BF16), upto).astype(jnp.int32)
    number = jnp.broadcast_to(number[:1], (count, LINES))
    acquired = jnp.broadcast_to(weight_ref[...], (count, LINES)) > 0.5
    line = lax.broadcasted_iota(jnp.int32, (count, LINES), 0) + (base + 1)
    select = jnp.where((number == line) & acquired, 1.0, 0.0).astype(BF16)
    step = in_ref.shape[0]
    for c in range(step):
        high, middle, low = split_three(in_ref[c, 0])
        lines_ref[pl.program_id(0) * step + c] = (
            dot(select, high) + dot(select, middle) + dot(select, low)
        )


def pack_lines(lines_ref, out_ref, start):
    for row in range(0, lines_ref.shape[1], 8):
        at = slice(row, row + 8)
        to = slice(start + row, start + row + 8)
        halves = [(lines_ref[c, at, :LANES], lines_ref[c, at, LANES:]) for c in range(COILS)]
        for j, (low, high) in enumerate(gather_coils(halves)):
            out_ref[j, to, :LANES] = low
            out_ref[j, to, LANES:] = high


def pack_image(maps_ref, frames_ref, aux_ref, dual_ref, out_ref):
    for part in range(2):
        for row in range(0, ROWS, 8):
            at = slice(row, row + 8)
            halves = [
                (maps_ref[c, part, at, :LANES], maps_ref[c, part, at, LANES:]) for c in range(COILS)
            ]
            to = slice(part * ROWS + row, part * ROWS + row + 8)
            for j, (low, high) in enumerate(gather_coils(halves)):
                out_ref[j, to, :LANES] = low
                out_ref[j, to, LANES:] = high
            for half in range(2):
                cols = slice(half * LANES, (half + 1) * LANES)
                frames = [frames_ref[part, t, at, cols] for t in range(PHASES)]
                splits = [
                    aux_ref[part, t, at, cols] - dual_ref[part, t, at, cols] for t in range(PHASES)
                ]
                lanes = slice(part * LANES, (part + 1) * LANES)
                for which, values in ((2, frames), (3, splits)):
                    to = slice(which * ROWS + row, which * ROWS + row + 8)
                    for jj, value in enumerate(transpose_groups(values)):
                        out_ref[half * 8 + jj, to, lanes] = value


def pack_first_kernel(
    weight_ref, in_ref, maps_ref, frames_ref, aux_ref, dual_ref, out_ref, lines_ref
):
    compact(weight_ref, in_ref, lines_ref, 0)

    @pl.when(pl.program_id(0) == pl.num_programs(0) - 1)
    def _():
        pack_image(maps_ref, frames_ref, aux_ref, dual_ref, out_ref)
        pack_lines(lines_ref, out_ref, IMAGE)


def whole_spec(value):
    return pl.BlockSpec(value.shape, lambda *_: (0,) * value.ndim)


def pack_first(weight, measured, *images):
    step = 4
    return pl.pallas_call(
        pack_first_kernel,
        grid=(COILS // step,),
        in_specs=[
            whole_spec(weight),
            pl.BlockSpec((step, 1, LINES, SIZE), lambda i: (i, 0, 0, 0)),
            *(whole_spec(value) for value in images),
        ],
        out_specs=pl.BlockSpec((ROW_SHARDS, IMAGE + MAIN, SIZE), lambda i: (0, 0, 0)),
        out_shape=jax.ShapeDtypeStruct((ROW_SHARDS, IMAGE + MAIN, SIZE), F32),
        scratch_shapes=[pltpu.VMEM((COILS, MAIN, SIZE), F32)],
        compiler_params=params(),
        name="pack_first",
    )(weight, measured, *images)


def pack_more_kernel(base, weight_ref, in_ref, out_ref, lines_ref):
    compact(weight_ref, in_ref, lines_ref, base)

    @pl.when(pl.program_id(0) == pl.num_programs(0) - 1)
    def _():
        pack_lines(lines_ref, out_ref, 0)


def pack_more(weight, measured, part, base, count):
    step = 4
    return pl.pallas_call(
        functools.partial(pack_more_kernel, base),
        grid=(COILS // step,),
        in_specs=[
            whole_spec(weight),
            pl.BlockSpec((step, 1, LINES, SIZE), lambda i: (i, part, 0, 0)),
        ],
        out_specs=pl.BlockSpec((ROW_SHARDS, count, SIZE), lambda i: (0, 0, 0)),
        out_shape=jax.ShapeDtypeStruct((ROW_SHARDS, count, SIZE), F32),
        scratch_shapes=[pltpu.VMEM((COILS, count, SIZE), F32)],
        compiler_params=params(),
        name=f"pack_more_{part}_{base}",
    )(weight, measured)


def line_table_kernel(index_ref, tables_ref, out_ref):
    row = lax.broadcasted_iota(jnp.int32, (SIZE, SIZE), 0)
    select = jnp.where(row == index_ref[0], 1.0, 0.0).astype(BF16)
    for i in range(4):
        out_ref[0, i] = dot(tables_ref[i], select).astype(BF16)


def line_tables(index, tables):
    return pl.pallas_call(
        line_table_kernel,
        grid=(PHASES,),
        in_specs=[pl.BlockSpec((1, 1, SIZE), lambda t: (t, 0, 0)), whole_spec(tables)],
        out_specs=pl.BlockSpec((1, 4, SIZE, SIZE), lambda t: (t, 0, 0, 0)),
        out_shape=jax.ShapeDtypeStruct((PHASES, 4, SIZE, SIZE), BF16),
        name="line_tables",
    )(index, tables)


def receive_kernel(image_ref, maps_ref, frames_ref, splits_ref, first_ref, last_ref):
    for part in range(2):
        lanes = slice(part * LANES, (part + 1) * LANES)
        for block in range(ROW_SHARDS):
            at = slice(block * ROWS, (block + 1) * ROWS)
            maps_ref[part, at] = image_ref[block, part * ROWS : (part + 1) * ROWS]
            frames_ref[part, at] = image_ref[block, 2 * ROWS : 3 * ROWS, lanes]
            splits_ref[part, at] = image_ref[block, 3 * ROWS : 4 * ROWS, lanes]
        first_ref[part] = fold_phase(frames_ref[part], 0)
        last_ref[part] = fold_phase(frames_ref[part] + splits_ref[part], PHASES - 1)


def receive(image):
    return pl.pallas_call(
        receive_kernel,
        grid=(1,),
        in_specs=[IMAGE_SPEC],
        out_specs=[MAPS_SPEC, VECTOR_SPEC, VECTOR_SPEC, FOLDED_SPEC, FOLDED_SPEC],
        out_shape=[jax.ShapeDtypeStruct((2, SIZE, SIZE), F32), VECTOR, VECTOR, FOLDED, FOLDED],
        name="receive",
    )(image)


def gram_table_kernel(weight_ref, tables_ref, out_ref):
    weight = weight_ref[0]
    cos_high, cos_low, sin_high, sin_low = (tables_ref[i] for i in range(4))

    def scaled(table):
        return (table.astype(F32) * weight).astype(BF16)

    cos_w = scaled(cos_high), scaled(cos_low)
    sin_w = scaled(sin_high), scaled(sin_low)
    cos, sin = (cos_high, cos_low), (sin_high, sin_low)
    real = dot3(cos_w, cos) + dot3(sin_w, sin)
    imag = dot3(sin_w, cos) - dot3(cos_w, sin)
    out_ref[0, 0], out_ref[0, 2] = split(real)
    out_ref[0, 1], out_ref[0, 3] = split(imag)


def gram_tables(weight, tables):
    return pl.pallas_call(
        gram_table_kernel,
        grid=(PHASES,),
        in_specs=[
            pl.BlockSpec((1, 1, SIZE), lambda t: (t, 0, 0)),
            pl.BlockSpec((4, SIZE, SIZE), lambda t: (0, 0, 0)),
        ],
        out_specs=pl.BlockSpec((1, 4, SIZE, SIZE), lambda t: (t, 0, 0, 0)),
        out_shape=jax.ShapeDtypeStruct((PHASES, 4, SIZE, SIZE), BF16),
        name="gram_tables",
    )(weight, tables)


GRAM_SPEC = pl.BlockSpec((4, 4, SIZE, SIZE), lambda i, *_: (i, 0, 0, 0))
IMAGE_SPEC = pl.BlockSpec((ROW_SHARDS, IMAGE, SIZE), lambda *_: (0, 0, 0))
MAPS_SPEC = pl.BlockSpec((2, SIZE, SIZE), lambda *_: (0, 0, 0))
VECTOR_SPEC = pl.BlockSpec((2, SIZE, LANES), lambda *_: (0, 0, 0))
VECTOR = jax.ShapeDtypeStruct((2, SIZE, LANES), F32)
FOLDED_SPEC = pl.BlockSpec((2, FOLD, LANES), lambda *_: (0, 0, 0))
FOLDED = jax.ShapeDtypeStruct((2, FOLD, LANES), F32)
SUMS_SPEC = pl.BlockSpec((4, 8, LANES), lambda i: (0, 0, 0))
PIECES = [pltpu.VMEM((4, SIZE, SIZE), BF16)] * 4
BACKS = [pltpu.VMEM((2, SIZE, SIZE), F32)] * 4


def params():
    return pltpu.CompilerParams(vmem_limit_bytes=48 << 20)


def start_kernel(
    gram_ref, maps_ref, frames_ref, splits_ref, before_ref, after_ref, in_ref, out_ref, *scratch
):
    pieces, backs = scratch[:4], scratch[4:]

    @pl.when(pl.program_id(0) == 0)
    def _():
        group = lane_group(FOLD)
        for i in range(8):
            at = slice(i * FOLD, (i + 1) * FOLD)
            for part in range(2):
                frames, splits = frames_ref[part, at], splits_ref[part, at]
                ahead = jnp.where(
                    group == PHASES - 1,
                    unfold_phase(after_ref[part], PHASES - 1, i),
                    pltpu.roll(frames, LANES - GROUP, 1),
                )
                behind = jnp.where(
                    group == 0,
                    unfold_phase(before_ref[part], 0, i),
                    pltpu.roll(frames + splits, GROUP, 1),
                )
                gap = splits - (ahead - frames)
                gap_behind = behind - frames
                out_ref[part, at] = (
                    in_ref[part, at] + PENALTY * (gap_behind - gap) - DAMPING * frames
                )

    expand(frames_ref, maps_ref, pieces)
    gram_products(gram_ref, pieces, backs)

    def finish(at, real, imag):
        keep = in_step(at.stop - at.start)
        for part, value in enumerate((real, imag)):
            out_ref[part, at] -= jnp.where(keep, value, 0.0)

    reduce(maps_ref, backs, finish)


def start(grams, maps, frames, splits, before, after, so_far):
    return pl.pallas_call(
        start_kernel,
        grid=(2,),
        in_specs=[GRAM_SPEC, MAPS_SPEC] + [VECTOR_SPEC] * 2 + [FOLDED_SPEC] * 2 + [VECTOR_SPEC],
        out_specs=VECTOR_SPEC,
        out_shape=VECTOR,
        scratch_shapes=PIECES + BACKS,
        compiler_params=params(),
        name="start",
    )(grams, maps, frames, splits, before, after, so_far)


def adjoint_kernel(
    part, base, window_ref, tables_ref, maps_ref, lines_ref, in_ref, out_ref, first_ref, last_ref, *scratch
):
    pieces, backs = scratch[:4], scratch[4:]
    half = pl.program_id(0)
    count = lines_ref.shape[1] - base

    @pl.when(half == 0)
    def _():
        out_ref[...] = in_ref[...]

    for t in range(4):
        for block in range(ROW_SHARDS):
            at = slice(block * ROWS, (block + 1) * ROWS)
            start = window_ref[(half * 4 + t) * ROW_SHARDS + block]
            aligned = jnp.minimum(start // 8, (count - ROWS) // 8 - 1) * 8
            rows = lines_ref[block, pl.ds(pl.multiple_of(base + aligned, 8), ROWS + 8)]
            rows = pltpu.roll(rows, lax.rem(ROWS + 8 - (start - aligned), ROWS + 8), 0)
            store_split(pieces[t], 0, at, rows[:ROWS])
        high, low = pieces[t][0], pieces[t][1]
        cos, cos_low, sin, sin_low = (tables_ref[t, i] for i in range(4))
        by_cos = dot(cos, high) + dot(cos, low) + dot(cos_low, high)
        by_sin = dot(sin, high) + dot(sin, low) + dot(sin_low, high)
        backs[t][0], backs[t][1] = (by_cos, by_sin) if part == 0 else (-by_sin, by_cos)

    def finish(at, real, imag):
        keep = in_step(at.stop - at.start)
        for which, value in enumerate((real, imag)):
            out_ref[which, at] += jnp.where(keep, value, 0.0)

    reduce(maps_ref, backs, finish)

    @pl.when(half == 1)
    def _():
        for which in range(2):
            value = out_ref[which]
            first_ref[which] = fold_phase(value, 0)
            last_ref[which] = fold_phase(value, PHASES - 1)


def adjoint(part, base, window, tables, maps, lines, so_far):
    return pl.pallas_call(
        functools.partial(adjoint_kernel, part, base),
        grid_spec=pltpu.PrefetchScalarGridSpec(
            num_scalar_prefetch=1,
            grid=(2,),
            in_specs=[GRAM_SPEC, MAPS_SPEC, whole_spec(lines), VECTOR_SPEC],
            out_specs=[VECTOR_SPEC, FOLDED_SPEC, FOLDED_SPEC],
            scratch_shapes=PIECES + BACKS,
        ),
        out_shape=[VECTOR, FOLDED, FOLDED],
        compiler_params=params(),
        name=f"adjoint_{part}_{base}",
    )(window, tables, maps, lines, so_far)


def gram_kernel(gram_ref, maps_ref, in_ref, out_ref, *scratch):
    pieces, backs = scratch[:4], scratch[4:]
    expand(in_ref, maps_ref, pieces)
    gram_products(gram_ref, pieces, backs)

    @pl.when(pl.program_id(0) == 0)
    def _():
        out_ref[...] = jnp.zeros_like(out_ref)

    def finish(at, real, imag):
        keep = in_step(at.stop - at.start)
        for part, value in enumerate((real, imag)):
            out_ref[part, at] += jnp.where(keep, value, 0.0)

    reduce(maps_ref, backs, finish)


def gram_apply(grams, maps, vector):
    return pl.pallas_call(
        gram_kernel,
        grid=(2,),
        in_specs=[GRAM_SPEC, MAPS_SPEC, VECTOR_SPEC],
        out_specs=VECTOR_SPEC,
        out_shape=VECTOR,
        scratch_shapes=PIECES + BACKS,
        compiler_params=params(),
        name="gram_apply",
    )(grams, maps, vector)


def fold(value):
    return jnp.sum(value.reshape(-1, 8, LANES), 0)


def normal_kernel(
    first_ref, gram_ref, before_ref, after_ref, image_ref, first_edge_ref, last_edge_ref, sums_ref
):
    rr = rw = ww = dd = 0.0
    group = lane_group(FOLD)
    for part in range(2):
        for i in range(8):
            at = slice(i * FOLD, (i + 1) * FOLD)
            value = first_ref[part, at]
            behind = jnp.where(
                group == 0, unfold_phase(before_ref[part], 0, i), pltpu.roll(value, GROUP, 1)
            )
            ahead = jnp.where(
                group == PHASES - 1,
                unfold_phase(after_ref[part], PHASES - 1, i),
                pltpu.roll(value, LANES - GROUP, 1),
            )
            image = (
                gram_ref[part, at]
                + PENALTY * ((value - behind) - (ahead - value))
                + DAMPING * value
            )
            image_ref[part, at] = image
            rr += fold(value * value)
            rw += fold(value * image)
            ww += fold(image * image)
            step = pltpu.roll(image, LANES - GROUP, 1) - image
            dd += fold(jnp.where(group == PHASES - 1, 0.0, step * step))
        whole = image_ref[part]
        first_edge_ref[part] = fold_phase(whole, 0)
        last_edge_ref[part] = fold_phase(whole, PHASES - 1)
    for i, value in enumerate((rr, rw, ww, dd)):
        sums_ref[i] = value


def normal(first, grams_first, before, after):
    return pl.pallas_call(
        normal_kernel,
        out_shape=[
            VECTOR,
            FOLDED,
            FOLDED,
            jax.ShapeDtypeStruct((4, 8, LANES), F32),
        ],
        name="normal",
    )(first, grams_first, before, after)


def curvature_kernel(gram_ref, maps_ref, in_ref, out_ref, *scratch):
    pieces, backs = scratch[:4], scratch[4:]
    half = pl.program_id(0)

    @pl.when(half == 0)
    def _():
        out_ref[...] = jnp.zeros_like(out_ref)

    for at in chunks(32):
        real = spread_half(in_ref[0, at], half)
        imag = spread_half(in_ref[1, at], half)
        for t in range(4):
            for which, value in enumerate(images_of(maps_ref, at, real[t], imag[t])):
                pieces[t][which, at] = value.astype(BF16)
    for t in range(4):
        table_real, table_imag = gram_ref[t, 0], gram_ref[t, 1]
        real, imag = pieces[t][0], pieces[t][1]
        backs[t][0] = dot(table_real, real) - dot(table_imag, imag)
        backs[t][1] = dot(table_real, imag) + dot(table_imag, real)
    total = 0.0
    for at in chunks(32):
        for t in range(4):
            both = pieces[t][0, at].astype(F32) * backs[t][0, at] + pieces[t][1, at].astype(
                F32
            ) * backs[t][1, at]
            total += fold(both[:, :LANES] + both[:, LANES:])
    out_ref[...] += total


def curvature(grams, maps, vector):
    return pl.pallas_call(
        curvature_kernel,
        grid=(2,),
        in_specs=[pl.BlockSpec((4, 2, SIZE, SIZE), lambda i: (i, 0, 0, 0)), MAPS_SPEC, VECTOR_SPEC],
        out_specs=pl.BlockSpec((8, LANES), lambda i: (0, 0)),
        out_shape=jax.ShapeDtypeStruct((8, LANES), F32),
        scratch_shapes=[pltpu.VMEM((2, SIZE, SIZE), BF16)] * 4 + BACKS,
        compiler_params=params(),
        name="curvature",
    )(grams, maps, vector)


def lane_row(values):
    lane = lax.broadcasted_iota(jnp.int32, (1, LANES), 1)
    row = jnp.zeros((1, LANES), F32)
    for i, value in enumerate(values):
        row = jnp.where(lane == i, value, row)
    return row


def whole_sum(value):
    return jnp.sum(jnp.sum(value, 0, keepdims=True), 1, keepdims=True)


def share_kernel(sums_ref, curve_ref, last_ref, after_ref, out_ref):
    rr, rw, ww, dd = (whole_sum(sums_ref[i]) for i in range(4))
    edge = 0.0
    for part in range(2):
        step = after_ref[part] - last_ref[part]
        edge = edge + fold(step * step)
    curve = whole_sum(curve_ref[...]) + PENALTY * (dd + whole_sum(edge)) + DAMPING * ww
    row = lane_row((rr, rw, ww, curve))
    out_ref[...] = jnp.broadcast_to(row[None], out_ref.shape)


def share(sums, curve, last, after):
    return pl.pallas_call(
        share_kernel, out_shape=jax.ShapeDtypeStruct((ALL, 1, LANES), F32), name="share"
    )(sums, curve, last, after)


def solve_kernel(
    shared_ref, frames_ref, residual_ref, product_ref, frames_after_ref, residual_after_ref, product_after_ref, out_ref
):
    row = jnp.sum(shared_ref[...], 0)
    rr, rw, ww, curve = (row[:, i : i + 1] for i in range(4))
    alpha = rr / rw
    fresh = rr - 2.0 * alpha * rw + alpha * alpha * ww
    beta = fresh / rr
    gamma = 1.0 + beta
    bend = gamma * gamma * rw - 2.0 * gamma * alpha * ww + alpha * alpha * curve
    second = fresh / bend
    by_first = alpha + second * gamma
    by_image = -second * alpha
    group = lane_group(ROWS)
    for j in range(ROW_SHARDS):
        at = slice(j * ROWS, (j + 1) * ROWS)
        piece, half = j // 2, slice(j % 2 * ROWS, (j % 2 + 1) * ROWS)
        edge = []
        for part in range(2):
            out_ref[j, part] = (
                frames_ref[part, at]
                + by_first * residual_ref[part, at]
                + by_image * product_ref[part, at]
            )
            after = (
                frames_after_ref[part, half]
                + by_first * residual_after_ref[part, half]
                + by_image * product_after_ref[part, half]
            )
            edge.append(roll(after, part - piece))
        out_ref[j, 2] = jnp.where(group == 0, edge[0], edge[1])


def solve(shared, frames, residual, product, frames_after, residual_after, product_after):
    return pl.pallas_call(
        solve_kernel,
        out_shape=jax.ShapeDtypeStruct((ROW_SHARDS, 3, ROWS, LANES), F32),
        name="solve",
    )(shared, frames, residual, product, frames_after, residual_after, product_after)


def finish_kernel(in_ref, aux_ref, dual_ref, x_ref, new_aux_ref, new_dual_ref, out_ref):
    primal = dual_sum = 0.0
    group = lane_group(8)
    for row in range(0, ROWS, 8):
        at = slice(row, row + 8)
        for half in range(2):
            cols = slice(half * LANES, (half + 1) * LANES)
            parts = []
            for part in range(2):
                blocks = [in_ref[half * 8 + jj, part, at] for jj in range(8)]
                values = transpose_groups(blocks)
                after = None
                for jj in range(8):
                    piece = roll(in_ref[half * 8 + jj, 2, at], jj - part)
                    after = piece if after is None else jnp.where(group == jj, piece, after)
                for t in range(PHASES):
                    x_ref[part, t, at, cols] = values[t]
                parts.append(values + [after])
            for t in range(PHASES):
                dual = [dual_ref[part, t, at, cols] for part in range(2)]
                shifted = [parts[part][t + 1] - parts[part][t] + dual[part] for part in range(2)]
                magnitude = jnp.sqrt(shifted[0] * shifted[0] + shifted[1] * shifted[1])
                factor = jnp.maximum(magnitude - THRESHOLD, 0.0) / jnp.maximum(magnitude, THRESHOLD)
                for part in range(2):
                    new_aux = shifted[part] * factor
                    new_dual = shifted[part] - new_aux
                    new_aux_ref[part, t, at, cols] = new_aux
                    new_dual_ref[part, t, at, cols] = new_dual
                    gap = new_dual - dual[part]
                    primal += gap * gap
                    gap = new_aux - aux_ref[part, t, at, cols]
                    dual_sum += gap * gap
    sums = lane_row((whole_sum(primal), whole_sum(dual_sum)))
    out_ref[...] = jnp.broadcast_to(sums[None], out_ref.shape)


def finish(back, auxiliary, scaled_dual):
    image = jax.ShapeDtypeStruct((2, PHASES, ROWS, SIZE), F32)
    return pl.pallas_call(
        finish_kernel,
        out_shape=[image, image, image, jax.ShapeDtypeStruct((ALL, 1, LANES), F32)],
        name="finish",
    )(back, auxiliary, scaled_dual)


def tables():
    index = np.arange(SIZE)
    angle = (index[:, None] * index[None, :] % SIZE) * (2.0 * math.pi / SIZE)
    out = []
    for table in (np.cos(angle), np.sin(angle)):
        table = (table / math.sqrt(SIZE)).astype(np.float32)
        high = table.astype(BF16)
        out += [high, (table - high.astype(np.float32)).astype(BF16)]
    return np.stack(out)


def shift(value, steps):
    pairs = [(i, (i + steps) % PHASE_SHARDS) for i in range(PHASE_SHARDS)]
    return lax.ppermute(value, "phase", pairs)


def exchange(value, axes):
    return lax.all_to_all(value, axes, 0, 0, tiled=True)


def windows(number, acquired, base, count):
    before = number[:, :, :1] - acquired[:, :, :1] - base
    window = jnp.clip(before, 0, count - ROWS)
    place = lax.broadcasted_iota(jnp.int32, (1, 1, 1, ROWS), 3)
    match = (acquired > 0)[..., None] & (number[..., None] - (1 + base) == window[..., None] + place)
    match = match & (number[..., None] > base) & (number[..., None] <= base + count)
    k = lax.broadcasted_iota(jnp.int32, (1, ROW_SHARDS, ROWS, 1), 1) * ROWS
    k = k + lax.broadcasted_iota(jnp.int32, (1, ROW_SHARDS, ROWS, 1), 2)
    index = jnp.sum(jnp.where(match, k + 1, 0), 2) - 1
    return window.reshape(PHASES * ROW_SHARDS), index.reshape(PHASES, 1, SIZE)


def in_hbm(value):
    return pltpu.with_memory_space_constraint(value, pltpu.HBM)


def local(frames, auxiliary, scaled_dual, coil_maps, measured, sampling):
    table = jnp.asarray(tables())
    lines = measured.reshape(COILS, 2, LINES, SIZE)
    own = lax.dynamic_slice_in_dim(sampling, lax.axis_index("row") * ROWS, ROWS, 1)
    own = own.astype(F32).reshape(1, LINES)

    packed = pack_first(own, lines, *(in_hbm(v) for v in (coil_maps, frames, auxiliary, scaled_dual)))
    image = exchange(packed, "row")
    lines, own, late_sampling, packed = lax.optimization_barrier((lines, own, sampling, packed))
    packed = pack_more(own, lines, 1, 0, MAIN)
    late_sampling, packed = lax.optimization_barrier((late_sampling, packed))
    grams = in_hbm(gram_tables(late_sampling.astype(F32)[:, None, :], table))

    acquired = late_sampling.reshape(PHASES, ROW_SHARDS, ROWS)
    by_phase = jnp.sum(acquired, 2, keepdims=True)
    number = jnp.cumsum(acquired, 2) + jnp.cumsum(by_phase, 0) - by_phase
    overflow = jnp.max(number) > MAIN
    window, index = windows(number, acquired, 0, MAIN)
    line_table = in_hbm(line_tables(index, table))
    image, packed, grams, line_table, window, overflow = lax.optimization_barrier(
        (image, packed, grams, line_table, window, overflow)
    )
    lines_imag = in_hbm(exchange(packed, "row"))
    image = in_hbm(image)

    maps, frames_cols, splits, first, last = receive(image)
    frames_before, frames_after = shift(last, 1), shift(first, -1)
    residual, _, _ = adjoint(0, IMAGE, window, line_table, maps, image, jnp.zeros((2, SIZE, LANES), F32))
    residual = start(grams, maps, frames_cols, splits, frames_before, frames_after, residual)

    residual, first, last = adjoint(1, 0, window, line_table, maps, lines_imag, residual)

    def more(carry):
        residual = carry[1]
        window, index = windows(number, acquired, MAIN, EXTRA)
        line_table = line_tables(index, table)
        for part in range(2):
            extra = exchange(pack_more(own, lines, part, MAIN, EXTRA), "row")
            residual, first, last = adjoint(part, 0, window, line_table, maps, extra, residual)
        return jnp.array(False), residual, first, last

    _, residual, first, last = lax.while_loop(
        lambda carry: carry[0], more, (overflow, residual, first, last)
    )

    residual_before = shift(last, 1)
    residual_after = shift(first, -1)
    grams_residual = gram_apply(grams, maps, residual)
    product, first, last, sums = normal(residual, grams_residual, residual_before, residual_after)
    product_after = shift(first, -1)
    shared = share(sums, curvature(grams, maps, product), last, product_after)
    shared = exchange(shared, ("phase", "row"))
    back = solve(shared, frames_cols, residual, product, frames_after, residual_after, product_after)
    new_frames, new_aux, new_dual, gaps = finish(exchange(back, "row"), auxiliary, scaled_dual)
    gaps = jnp.sum(exchange(gaps, ("phase", "row"))[:, 0, :2], 0)
    residual_norms = jnp.sqrt(gaps) * jnp.array([1.0, PENALTY], F32)
    return new_frames, new_aux, new_dual, residual_norms


def solution(mesh):
    image = P(None, "phase", "row", None)
    in_specs = (
        image,
        image,
        image,
        P(None, None, "row", None),
        P(None, None, "phase", "row", None),
        P("phase", None),
    )
    return jax.shard_map(
        local, mesh=mesh, in_specs=in_specs, out_specs=(image, image, image, P()), check_vma=False
    )
```

```python
import functools
import math

import jax
import jax.numpy as jnp
import numpy as np
from jax import lax
from jax.experimental import pallas as pl
from jax.experimental.pallas import tpu as pltpu
from jax.sharding import PartitionSpec as P

PENALTY = 0.5
DAMPING = 0.1
THRESHOLD = 1.0

COILS = 16
PHASES = 8
ROWS = 16
SIZE = 256
LANES = 128
GROUP = 16
FOLD = 32
LINES = PHASES * ROWS
MAIN = 88
EXTRA = LINES - MAIN
IMAGE = 4 * ROWS
ROW_SHARDS = 16
PHASE_SHARDS = 8
ALL = ROW_SHARDS * PHASE_SHARDS

IN_VMEM = pl.BlockSpec(memory_space=pltpu.VMEM)

F32 = jnp.float32
BF16 = jnp.bfloat16


def lane_bit(rows, bit):
    lane = lax.broadcasted_iota(jnp.int32, (rows, LANES), 1)
    return (lane & (GROUP << bit)) != 0


def lane_group(rows):
    return lax.broadcasted_iota(jnp.int32, (rows, LANES), 1) // GROUP


def roll(value, groups):
    groups %= 8
    if groups == 0:
        return value
    return pltpu.roll(value, groups * GROUP, 1)


def gather_coils(halves):
    rows = halves[0][0].shape[0]
    lane = lax.broadcasted_iota(jnp.int32, (rows, LANES), 1)
    turned = []
    for c, (low, high) in enumerate(halves):
        if c >= 8:
            low, high = high, low
        shift = c % 8
        if shift:
            low, high = roll(low, shift), roll(high, shift)
            wrapped = lane < shift * GROUP
            low, high = jnp.where(wrapped, high, low), jnp.where(wrapped, low, high)
        turned.append((low, high))
    for bit in range(3):
        mask = lane_bit(rows, bit)
        turned = [
            tuple(jnp.where(mask, turned[(i + (1 << bit)) % 16][h], turned[i][h]) for h in range(2))
            for i in range(16)
        ]
    turned = [(turned[i][0], turned[(i + 8) % 16][1]) for i in range(16)]
    return [turned[(-j) % 16] for j in range(16)]


def transpose_groups(values):
    rows = values[0].shape[0]
    turned = [roll(value, a) for a, value in enumerate(values)]
    for bit in range(3):
        mask = lane_bit(rows, bit)
        turned = [jnp.where(mask, turned[(i + (1 << bit)) % 8], turned[i]) for i in range(8)]
    return [roll(turned[(-b) % 8], -b) for b in range(8)]


def spread_half(value, half):
    rows = value.shape[0]
    turned = pltpu.roll(value, 4 * GROUP, 1)
    low = ~lane_bit(rows, 2)
    values = [jnp.where(low == (half == 0), value, turned)]
    for bit in (1, 0):
        low = ~lane_bit(rows, bit)
        spread = []
        for value in values:
            turned = pltpu.roll(value, GROUP << bit, 1)
            spread += [jnp.where(low, value, turned), jnp.where(low, turned, value)]
        values = spread
    return values


def sum_four(values):
    rows = values[0].shape[0]
    for bit in range(2):
        low = ~lane_bit(rows, bit)
        values = [
            jnp.where(low, a, b) + pltpu.roll(jnp.where(low, b, a), GROUP << bit, 1)
            for a, b in zip(values[::2], values[1::2])
        ]
    return values[0] + pltpu.roll(values[0], 4 * GROUP, 1)


def fold_phase(value, phase):
    group = lane_group(FOLD)
    out = None
    for i in range(8):
        piece = roll(value[i * FOLD : (i + 1) * FOLD], i - phase)
        out = piece if out is None else jnp.where(group == i, piece, out)
    return out


def unfold_phase(value, phase, i):
    return roll(value, phase - i)


def split(value):
    high = value.astype(BF16)
    return high, (value - high.astype(F32)).astype(BF16)


def dot(a, b):
    return jnp.dot(a, b, preferred_element_type=F32)


def dot3(table, value):
    return dot(table[0], value[0]) + (dot(table[0], value[1]) + dot(table[1], value[0]))


def wide(value):
    return jnp.concatenate([value, value], 1)


def images_of(maps_ref, at, real, imag):
    maps_real, maps_imag = maps_at(maps_ref, at)
    real, imag = wide(real), wide(imag)
    return maps_real * real - maps_imag * imag, maps_real * imag + maps_imag * real


def maps_at(maps_ref, at):
    return maps_ref[0, at], maps_ref[1, at]


def combine(maps_real, maps_imag, real, imag):
    out_real = maps_real * real + maps_imag * imag
    out_imag = maps_real * imag - maps_imag * real
    return out_real[:, :LANES] + out_real[:, LANES:], out_imag[:, :LANES] + out_imag[:, LANES:]


def chunks(step):
    return [slice(row, row + step) for row in range(0, SIZE, step)]


def store_split(ref, which, at, value):
    ref[which, at], ref[which + 1, at] = split(value)


def expand(vector_ref, maps_ref, pieces):
    half = pl.program_id(0)
    for at in chunks(32):
        real = spread_half(vector_ref[0, at], half)
        imag = spread_half(vector_ref[1, at], half)
        for t in range(4):
            image_real, image_imag = images_of(maps_ref, at, real[t], imag[t])
            store_split(pieces[t], 0, at, image_real)
            store_split(pieces[t], 2, at, image_imag)


def reduce(maps_ref, backs, finish):
    for at in chunks(32):
        maps = maps_at(maps_ref, at)
        terms = [combine(*maps, backs[t][0, at], backs[t][1, at]) for t in range(4)]
        finish(at, sum_four([term[0] for term in terms]), sum_four([term[1] for term in terms]))


def products(tables_ref, pieces, backs):
    for t in range(4):
        real_high, real_low, imag_high, imag_low = (pieces[t][i] for i in range(4))
        table_real, table_imag, low_real, low_imag = (tables_ref[t, i] for i in range(4))
        backs[t][0] = (
            dot(table_real, real_high) + dot(table_real, real_low) + dot(low_real, real_high)
        ) - (dot(table_imag, imag_high) + dot(table_imag, imag_low) + dot(low_imag, imag_high))
        backs[t][1] = (
            dot(table_real, imag_high) + dot(table_real, imag_low) + dot(low_real, imag_high)
        ) + (dot(table_imag, real_high) + dot(table_imag, real_low) + dot(low_imag, real_high))


def in_step(rows):
    return lane_bit(rows, 2) == (pl.program_id(0) == 1)


def split_three(value):
    high = value.astype(BF16)
    value = value - high.astype(F32)
    middle = value.astype(BF16)
    return high, middle, (value - middle.astype(F32)).astype(BF16)


def compact(weight_ref, in_ref, lines_ref, base, at_step):
    count = lines_ref.shape[1]
    weight = jnp.broadcast_to(weight_ref[...], (8, LINES))
    row = lax.broadcasted_iota(jnp.int32, (LINES, LINES), 0)
    col = lax.broadcasted_iota(jnp.int32, (LINES, LINES), 1)
    upto = jnp.where(row <= col, 1.0, 0.0).astype(BF16)
    number = dot(weight.astype(BF16), upto).astype(jnp.int32)
    number = jnp.broadcast_to(number[:1], (count, LINES))
    acquired = jnp.broadcast_to(weight_ref[...], (count, LINES)) > 0.5
    line = lax.broadcasted_iota(jnp.int32, (count, LINES), 0) + (base + 1)
    select = jnp.where((number == line) & acquired, 1.0, 0.0).astype(BF16)
    step = in_ref.shape[0]
    for c in range(step):
        high, middle, low = split_three(in_ref[c, 0])
        lines_ref[at_step * step + c] = (
            dot(select, high) + dot(select, middle) + dot(select, low)
        )


def pack_lines(lines_ref, out_ref):
    for row in range(0, lines_ref.shape[1], 8):
        at = slice(row, row + 8)
        halves = [(lines_ref[c, at, :LANES], lines_ref[c, at, LANES:]) for c in range(COILS)]
        for j, (low, high) in enumerate(gather_coils(halves)):
            out_ref[j, at, :LANES] = low
            out_ref[j, at, LANES:] = high


def pack_image_kernel(maps_ref, frames_ref, aux_ref, dual_ref, out_ref):
    for part in range(2):
        to = slice(part * 8, (part + 1) * 8)
        halves = [(maps_ref[c, part, :, :LANES], maps_ref[c, part, :, LANES:]) for c in range(COILS)]
        for j, (low, high) in enumerate(gather_coils(halves)):
            out_ref[j, to, :LANES] = low
            out_ref[j, to, LANES:] = high
        for half in range(2):
            cols = slice(half * LANES, (half + 1) * LANES)
            frames = [frames_ref[part, t, :, cols] for t in range(PHASES)]
            splits = [aux_ref[part, t, :, cols] - dual_ref[part, t, :, cols] for t in range(PHASES)]
            lanes = slice(part * LANES, (part + 1) * LANES)
            for which, values in ((2, frames), (3, splits)):
                to_rows = slice(which * 8, (which + 1) * 8)
                for jj, value in enumerate(transpose_groups(values)):
                    out_ref[half * 8 + jj, to_rows, lanes] = value


def whole_spec(value):
    return pl.BlockSpec(value.shape, lambda *_: (0,) * len(value.shape))


def pack_image(coil_maps, *images):
    rows = pl.BlockSpec((2, PHASES, 8, SIZE), lambda i: (0, 0, i, 0))
    return pl.pallas_call(
        pack_image_kernel,
        grid=(ROWS // 8,),
        in_specs=[pl.BlockSpec((COILS, 2, 8, SIZE), lambda i: (0, 0, i, 0))] + [rows] * 3,
        out_specs=pl.BlockSpec((ROW_SHARDS, 32, SIZE), lambda i: (0, i, 0)),
        out_shape=jax.ShapeDtypeStruct((ROW_SHARDS, IMAGE, SIZE), F32),
        compiler_params=params(),
        name="pack_image",
    )(coil_maps, *images)


PACK_STEPS = 4


def pack_measured_kernel(base, weight_ref, in_ref, out_ref, lines_ref):
    step = pl.program_id(1)
    compact(weight_ref, in_ref, lines_ref, base, step)

    @pl.when(step == PACK_STEPS - 1)
    def _():
        pack_lines(lines_ref, out_ref)


def pack_measured(weight, measured, base, count):
    return pl.pallas_call(
        functools.partial(pack_measured_kernel, base),
        grid=(2, PACK_STEPS),
        in_specs=[
            whole_spec(weight),
            pl.BlockSpec((COILS // PACK_STEPS, 1, LINES, SIZE), lambda part, i: (i, part, 0, 0)),
        ],
        out_specs=pl.BlockSpec((ROW_SHARDS, count, SIZE), lambda part, i: (0, part, 0)),
        out_shape=jax.ShapeDtypeStruct((ROW_SHARDS, 2 * count, SIZE), F32),
        scratch_shapes=[pltpu.VMEM((COILS, count, SIZE), F32)],
        compiler_params=params(),
        name=f"pack_measured_{base}",
    )(weight, measured)


def line_table_kernel(index_ref, tables_ref, out_ref):
    row = lax.broadcasted_iota(jnp.int32, (SIZE, SIZE), 0)
    select = jnp.where(row == index_ref[0], 1.0, 0.0).astype(BF16)
    for i, table in enumerate((0, 2, 1, 3)):
        out_ref[0, i] = dot(tables_ref[table], select).astype(BF16)


def line_tables(index, tables):
    return pl.pallas_call(
        line_table_kernel,
        grid=(PHASES,),
        in_specs=[pl.BlockSpec((1, 1, SIZE), lambda t: (t, 0, 0)), whole_spec(tables)],
        out_specs=pl.BlockSpec((1, 4, SIZE, SIZE), lambda t: (t, 0, 0, 0)),
        out_shape=jax.ShapeDtypeStruct((PHASES, 4, SIZE, SIZE), BF16),
        compiler_params=params(),
        name="line_tables",
    )(index, tables)


def receive_kernel(image_ref, maps_ref, frames_ref, splits_ref, first_ref, last_ref):
    for part in range(2):
        lanes = slice(part * LANES, (part + 1) * LANES)
        for block in range(ROW_SHARDS):
            for half in range(2):
                row = block * ROWS + half * 8
                at = slice(row, row + 8)
                maps, frames, splits = (
                    slice(half * 32 + which * 8, half * 32 + (which + 1) * 8) for which in (part, 2, 3)
                )
                maps_ref[part, at] = image_ref[block, maps]
                frames_ref[part, at] = image_ref[block, frames, lanes]
                splits_ref[part, at] = image_ref[block, splits, lanes]
        first_ref[part] = fold_phase(frames_ref[part], 0)
        last_ref[part] = fold_phase(frames_ref[part] + splits_ref[part], PHASES - 1)


def receive(image):
    return pl.pallas_call(
        receive_kernel,
        grid=(1,),
        in_specs=[IMAGE_SPEC],
        out_specs=[MAPS_SPEC, VECTOR_SPEC, VECTOR_SPEC, FOLDED_SPEC, FOLDED_SPEC],
        out_shape=[jax.ShapeDtypeStruct((2, SIZE, SIZE), F32), VECTOR, VECTOR, FOLDED, FOLDED],
        compiler_params=params(),
        name="receive",
    )(image)


def gram_table_kernel(weight_ref, tables_ref, out_ref):
    weight = weight_ref[0]
    cos_high, cos_low, sin_high, sin_low = (tables_ref[i] for i in range(4))

    def scaled(table):
        return (table.astype(F32) * weight).astype(BF16)

    cos_w = scaled(cos_high), scaled(cos_low)
    sin_w = scaled(sin_high), scaled(sin_low)
    cos, sin = (cos_high, cos_low), (sin_high, sin_low)
    real = dot3(cos_w, cos) + dot3(sin_w, sin)
    imag = dot3(sin_w, cos) - dot3(cos_w, sin)
    out_ref[0, 0], out_ref[0, 2] = split(real)
    out_ref[0, 1], out_ref[0, 3] = split(imag)


def gram_tables(weight, tables):
    return pl.pallas_call(
        gram_table_kernel,
        grid=(PHASES,),
        in_specs=[
            pl.BlockSpec((1, 1, SIZE), lambda t: (t, 0, 0)),
            pl.BlockSpec((4, SIZE, SIZE), lambda t: (0, 0, 0)),
        ],
        out_specs=pl.BlockSpec((1, 4, SIZE, SIZE), lambda t: (t, 0, 0, 0)),
        out_shape=jax.ShapeDtypeStruct((PHASES, 4, SIZE, SIZE), BF16),
        compiler_params=params(),
        name="gram_tables",
    )(weight, tables)


GRAM_SPEC = pl.BlockSpec((4, 4, SIZE, SIZE), lambda i, *_: (i, 0, 0, 0))
IMAGE_SPEC = pl.BlockSpec((ROW_SHARDS, IMAGE, SIZE), lambda *_: (0, 0, 0))
MAPS_SPEC = pl.BlockSpec((2, SIZE, SIZE), lambda *_: (0, 0, 0))
VECTOR_SPEC = pl.BlockSpec((2, SIZE, LANES), lambda *_: (0, 0, 0))
VECTOR = jax.ShapeDtypeStruct((2, SIZE, LANES), F32)
FOLDED_SPEC = pl.BlockSpec((2, FOLD, LANES), lambda *_: (0, 0, 0))
FOLDED = jax.ShapeDtypeStruct((2, FOLD, LANES), F32)
SUMS_SPEC = pl.BlockSpec((4, 8, LANES), lambda i: (0, 0, 0))
PIECES = [pltpu.VMEM((4, SIZE, SIZE), BF16)] * 4
BACKS = [pltpu.VMEM((2, SIZE, SIZE), F32)] * 4


def params():
    return pltpu.CompilerParams(vmem_limit_bytes=16 << 20)


def start_kernel(gram_ref, maps_ref, frames_ref, out_ref, *scratch):
    pieces, backs = scratch[:4], scratch[4:]

    @pl.when(pl.program_id(0) == 0)
    def _():
        out_ref[...] = jnp.zeros_like(out_ref)

    expand(frames_ref, maps_ref, pieces)
    products(gram_ref, pieces, backs)

    def finish(at, real, imag):
        keep = in_step(at.stop - at.start)
        for part, value in enumerate((real, imag)):
            out_ref[part, at] -= jnp.where(keep, value, 0.0)

    reduce(maps_ref, backs, finish)


def start(grams, maps, frames):
    return pl.pallas_call(
        start_kernel,
        grid=(2,),
        in_specs=[GRAM_SPEC] + [IN_VMEM] * 2,
        out_specs=VECTOR_SPEC,
        out_shape=VECTOR,
        scratch_shapes=PIECES + BACKS,
        compiler_params=params(),
        name="start",
    )(grams, maps, frames)


def add_local(frames_ref, splits_ref, before_ref, after_ref, in_ref, out_ref):
    group = lane_group(FOLD)
    for i in range(8):
        at = slice(i * FOLD, (i + 1) * FOLD)
        for part in range(2):
            frames, splits = frames_ref[part, at], splits_ref[part, at]
            ahead = jnp.where(
                group == PHASES - 1,
                unfold_phase(after_ref[part], PHASES - 1, i),
                pltpu.roll(frames, LANES - GROUP, 1),
            )
            behind = jnp.where(
                group == 0,
                unfold_phase(before_ref[part], 0, i),
                pltpu.roll(frames + splits, GROUP, 1),
            )
            gap = splits - (ahead - frames)
            gap_behind = behind - frames
            out_ref[part, at] = in_ref[part, at] + PENALTY * (gap_behind - gap) - DAMPING * frames


def adjoint_kernel(local_terms, window_ref, tables_ref, maps_ref, lines_ref, in_ref, *refs):
    locals_in, refs = refs[:local_terms], refs[local_terms:]
    out_ref, first_ref, last_ref = refs[:3]
    pieces, backs = refs[3:7], refs[7:]
    half = pl.program_id(0)
    count = lines_ref.shape[1] // 2

    @pl.when(half == 0)
    def _():
        if local_terms:
            add_local(*locals_in, in_ref, out_ref)
        else:
            out_ref[...] = in_ref[...]

    for t in range(4):
        for block in range(ROW_SHARDS):
            at = slice(block * ROWS, (block + 1) * ROWS)
            start = window_ref[(half * 4 + t) * ROW_SHARDS + block]
            aligned = jnp.minimum(start // 8, (count - ROWS) // 8 - 1) * 8
            turn = lax.rem(ROWS + 8 - (start - aligned), ROWS + 8)
            for part in range(2):
                rows = pl.ds(pl.multiple_of(part * count + aligned, 8), ROWS + 8)
                rows = pltpu.roll(lines_ref[block, rows], turn, 0)
                store_split(pieces[t], 2 * part, at, rows[:ROWS])
    products(tables_ref, pieces, backs)

    def finish(at, real, imag):
        keep = in_step(at.stop - at.start)
        for which, value in enumerate((real, imag)):
            out_ref[which, at] += jnp.where(keep, value, 0.0)

    reduce(maps_ref, backs, finish)

    @pl.when(half == 1)
    def _():
        for which in range(2):
            value = out_ref[which]
            first_ref[which] = fold_phase(value, 0)
            last_ref[which] = fold_phase(value, PHASES - 1)


def adjoint(window, tables, maps, lines, so_far, *local_terms):
    return pl.pallas_call(
        functools.partial(adjoint_kernel, len(local_terms)),
        grid_spec=pltpu.PrefetchScalarGridSpec(
            num_scalar_prefetch=1,
            grid=(2,),
            in_specs=[GRAM_SPEC] + [IN_VMEM] * (3 + len(local_terms)),
            out_specs=[IN_VMEM] * 3,
            scratch_shapes=PIECES + BACKS,
        ),
        out_shape=[VECTOR, FOLDED, FOLDED],
        compiler_params=params(),
        name="adjoint",
    )(window, tables, maps, lines, so_far, *local_terms)


def gram_kernel(gram_ref, maps_ref, in_ref, out_ref, *scratch):
    pieces, backs = scratch[:4], scratch[4:]
    expand(in_ref, maps_ref, pieces)
    products(gram_ref, pieces, backs)

    @pl.when(pl.program_id(0) == 0)
    def _():
        out_ref[...] = jnp.zeros_like(out_ref)

    def finish(at, real, imag):
        keep = in_step(at.stop - at.start)
        for part, value in enumerate((real, imag)):
            out_ref[part, at] += jnp.where(keep, value, 0.0)

    reduce(maps_ref, backs, finish)


def gram_apply(grams, maps, vector):
    return pl.pallas_call(
        gram_kernel,
        grid=(2,),
        in_specs=[GRAM_SPEC, IN_VMEM, IN_VMEM],
        out_specs=IN_VMEM,
        out_shape=VECTOR,
        scratch_shapes=PIECES + BACKS,
        compiler_params=params(),
        name="gram_apply",
    )(grams, maps, vector)


def fold(value):
    return jnp.sum(value.reshape(-1, 8, LANES), 0)


def normal_kernel(
    first_ref, gram_ref, before_ref, after_ref, image_ref, first_edge_ref, last_edge_ref, sums_ref
):
    rr = rw = ww = dd = 0.0
    group = lane_group(FOLD)
    for part in range(2):
        for i in range(8):
            at = slice(i * FOLD, (i + 1) * FOLD)
            value = first_ref[part, at]
            behind = jnp.where(
                group == 0, unfold_phase(before_ref[part], 0, i), pltpu.roll(value, GROUP, 1)
            )
            ahead = jnp.where(
                group == PHASES - 1,
                unfold_phase(after_ref[part], PHASES - 1, i),
                pltpu.roll(value, LANES - GROUP, 1),
            )
            image = (
                gram_ref[part, at]
                + PENALTY * ((value - behind) - (ahead - value))
                + DAMPING * value
            )
            image_ref[part, at] = image
            rr += fold(value * value)
            rw += fold(value * image)
            ww += fold(image * image)
            step = pltpu.roll(image, LANES - GROUP, 1) - image
            dd += fold(jnp.where(group == PHASES - 1, 0.0, step * step))
        whole = image_ref[part]
        first_edge_ref[part] = fold_phase(whole, 0)
        last_edge_ref[part] = fold_phase(whole, PHASES - 1)
    for i, value in enumerate((rr, rw, ww, dd)):
        sums_ref[i] = value


def normal(first, grams_first, before, after):
    return pl.pallas_call(
        normal_kernel,
        grid=(1,),
        in_specs=[IN_VMEM] * 4,
        out_specs=[IN_VMEM] * 4,
        out_shape=[
            VECTOR,
            FOLDED,
            FOLDED,
            jax.ShapeDtypeStruct((4, 8, LANES), F32),
        ],
        compiler_params=params(),
        name="normal",
    )(first, grams_first, before, after)


def curvature_kernel(gram_ref, maps_ref, in_ref, out_ref, *scratch):
    pieces, backs = scratch[:4], scratch[4:]

    @pl.when(pl.program_id(0) == 0)
    def _():
        out_ref[...] = jnp.zeros_like(out_ref)

    expand(in_ref, maps_ref, pieces)
    products(gram_ref, pieces, backs)
    total = 0.0
    for at in chunks(32):
        for t in range(4):
            real_high, real_low, imag_high, imag_low = (pieces[t][i, at].astype(F32) for i in range(4))
            both = (real_high + real_low) * backs[t][0, at] + (imag_high + imag_low) * backs[t][1, at]
            total += fold(both[:, :LANES] + both[:, LANES:])
    out_ref[...] += total


def curvature(grams, maps, vector):
    return pl.pallas_call(
        curvature_kernel,
        grid=(2,),
        in_specs=[GRAM_SPEC, IN_VMEM, IN_VMEM],
        out_specs=IN_VMEM,
        out_shape=jax.ShapeDtypeStruct((8, LANES), F32),
        scratch_shapes=PIECES + BACKS,
        compiler_params=params(),
        name="curvature",
    )(grams, maps, vector)


def lane_row(values):
    lane = lax.broadcasted_iota(jnp.int32, (1, LANES), 1)
    row = jnp.zeros((1, LANES), F32)
    for i, value in enumerate(values):
        row = jnp.where(lane == i, value, row)
    return row


def whole_sum(value):
    return jnp.sum(jnp.sum(value, 0, keepdims=True), 1, keepdims=True)


def share_kernel(sums_ref, curve_ref, last_ref, after_ref, out_ref):
    rr, rw, ww, dd = (whole_sum(sums_ref[i]) for i in range(4))
    edge = 0.0
    for part in range(2):
        step = after_ref[part] - last_ref[part]
        edge = edge + fold(step * step)
    curve = whole_sum(curve_ref[...]) + PENALTY * (dd + whole_sum(edge)) + DAMPING * ww
    row = lane_row((rr, rw, ww, curve))
    out_ref[...] = jnp.broadcast_to(row[None], out_ref.shape)


def share(sums, curve, last, after):
    return pl.pallas_call(
        share_kernel,
        grid=(1,),
        in_specs=[IN_VMEM] * 4,
        out_specs=pl.BlockSpec((ALL, 1, LANES), lambda i: (0, 0, 0)),
        out_shape=jax.ShapeDtypeStruct((ALL, 1, LANES), F32),
        compiler_params=params(),
        name="share",
    )(sums, curve, last, after)


def solve_kernel(
    shared_ref, frames_ref, residual_ref, product_ref, frames_after_ref, residual_after_ref, product_after_ref, out_ref
):
    row = jnp.sum(shared_ref[...], 0)
    rr, rw, ww, curve = (row[:, i : i + 1] for i in range(4))
    alpha = rr / rw
    fresh = rr - 2.0 * alpha * rw + alpha * alpha * ww
    beta = fresh / rr
    gamma = 1.0 + beta
    bend = gamma * gamma * rw - 2.0 * gamma * alpha * ww + alpha * alpha * curve
    second = fresh / bend
    by_first = alpha + second * gamma
    by_image = -second * alpha
    group = lane_group(ROWS)
    for j in range(ROW_SHARDS):
        at = slice(j * ROWS, (j + 1) * ROWS)
        piece, half = j // 2, slice(j % 2 * ROWS, (j % 2 + 1) * ROWS)
        edge = []
        for part in range(2):
            out_ref[j, part] = (
                frames_ref[part, at]
                + by_first * residual_ref[part, at]
                + by_image * product_ref[part, at]
            )
            after = (
                frames_after_ref[part, half]
                + by_first * residual_after_ref[part, half]
                + by_image * product_after_ref[part, half]
            )
            edge.append(roll(after, part - piece))
        out_ref[j, 2] = jnp.where(group == 0, edge[0], edge[1])


def solve(shared, frames, residual, product, frames_after, residual_after, product_after):
    return pl.pallas_call(
        solve_kernel,
        grid=(1,),
        in_specs=[IN_VMEM] * 7,
        out_specs=pl.BlockSpec((ROW_SHARDS, 3, ROWS, LANES), lambda i: (0, 0, 0, 0)),
        out_shape=jax.ShapeDtypeStruct((ROW_SHARDS, 3, ROWS, LANES), F32),
        compiler_params=params(),
        name="solve",
    )(shared, frames, residual, product, frames_after, residual_after, product_after)


def finish_kernel(in_ref, aux_ref, dual_ref, x_ref, new_aux_ref, new_dual_ref, out_ref):
    primal = dual_sum = 0.0
    group = lane_group(8)
    for row in range(0, ROWS, 8):
        at = slice(row, row + 8)
        for half in range(2):
            cols = slice(half * LANES, (half + 1) * LANES)
            parts = []
            for part in range(2):
                blocks = [in_ref[half * 8 + jj, part, at] for jj in range(8)]
                values = transpose_groups(blocks)
                after = None
                for jj in range(8):
                    piece = roll(in_ref[half * 8 + jj, 2, at], jj - part)
                    after = piece if after is None else jnp.where(group == jj, piece, after)
                for t in range(PHASES):
                    x_ref[part, t, at, cols] = values[t]
                parts.append(values + [after])
            for t in range(PHASES):
                dual = [dual_ref[part, t, at, cols] for part in range(2)]
                shifted = [parts[part][t + 1] - parts[part][t] + dual[part] for part in range(2)]
                magnitude = jnp.sqrt(shifted[0] * shifted[0] + shifted[1] * shifted[1])
                factor = jnp.maximum(magnitude - THRESHOLD, 0.0) / jnp.maximum(magnitude, THRESHOLD)
                for part in range(2):
                    new_aux = shifted[part] * factor
                    new_dual = shifted[part] - new_aux
                    new_aux_ref[part, t, at, cols] = new_aux
                    new_dual_ref[part, t, at, cols] = new_dual
                    gap = new_dual - dual[part]
                    primal += gap * gap
                    gap = new_aux - aux_ref[part, t, at, cols]
                    dual_sum += gap * gap
    sums = lane_row((whole_sum(primal), whole_sum(dual_sum)))
    out_ref[...] = jnp.broadcast_to(sums[None], out_ref.shape)


def finish(back, auxiliary, scaled_dual):
    image = jax.ShapeDtypeStruct(auxiliary.shape, F32)
    return pl.pallas_call(
        finish_kernel,
        grid=(1,),
        in_specs=[whole_spec(value) for value in (back, auxiliary, scaled_dual)],
        out_specs=[whole_spec(image)] * 3 + [pl.BlockSpec((ALL, 1, LANES), lambda i: (0, 0, 0))],
        out_shape=[image, image, image, jax.ShapeDtypeStruct((ALL, 1, LANES), F32)],
        compiler_params=params(),
        name="finish",
    )(back, auxiliary, scaled_dual)


def tables():
    index = np.arange(SIZE)
    angle = (index[:, None] * index[None, :] % SIZE) * (2.0 * math.pi / SIZE)
    out = []
    for table in (np.cos(angle), np.sin(angle)):
        table = (table / math.sqrt(SIZE)).astype(np.float32)
        high = table.astype(BF16)
        out += [high, (table - high.astype(np.float32)).astype(BF16)]
    return np.stack(out)


def shift(value, steps):
    pairs = [(i, (i + steps) % PHASE_SHARDS) for i in range(PHASE_SHARDS)]
    return lax.ppermute(value, "phase", pairs)


def exchange(value, axes):
    return lax.all_to_all(value, axes, 0, 0, tiled=True)


def windows(number, acquired, base, count):
    before = number[:, :, :1] - acquired[:, :, :1] - base
    window = jnp.clip(before, 0, count - ROWS)
    place = lax.broadcasted_iota(jnp.int32, (1, 1, 1, ROWS), 3)
    match = (acquired > 0)[..., None] & (number[..., None] - (1 + base) == window[..., None] + place)
    match = match & (number[..., None] > base) & (number[..., None] <= base + count)
    k = lax.broadcasted_iota(jnp.int32, (1, ROW_SHARDS, ROWS, 1), 1) * ROWS
    k = k + lax.broadcasted_iota(jnp.int32, (1, ROW_SHARDS, ROWS, 1), 2)
    index = jnp.sum(jnp.where(match, k + 1, 0), 2) - 1
    return window.reshape(PHASES * ROW_SHARDS), index.reshape(PHASES, 1, SIZE)


def in_hbm(value):
    return pltpu.with_memory_space_constraint(value, pltpu.HBM)


def local(frames, auxiliary, scaled_dual, coil_maps, measured, sampling):
    table = jnp.asarray(tables())
    lines = measured.reshape(COILS, 2, LINES, SIZE)
    own = lax.dynamic_slice_in_dim(sampling, lax.axis_index("row") * ROWS, ROWS, 1)
    own = own.astype(F32).reshape(1, LINES)

    packed = pack_image(*(in_hbm(v) for v in (coil_maps, frames, auxiliary, scaled_dual)))
    image = exchange(packed, "row")
    lines, own, packed = lax.optimization_barrier((lines, own, packed))
    packed = pack_measured(own, lines, 0, MAIN)
    packed, late_sampling = lax.optimization_barrier((packed, sampling))
    received = exchange(packed, "row")

    grams = in_hbm(gram_tables(late_sampling.astype(F32)[:, None, :], table))
    maps, frames_cols, splits, first, last = receive(image)
    frames_before, frames_after = shift(last, 1), shift(first, -1)
    residual = start(grams, maps, frames_cols)

    acquired = late_sampling.reshape(PHASES, ROW_SHARDS, ROWS)
    by_phase = jnp.sum(acquired, 2, keepdims=True)
    number = jnp.cumsum(acquired, 2) + jnp.cumsum(by_phase, 0) - by_phase
    overflow = jnp.max(number) > MAIN
    window, index = windows(number, acquired, 0, MAIN)
    line_table = in_hbm(line_tables(index, table))
    residual, first, last = adjoint(
        window, line_table, maps, received, residual, frames_cols, splits, frames_before, frames_after
    )

    def more(carry):
        window, index = windows(number, acquired, MAIN, EXTRA)
        extra = exchange(pack_measured(own, lines, MAIN, EXTRA), "row")
        return jnp.array(False), *adjoint(window, line_tables(index, table), maps, extra, carry[1])

    _, residual, first, last = lax.while_loop(
        lambda carry: carry[0], more, (overflow, residual, first, last)
    )

    residual_before = shift(last, 1)
    residual_after = shift(first, -1)
    grams_residual = gram_apply(grams, maps, residual)
    product, first, last, sums = normal(residual, grams_residual, residual_before, residual_after)
    product_after = shift(first, -1)
    shared = share(sums, curvature(grams, maps, product), last, product_after)
    shared = exchange(shared, ("phase", "row"))
    back = solve(shared, frames_cols, residual, product, frames_after, residual_after, product_after)
    new_frames, new_aux, new_dual, gaps = finish(exchange(back, "row"), auxiliary, scaled_dual)
    gaps = jnp.sum(exchange(gaps, ("phase", "row"))[:, 0, :2], 0)
    residual_norms = jnp.sqrt(gaps) * jnp.array([1.0, PENALTY], F32)
    return new_frames, new_aux, new_dual, residual_norms


def solution(mesh):
    image = P(None, "phase", "row", None)
    in_specs = (
        image,
        image,
        image,
        P(None, None, "row", None),
        P(None, None, "phase", "row", None),
        P("phase", None),
    )
    return jax.shard_map(
        local, mesh=mesh, in_specs=in_specs, out_specs=(image, image, image, P()), check_vma=False
    )
```

```python
import functools
import math

import jax
import jax.numpy as jnp
import numpy as np
from jax import lax
from jax.experimental import pallas as pl
from jax.experimental.pallas import tpu as pltpu
from jax.sharding import PartitionSpec as P

PENALTY = 0.5
DAMPING = 0.1
THRESHOLD = 1.0

COILS = 16
PHASES = 8
ROWS = 16
SIZE = 256
LANES = 128
GROUP = 16
FOLD = 32
LINES = PHASES * ROWS
MAIN = 88
EXTRA = LINES - MAIN
IMAGE = 4 * ROWS
ROW_SHARDS = 16
PHASE_SHARDS = 8
ALL = ROW_SHARDS * PHASE_SHARDS

IN_VMEM = pl.BlockSpec(memory_space=pltpu.VMEM)

F32 = jnp.float32
BF16 = jnp.bfloat16


def lane_bit(rows, bit):
    lane = lax.broadcasted_iota(jnp.int32, (rows, LANES), 1)
    return (lane & (GROUP << bit)) != 0


def lane_group(rows):
    return lax.broadcasted_iota(jnp.int32, (rows, LANES), 1) // GROUP


def roll(value, groups):
    groups %= 8
    if groups == 0:
        return value
    return pltpu.roll(value, groups * GROUP, 1)


def gather_coils(halves):
    rows = halves[0][0].shape[0]
    lane = lax.broadcasted_iota(jnp.int32, (rows, LANES), 1)
    turned = []
    for c, (low, high) in enumerate(halves):
        if c >= 8:
            low, high = high, low
        shift = c % 8
        if shift:
            low, high = roll(low, shift), roll(high, shift)
            wrapped = lane < shift * GROUP
            low, high = jnp.where(wrapped, high, low), jnp.where(wrapped, low, high)
        turned.append((low, high))
    for bit in range(3):
        mask = lane_bit(rows, bit)
        turned = [
            tuple(jnp.where(mask, turned[(i + (1 << bit)) % 16][h], turned[i][h]) for h in range(2))
            for i in range(16)
        ]
    turned = [(turned[i][0], turned[(i + 8) % 16][1]) for i in range(16)]
    return [turned[(-j) % 16] for j in range(16)]


def transpose_groups(values):
    rows = values[0].shape[0]
    turned = [roll(value, a) for a, value in enumerate(values)]
    for bit in range(3):
        mask = lane_bit(rows, bit)
        turned = [jnp.where(mask, turned[(i + (1 << bit)) % 8], turned[i]) for i in range(8)]
    return [roll(turned[(-b) % 8], -b) for b in range(8)]


def spread_half(value, half):
    rows = value.shape[0]
    turned = pltpu.roll(value, 4 * GROUP, 1)
    low = ~lane_bit(rows, 2)
    values = [jnp.where(low == (half == 0), value, turned)]
    for bit in (1, 0):
        low = ~lane_bit(rows, bit)
        spread = []
        for value in values:
            turned = pltpu.roll(value, GROUP << bit, 1)
            spread += [jnp.where(low, value, turned), jnp.where(low, turned, value)]
        values = spread
    return values


def sum_four(values):
    rows = values[0].shape[0]
    for bit in range(2):
        low = ~lane_bit(rows, bit)
        values = [
            jnp.where(low, a, b) + pltpu.roll(jnp.where(low, b, a), GROUP << bit, 1)
            for a, b in zip(values[::2], values[1::2])
        ]
    return values[0] + pltpu.roll(values[0], 4 * GROUP, 1)


def fold_phase(value, phase):
    group = lane_group(FOLD)
    out = None
    for i in range(8):
        piece = roll(value[i * FOLD : (i + 1) * FOLD], i - phase)
        out = piece if out is None else jnp.where(group == i, piece, out)
    return out


def unfold_phase(value, phase, i):
    return roll(value, phase - i)


def split(value):
    high = value.astype(BF16)
    return high, (value - high.astype(F32)).astype(BF16)


def dot(a, b):
    return jnp.dot(a, b, preferred_element_type=F32)


def dot3(table, value):
    return dot(table[0], value[0]) + (dot(table[0], value[1]) + dot(table[1], value[0]))


def wide(value):
    return jnp.concatenate([value, value], 1)


def images_of(maps_ref, at, real, imag):
    maps_real, maps_imag = maps_at(maps_ref, at)
    real, imag = wide(real), wide(imag)
    return maps_real * real - maps_imag * imag, maps_real * imag + maps_imag * real


def maps_at(maps_ref, at):
    return maps_ref[0, at], maps_ref[1, at]


def combine(maps_real, maps_imag, real, imag):
    out_real = maps_real * real + maps_imag * imag
    out_imag = maps_real * imag - maps_imag * real
    return out_real[:, :LANES] + out_real[:, LANES:], out_imag[:, :LANES] + out_imag[:, LANES:]


def row_pairs(step):
    half = SIZE // 2
    return [
        (slice(row, row + step), slice(half + row, half + row + step)) for row in range(0, half, step)
    ]


def store_split(ref, which, at, value):
    ref[which, at], ref[which + 1, at] = split(value)


def expand(vector_ref, maps_ref, pieces):
    half = pl.program_id(0)
    for near, far in row_pairs(16):
        values = [
            [spread_half(vector_ref[part, at], half) for part in range(2)] for at in (near, far)
        ]
        for t in range(4):
            real, imag = images_of(maps_ref, near, values[0][0][t], values[0][1][t])
            far_real, far_imag = images_of(maps_ref, far, values[1][0][t], values[1][1][t])
            store_split(pieces[t], 0, near, real + far_real)
            store_split(pieces[t], 0, far, imag - far_imag)
            store_split(pieces[t], 2, near, imag + far_imag)
            store_split(pieces[t], 2, far, far_real - real)


def reduce(maps_ref, backs, finish):
    for near, far in row_pairs(32):
        near_maps, far_maps = maps_at(maps_ref, near), maps_at(maps_ref, far)
        near_terms, far_terms = [], []
        for t in range(4):
            p_even, p_odd, q_even, q_odd = (
                backs[t][which, at] for which in range(2) for at in (near, far)
            )
            near_terms.append(combine(*near_maps, p_even - q_odd, q_even + p_odd))
            far_terms.append(combine(*far_maps, p_even + q_odd, q_even - p_odd))
        for at, terms in ((near, near_terms), (far, far_terms)):
            finish(at, *(sum_four([term[part] for term in terms]) for part in range(2)))


def products(tables_ref, pieces, backs):
    for t in range(4):
        high, low = tables_ref[t, 0], tables_ref[t, 1]
        for which in range(2):
            value_high, value_low = pieces[t][2 * which], pieces[t][2 * which + 1]
            backs[t][which] = dot(high, value_high) + dot(high, value_low) + dot(low, value_high)


def in_step(rows):
    return lane_bit(rows, 2) == (pl.program_id(0) == 1)


def split_three(value):
    high = value.astype(BF16)
    value = value - high.astype(F32)
    middle = value.astype(BF16)
    return high, middle, (value - middle.astype(F32)).astype(BF16)


def compact(weight_ref, turn_ref, in_ref, lines_ref, base, at_step):
    count = lines_ref.shape[2]
    weight = jnp.broadcast_to(weight_ref[...], (8, LINES))
    row = lax.broadcasted_iota(jnp.int32, (LINES, LINES), 0)
    col = lax.broadcasted_iota(jnp.int32, (LINES, LINES), 1)
    upto = jnp.where(row <= col, 1.0, 0.0).astype(BF16)
    number = dot(weight.astype(BF16), upto).astype(jnp.int32)
    number = jnp.broadcast_to(number[:1], (count, LINES))
    acquired = jnp.broadcast_to(weight_ref[...], (count, LINES)) > 0.5
    line = lax.broadcasted_iota(jnp.int32, (count, LINES), 0) + (base + 1)
    select = jnp.where((number == line) & acquired, 1.0, 0.0).astype(BF16)
    step = in_ref.shape[0]
    cos, sin = (jnp.concatenate([turn_ref[i]] * 2, 1) for i in range(2))
    for c in range(step):
        real, imag = in_ref[c, 0], in_ref[c, 1]
        for part, value in enumerate((real * cos - imag * sin, real * sin + imag * cos)):
            high, middle, low = split_three(value)
            lines_ref[part, at_step * step + c] = (
                dot(select, high) + dot(select, middle) + dot(select, low)
            )


def pack_lines(lines_ref, out_ref):
    count = lines_ref.shape[2]
    for part in range(2):
        for row in range(0, count, 8):
            at = slice(row, row + 8)
            to = slice(part * count + row, part * count + row + 8)
            halves = [
                (lines_ref[part, c, at, :LANES], lines_ref[part, c, at, LANES:]) for c in range(COILS)
            ]
            for j, (low, high) in enumerate(gather_coils(halves)):
                out_ref[j, to, :LANES] = low
                out_ref[j, to, LANES:] = high


def pack_image_kernel(maps_ref, frames_ref, aux_ref, dual_ref, out_ref):
    for part in range(2):
        to = slice(part * 8, (part + 1) * 8)
        halves = [(maps_ref[c, part, :, :LANES], maps_ref[c, part, :, LANES:]) for c in range(COILS)]
        for j, (low, high) in enumerate(gather_coils(halves)):
            out_ref[j, to, :LANES] = low
            out_ref[j, to, LANES:] = high
        for half in range(2):
            cols = slice(half * LANES, (half + 1) * LANES)
            frames = [frames_ref[part, t, :, cols] for t in range(PHASES)]
            splits = [aux_ref[part, t, :, cols] - dual_ref[part, t, :, cols] for t in range(PHASES)]
            lanes = slice(part * LANES, (part + 1) * LANES)
            for which, values in ((2, frames), (3, splits)):
                to_rows = slice(which * 8, (which + 1) * 8)
                for jj, value in enumerate(transpose_groups(values)):
                    out_ref[half * 8 + jj, to_rows, lanes] = value


def whole_spec(value):
    return pl.BlockSpec(value.shape, lambda *_: (0,) * len(value.shape))


def pack_image(coil_maps, *images):
    rows = pl.BlockSpec((2, PHASES, 8, SIZE), lambda i: (0, 0, i, 0))
    return pl.pallas_call(
        pack_image_kernel,
        grid=(ROWS // 8,),
        in_specs=[pl.BlockSpec((COILS, 2, 8, SIZE), lambda i: (0, 0, i, 0))] + [rows] * 3,
        out_specs=pl.BlockSpec((ROW_SHARDS, 32, SIZE), lambda i: (0, i, 0)),
        out_shape=jax.ShapeDtypeStruct((ROW_SHARDS, IMAGE, SIZE), F32),
        compiler_params=params(),
        name="pack_image",
    )(coil_maps, *images)


PACK_STEPS = 4


def pack_measured_kernel(base, weight_ref, turn_ref, in_ref, out_ref, lines_ref):
    step = pl.program_id(0)
    compact(weight_ref, turn_ref, in_ref, lines_ref, base, step)

    @pl.when(step == PACK_STEPS - 1)
    def _():
        pack_lines(lines_ref, out_ref)


def pack_measured(weight, turn, measured, base, count):
    return pl.pallas_call(
        functools.partial(pack_measured_kernel, base),
        grid=(PACK_STEPS,),
        in_specs=[
            whole_spec(weight),
            whole_spec(turn),
            pl.BlockSpec((COILS // PACK_STEPS, 2, LINES, SIZE), lambda i: (i, 0, 0, 0)),
        ],
        out_specs=pl.BlockSpec((ROW_SHARDS, 2 * count, SIZE), lambda i: (0, 0, 0)),
        out_shape=jax.ShapeDtypeStruct((ROW_SHARDS, 2 * count, SIZE), F32),
        scratch_shapes=[pltpu.VMEM((2, COILS, count, SIZE), F32)],
        compiler_params=params(),
        name=f"pack_measured_{base}",
    )(weight, turn, measured)


def line_table_kernel(index_ref, tables_ref, out_ref):
    row = lax.broadcasted_iota(jnp.int32, (SIZE, SIZE), 0)
    select = jnp.where(row == index_ref[0], 1.0, 0.0).astype(BF16)
    for i in range(2):
        out_ref[0, i] = dot(tables_ref[i], select).astype(BF16)


def line_tables(index, tables):
    return pl.pallas_call(
        line_table_kernel,
        grid=(PHASES,),
        in_specs=[pl.BlockSpec((1, 1, SIZE), lambda t: (t, 0, 0)), whole_spec(tables)],
        out_specs=pl.BlockSpec((1, 2, SIZE, SIZE), lambda t: (t, 0, 0, 0)),
        out_shape=jax.ShapeDtypeStruct((PHASES, 2, SIZE, SIZE), BF16),
        compiler_params=params(),
        name="line_tables",
    )(index, tables)


def reverse_eight(value):
    row = lax.broadcasted_iota(jnp.int32, value.shape, 0)
    value = pltpu.roll(value, 4, 0)
    for bit in (2, 1):
        value = jnp.where((row & bit) != 0, pltpu.roll(value, bit, 0), pltpu.roll(value, 8 - bit, 0))
    return value


def receive_kernel(image_ref, maps_ref, frames_ref, splits_ref, first_ref, last_ref):
    for part in range(2):
        lanes = slice(part * LANES, (part + 1) * LANES)
        for block in range(ROW_SHARDS):
            turned = block >= ROW_SHARDS // 2
            source = ROW_SHARDS + ROW_SHARDS // 2 - 1 - block if turned else block
            for half in range(2):
                row = block * ROWS + half * 8
                at = slice(row, row + 8)
                start = 32 * (1 - half if turned else half)
                maps, frames, splits = (
                    image_ref[source, start + which * 8 : start + (which + 1) * 8, columns]
                    for which, columns in ((part, slice(0, SIZE)), (2, lanes), (3, lanes))
                )
                if turned:
                    maps, frames, splits = (reverse_eight(v) for v in (maps, frames, splits))
                maps_ref[part, at] = maps
                frames_ref[part, at] = frames
                splits_ref[part, at] = splits
        first_ref[part] = fold_phase(frames_ref[part], 0)
        last_ref[part] = fold_phase(frames_ref[part] + splits_ref[part], PHASES - 1)


def receive(image):
    return pl.pallas_call(
        receive_kernel,
        grid=(1,),
        in_specs=[IMAGE_SPEC],
        out_specs=[MAPS_SPEC, VECTOR_SPEC, VECTOR_SPEC, FOLDED_SPEC, FOLDED_SPEC],
        out_shape=[jax.ShapeDtypeStruct((2, SIZE, SIZE), F32), VECTOR, VECTOR, FOLDED, FOLDED],
        compiler_params=params(),
        name="receive",
    )(image)


def gram_table_kernel(weight_ref, tables_ref, out_ref):
    weight = weight_ref[0]
    left = tuple((tables_ref[i].astype(F32) * weight).astype(BF16) for i in range(2))
    right = tables_ref[2], tables_ref[3]
    out_ref[0, 0], out_ref[0, 1] = split(dot3(left, right))


def gram_tables(weight, tables):
    return pl.pallas_call(
        gram_table_kernel,
        grid=(PHASES,),
        in_specs=[
            pl.BlockSpec((1, 1, SIZE), lambda t: (t, 0, 0)),
            pl.BlockSpec((4, SIZE, SIZE), lambda t: (0, 0, 0)),
        ],
        out_specs=pl.BlockSpec((1, 2, SIZE, SIZE), lambda t: (t, 0, 0, 0)),
        out_shape=jax.ShapeDtypeStruct((PHASES, 2, SIZE, SIZE), BF16),
        compiler_params=params(),
        name="gram_tables",
    )(weight, tables)


GRAM_SPEC = pl.BlockSpec((4, 2, SIZE, SIZE), lambda i, *_: (i, 0, 0, 0))
IMAGE_SPEC = pl.BlockSpec((ROW_SHARDS, IMAGE, SIZE), lambda *_: (0, 0, 0))
MAPS_SPEC = pl.BlockSpec((2, SIZE, SIZE), lambda *_: (0, 0, 0))
VECTOR_SPEC = pl.BlockSpec((2, SIZE, LANES), lambda *_: (0, 0, 0))
VECTOR = jax.ShapeDtypeStruct((2, SIZE, LANES), F32)
FOLDED_SPEC = pl.BlockSpec((2, FOLD, LANES), lambda *_: (0, 0, 0))
FOLDED = jax.ShapeDtypeStruct((2, FOLD, LANES), F32)
SUMS_SPEC = pl.BlockSpec((4, 8, LANES), lambda i: (0, 0, 0))
PIECES = [pltpu.VMEM((4, SIZE, SIZE), BF16)] * 4
BACKS = [pltpu.VMEM((2, SIZE, SIZE), F32)] * 4


def params():
    return pltpu.CompilerParams(vmem_limit_bytes=16 << 20)


def start_kernel(gram_ref, maps_ref, frames_ref, splits_ref, in_ref, out_ref, *scratch):
    pieces, backs = scratch[:4], scratch[4:]

    @pl.when(pl.program_id(0) == 0)
    def _():
        group = lane_group(FOLD)
        for row in range(0, SIZE, FOLD):
            at = slice(row, row + FOLD)
            for part in range(2):
                frames, splits = frames_ref[part, at], splits_ref[part, at]
                ahead = pltpu.roll(frames, LANES - GROUP, 1)
                behind = pltpu.roll(frames + splits, GROUP, 1)
                gap = splits - (jnp.where(group == PHASES - 1, 0.0, ahead) - frames)
                gap_behind = jnp.where(group == 0, 0.0, behind) - frames
                out_ref[part, at] = in_ref[part, at] + PENALTY * (gap_behind - gap) - DAMPING * frames

    expand(frames_ref, maps_ref, pieces)
    products(gram_ref, pieces, backs)

    def finish(at, real, imag):
        keep = in_step(at.stop - at.start)
        for part, value in enumerate((real, imag)):
            out_ref[part, at] -= jnp.where(keep, value, 0.0)

    reduce(maps_ref, backs, finish)


def start(grams, maps, frames, splits, so_far):
    return pl.pallas_call(
        start_kernel,
        grid=(2,),
        in_specs=[GRAM_SPEC] + [IN_VMEM] * 4,
        out_specs=VECTOR_SPEC,
        out_shape=VECTOR,
        scratch_shapes=PIECES + BACKS,
        compiler_params=params(),
        name="start",
    )(grams, maps, frames, splits, so_far)


def add_edges(before_ref, after_ref, in_ref, out_ref):
    group = lane_group(FOLD)
    for i in range(8):
        at = slice(i * FOLD, (i + 1) * FOLD)
        for part in range(2):
            before = unfold_phase(before_ref[part], 0, i)
            after = unfold_phase(after_ref[part], PHASES - 1, i)
            edge = jnp.where(group == 0, before, jnp.where(group == PHASES - 1, after, 0.0))
            out_ref[part, at] = in_ref[part, at] + PENALTY * edge


def adjoint_kernel(edges, window_ref, tables_ref, maps_ref, lines_ref, in_ref, *refs):
    edges_in, refs = refs[:edges], refs[edges:]
    out_ref, first_ref, last_ref = refs[:3]
    pieces, backs = refs[3:7], refs[7:]
    half = pl.program_id(0)
    count = lines_ref.shape[1] // 2

    @pl.when(half == 0)
    def _():
        if edges:
            add_edges(*edges_in, in_ref, out_ref)
        else:
            out_ref[...] = in_ref[...]

    for t in range(4):
        for block in range(ROW_SHARDS):
            at = slice(block * ROWS, (block + 1) * ROWS)
            start = window_ref[(half * 4 + t) * ROW_SHARDS + block]
            aligned = jnp.minimum(start // 8, (count - ROWS) // 8 - 1) * 8
            turn = lax.rem(ROWS + 8 - (start - aligned), ROWS + 8)
            for part in range(2):
                rows = pl.ds(pl.multiple_of(part * count + aligned, 8), ROWS + 8)
                rows = pltpu.roll(lines_ref[block, rows], turn, 0)
                store_split(pieces[t], 2 * part, at, rows[:ROWS])
    products(tables_ref, pieces, backs)

    def finish(at, real, imag):
        keep = in_step(at.stop - at.start)
        for which, value in enumerate((real, imag)):
            out_ref[which, at] += jnp.where(keep, value, 0.0)

    reduce(maps_ref, backs, finish)

    @pl.when(half == 1)
    def _():
        for which in range(2):
            value = out_ref[which]
            first_ref[which] = fold_phase(value, 0)
            last_ref[which] = fold_phase(value, PHASES - 1)


def adjoint(window, tables, maps, lines, so_far, *edges):
    return pl.pallas_call(
        functools.partial(adjoint_kernel, len(edges)),
        grid_spec=pltpu.PrefetchScalarGridSpec(
            num_scalar_prefetch=1,
            grid=(2,),
            in_specs=[GRAM_SPEC] + [IN_VMEM] * (3 + len(edges)),
            out_specs=[IN_VMEM] * 3,
            scratch_shapes=PIECES + BACKS,
        ),
        out_shape=[VECTOR, FOLDED, FOLDED],
        compiler_params=params(),
        name="adjoint",
    )(window, tables, maps, lines, so_far, *edges)


def gram_kernel(gram_ref, maps_ref, in_ref, out_ref, *scratch):
    pieces, backs = scratch[:4], scratch[4:]
    expand(in_ref, maps_ref, pieces)
    products(gram_ref, pieces, backs)

    def finish(at, real, imag):
        keep = in_step(at.stop - at.start)
        for part, value in enumerate((real, imag)):
            out_ref[part, at] = jnp.where(keep, value, out_ref[part, at])

    reduce(maps_ref, backs, finish)


def gram_apply(grams, maps, vector):
    return pl.pallas_call(
        gram_kernel,
        grid=(2,),
        in_specs=[GRAM_SPEC, IN_VMEM, IN_VMEM],
        out_specs=IN_VMEM,
        out_shape=VECTOR,
        scratch_shapes=PIECES + BACKS,
        compiler_params=params(),
        name="gram_apply",
    )(grams, maps, vector)


def fold(value):
    return jnp.sum(value.reshape(-1, 8, LANES), 0)


def normal_kernel(
    first_ref, gram_ref, before_ref, after_ref, image_ref, first_edge_ref, last_edge_ref, sums_ref
):
    rr = rw = ww = dd = 0.0
    group = lane_group(FOLD)
    for part in range(2):
        for i in range(8):
            at = slice(i * FOLD, (i + 1) * FOLD)
            value = first_ref[part, at]
            behind = jnp.where(
                group == 0, unfold_phase(before_ref[part], 0, i), pltpu.roll(value, GROUP, 1)
            )
            ahead = jnp.where(
                group == PHASES - 1,
                unfold_phase(after_ref[part], PHASES - 1, i),
                pltpu.roll(value, LANES - GROUP, 1),
            )
            image = (
                gram_ref[part, at]
                + PENALTY * ((value - behind) - (ahead - value))
                + DAMPING * value
            )
            image_ref[part, at] = image
            rr += fold(value * value)
            rw += fold(value * image)
            ww += fold(image * image)
            step = pltpu.roll(image, LANES - GROUP, 1) - image
            dd += fold(jnp.where(group == PHASES - 1, 0.0, step * step))
        whole = image_ref[part]
        first_edge_ref[part] = fold_phase(whole, 0)
        last_edge_ref[part] = fold_phase(whole, PHASES - 1)
    for i, value in enumerate((rr, rw, ww, dd)):
        sums_ref[i] = value


def normal(first, grams_first, before, after):
    return pl.pallas_call(
        normal_kernel,
        grid=(1,),
        in_specs=[IN_VMEM] * 4,
        out_specs=[IN_VMEM] * 4,
        out_shape=[
            VECTOR,
            FOLDED,
            FOLDED,
            jax.ShapeDtypeStruct((4, 8, LANES), F32),
        ],
        compiler_params=params(),
        name="normal",
    )(first, grams_first, before, after)


def curvature_kernel(gram_ref, maps_ref, in_ref, out_ref, *scratch):
    pieces, backs = scratch[:4], scratch[4:]

    @pl.when(pl.program_id(0) == 0)
    def _():
        out_ref[...] = jnp.zeros_like(out_ref)

    expand(in_ref, maps_ref, pieces)
    products(gram_ref, pieces, backs)
    total = 0.0
    for row in range(0, SIZE, 32):
        at = slice(row, row + 32)
        for t in range(4):
            p_high, p_low, q_high, q_low = (pieces[t][i, at].astype(F32) for i in range(4))
            both = (p_high + p_low) * backs[t][0, at] + (q_high + q_low) * backs[t][1, at]
            total += fold(both[:, :LANES] + both[:, LANES:])
    out_ref[...] += total


def curvature(grams, maps, vector):
    return pl.pallas_call(
        curvature_kernel,
        grid=(2,),
        in_specs=[GRAM_SPEC, IN_VMEM, IN_VMEM],
        out_specs=IN_VMEM,
        out_shape=jax.ShapeDtypeStruct((8, LANES), F32),
        scratch_shapes=PIECES + BACKS,
        compiler_params=params(),
        name="curvature",
    )(grams, maps, vector)


def lane_row(values):
    lane = lax.broadcasted_iota(jnp.int32, (1, LANES), 1)
    row = jnp.zeros((1, LANES), F32)
    for i, value in enumerate(values):
        row = jnp.where(lane == i, value, row)
    return row


def whole_sum(value):
    return jnp.sum(jnp.sum(value, 0, keepdims=True), 1, keepdims=True)


def share_kernel(sums_ref, curve_ref, last_ref, after_ref, out_ref):
    rr, rw, ww, dd = (whole_sum(sums_ref[i]) for i in range(4))
    edge = 0.0
    for part in range(2):
        step = after_ref[part] - last_ref[part]
        edge = edge + fold(step * step)
    curve = whole_sum(curve_ref[...]) + PENALTY * (dd + whole_sum(edge)) + DAMPING * ww
    row = lane_row((rr, rw, ww, curve))
    out_ref[...] = jnp.broadcast_to(row[None], out_ref.shape)


def share(sums, curve, last, after):
    return pl.pallas_call(
        share_kernel,
        grid=(1,),
        in_specs=[IN_VMEM] * 4,
        out_specs=pl.BlockSpec((ALL, 1, LANES), lambda i: (0, 0, 0)),
        out_shape=jax.ShapeDtypeStruct((ALL, 1, LANES), F32),
        compiler_params=params(),
        name="share",
    )(sums, curve, last, after)


def solve_kernel(
    shared_ref, frames_ref, residual_ref, product_ref, frames_after_ref, residual_after_ref, product_after_ref, out_ref
):
    row = jnp.sum(shared_ref[...], 0)
    rr, rw, ww, curve = (row[:, i : i + 1] for i in range(4))
    alpha = rr / rw
    fresh = rr - 2.0 * alpha * rw + alpha * alpha * ww
    beta = fresh / rr
    gamma = 1.0 + beta
    bend = gamma * gamma * rw - 2.0 * gamma * alpha * ww + alpha * alpha * curve
    second = fresh / bend
    by_first = alpha + second * gamma
    by_image = -second * alpha
    group = lane_group(8)
    for j in range(ROW_SHARDS):
        turned = j >= ROW_SHARDS // 2
        block = ROW_SHARDS + ROW_SHARDS // 2 - 1 - j if turned else j
        for row in range(0, ROWS, 8):
            at = slice(block * ROWS + row, block * ROWS + row + 8)
            piece, start = divmod(at.start, FOLD)
            folded = slice(start, start + 8)
            values = [
                frames_ref[part, at]
                + by_first * residual_ref[part, at]
                + by_image * product_ref[part, at]
                for part in range(2)
            ]
            edge = [
                roll(
                    frames_after_ref[part, folded]
                    + by_first * residual_after_ref[part, folded]
                    + by_image * product_after_ref[part, folded],
                    part - piece,
                )
                for part in range(2)
            ]
            values.append(jnp.where(group == 0, edge[0], edge[1]))
            to = slice(ROWS - 8 - row, ROWS - row) if turned else slice(row, row + 8)
            for which, value in enumerate(values):
                out_ref[j, which, to] = reverse_eight(value) if turned else value


def solve(shared, frames, residual, product, frames_after, residual_after, product_after):
    return pl.pallas_call(
        solve_kernel,
        grid=(1,),
        in_specs=[IN_VMEM] * 7,
        out_specs=pl.BlockSpec((ROW_SHARDS, 3, ROWS, LANES), lambda i: (0, 0, 0, 0)),
        out_shape=jax.ShapeDtypeStruct((ROW_SHARDS, 3, ROWS, LANES), F32),
        compiler_params=params(),
        name="solve",
    )(shared, frames, residual, product, frames_after, residual_after, product_after)


def finish_kernel(in_ref, aux_ref, dual_ref, x_ref, new_aux_ref, new_dual_ref, out_ref):
    primal = dual_sum = 0.0
    group = lane_group(8)
    for row in range(0, ROWS, 8):
        at = slice(row, row + 8)
        for half in range(2):
            cols = slice(half * LANES, (half + 1) * LANES)
            parts = []
            for part in range(2):
                blocks = [in_ref[half * 8 + jj, part, at] for jj in range(8)]
                values = transpose_groups(blocks)
                after = None
                for jj in range(8):
                    piece = roll(in_ref[half * 8 + jj, 2, at], jj - part)
                    after = piece if after is None else jnp.where(group == jj, piece, after)
                for t in range(PHASES):
                    x_ref[part, t, at, cols] = values[t]
                parts.append(values + [after])
            for t in range(PHASES):
                dual = [dual_ref[part, t, at, cols] for part in range(2)]
                shifted = [parts[part][t + 1] - parts[part][t] + dual[part] for part in range(2)]
                magnitude = jnp.sqrt(shifted[0] * shifted[0] + shifted[1] * shifted[1])
                factor = jnp.maximum(magnitude - THRESHOLD, 0.0) / jnp.maximum(magnitude, THRESHOLD)
                for part in range(2):
                    new_aux = shifted[part] * factor
                    new_dual = shifted[part] - new_aux
                    new_aux_ref[part, t, at, cols] = new_aux
                    new_dual_ref[part, t, at, cols] = new_dual
                    gap = new_dual - dual[part]
                    primal += gap * gap
                    gap = new_aux - aux_ref[part, t, at, cols]
                    dual_sum += gap * gap
    sums = lane_row((whole_sum(primal), whole_sum(dual_sum)))
    out_ref[...] = jnp.broadcast_to(sums[None], out_ref.shape)


def finish(back, auxiliary, scaled_dual):
    image = jax.ShapeDtypeStruct(auxiliary.shape, F32)
    return pl.pallas_call(
        finish_kernel,
        grid=(1,),
        in_specs=[whole_spec(value) for value in (back, auxiliary, scaled_dual)],
        out_specs=[whole_spec(image)] * 3 + [pl.BlockSpec((ALL, 1, LANES), lambda i: (0, 0, 0))],
        out_shape=[image, image, image, jax.ShapeDtypeStruct((ALL, 1, LANES), F32)],
        compiler_params=params(),
        name="finish",
    )(back, auxiliary, scaled_dual)


def tables():
    k = np.arange(SIZE)
    x = np.arange(SIZE // 2)
    unit = 2.0 * math.pi / (2 * SIZE)
    angle = (k[None, :] * (2 * x[:, None] - (SIZE - 1)) % (2 * SIZE)) * unit
    table = (np.concatenate([np.cos(angle), np.sin(angle)]) / math.sqrt(SIZE)).astype(np.float32)
    high = table.astype(BF16)
    low = (table - high.astype(np.float32)).astype(BF16)
    turn = (k * (SIZE - 1) % (2 * SIZE)) * unit
    turn = np.stack([np.cos(turn), np.sin(turn)]).astype(np.float32)
    return np.stack([high, low, high.T, low.T]), turn


def shift(value, steps):
    pairs = [(i, (i + steps) % PHASE_SHARDS) for i in range(PHASE_SHARDS)]
    return lax.ppermute(value, "phase", pairs)


def exchange(value, axes):
    return lax.all_to_all(value, axes, 0, 0, tiled=True)


def windows(number, acquired, base, count):
    before = number[:, :, :1] - acquired[:, :, :1] - base
    window = jnp.clip(before, 0, count - ROWS)
    place = lax.broadcasted_iota(jnp.int32, (1, 1, 1, ROWS), 3)
    match = (acquired > 0)[..., None] & (number[..., None] - (1 + base) == window[..., None] + place)
    match = match & (number[..., None] > base) & (number[..., None] <= base + count)
    k = lax.broadcasted_iota(jnp.int32, (1, ROW_SHARDS, ROWS, 1), 1) * ROWS
    k = k + lax.broadcasted_iota(jnp.int32, (1, ROW_SHARDS, ROWS, 1), 2)
    index = jnp.sum(jnp.where(match, k + 1, 0), 2) - 1
    return window.reshape(PHASES * ROW_SHARDS), index.reshape(PHASES, 1, SIZE)


def in_hbm(value):
    return pltpu.with_memory_space_constraint(value, pltpu.HBM)


def local(frames, auxiliary, scaled_dual, coil_maps, measured, sampling):
    table, turn = (jnp.asarray(value) for value in tables())
    lines = measured.reshape(COILS, 2, LINES, SIZE)
    own = lax.dynamic_slice_in_dim(sampling, lax.axis_index("row") * ROWS, ROWS, 1)
    own = own.astype(F32).reshape(1, LINES)

    packed = pack_image(*(in_hbm(v) for v in (coil_maps, frames, auxiliary, scaled_dual)))
    image = exchange(packed, "row")
    lines, own, turn, packed = lax.optimization_barrier((lines, own, turn, packed))
    turn = lax.dynamic_slice_in_dim(turn, lax.axis_index("row") * ROWS, ROWS, 1)
    turn = jnp.broadcast_to(turn[:, None, :, None], (2, PHASES, ROWS, LANES)).reshape(2, LINES, LANES)
    packed = pack_measured(own, turn, lines, 0, MAIN)
    packed, late_sampling = lax.optimization_barrier((packed, sampling))
    acquired = late_sampling.reshape(PHASES, ROW_SHARDS, ROWS)
    by_phase = jnp.sum(acquired, 2, keepdims=True)
    number = jnp.cumsum(acquired, 2) + jnp.cumsum(by_phase, 0) - by_phase
    overflow = jnp.max(number) > MAIN

    def more(carry):
        window, index = windows(number, acquired, MAIN, EXTRA)
        maps = receive(image)[0]
        extra = exchange(pack_measured(own, turn, lines, MAIN, EXTRA), "row")
        residual, _, _ = adjoint(window, line_tables(index, table), maps, extra, carry[1])
        return jnp.array(False), residual

    _, residual = lax.while_loop(
        lambda carry: carry[0], more, (overflow, jnp.zeros((2, SIZE, LANES), F32))
    )
    packed, residual = lax.optimization_barrier((packed, residual))
    received = exchange(packed, "row")

    grams = in_hbm(gram_tables(late_sampling.astype(F32)[:, None, :], table))
    maps, frames_cols, splits, first, last = receive(image)
    frames_before, frames_after = shift(last, 1), shift(first, -1)
    residual = start(grams, maps, frames_cols, splits, residual)

    window, index = windows(number, acquired, 0, MAIN)
    line_table = in_hbm(line_tables(index, table))
    residual, first, last = adjoint(
        window, line_table, maps, received, residual, frames_before, frames_after
    )

    residual_before = shift(last, 1)
    residual_after = shift(first, -1)
    grams_residual = gram_apply(grams, maps, residual)
    product, first, last, sums = normal(residual, grams_residual, residual_before, residual_after)
    product_after = shift(first, -1)
    shared = share(sums, curvature(grams, maps, product), last, product_after)
    shared = exchange(shared, ("phase", "row"))
    back = solve(shared, frames_cols, residual, product, frames_after, residual_after, product_after)
    new_frames, new_aux, new_dual, gaps = finish(exchange(back, "row"), auxiliary, scaled_dual)
    gaps = jnp.sum(exchange(gaps, ("phase", "row"))[:, 0, :2], 0)
    residual_norms = jnp.sqrt(gaps) * jnp.array([1.0, PENALTY], F32)
    return new_frames, new_aux, new_dual, residual_norms


def solution(mesh):
    image = P(None, "phase", "row", None)
    in_specs = (
        image,
        image,
        image,
        P(None, None, "row", None),
        P(None, None, "phase", "row", None),
        P("phase", None),
    )
    return jax.shard_map(
        local, mesh=mesh, in_specs=in_specs, out_specs=(image, image, image, P()), check_vma=False
    )
```

```python
import functools
import math

import jax
import jax.numpy as jnp
import numpy as np
from jax import lax
from jax.experimental import pallas as pl
from jax.experimental.pallas import tpu as pltpu
from jax.sharding import PartitionSpec as P

PENALTY = 0.5
DAMPING = 0.1
THRESHOLD = 1.0

COILS = 16
PHASES = 8
ROWS = 16
SIZE = 256
LANES = 128
GROUP = 16
FOLD = 32
LINES = PHASES * ROWS
MAIN = 88
EXTRA = LINES - MAIN
IMAGE = 4 * ROWS
ROW_SHARDS = 16
PHASE_SHARDS = 8
ALL = ROW_SHARDS * PHASE_SHARDS

IN_VMEM = pl.BlockSpec(memory_space=pltpu.VMEM)

F32 = jnp.float32
BF16 = jnp.bfloat16


def lane_bit(rows, bit):
    lane = lax.broadcasted_iota(jnp.int32, (rows, LANES), 1)
    return (lane & (GROUP << bit)) != 0


def lane_group(rows):
    return lax.broadcasted_iota(jnp.int32, (rows, LANES), 1) // GROUP


def roll(value, groups):
    groups %= 8
    if groups == 0:
        return value
    return pltpu.roll(value, groups * GROUP, 1)


def gather_coils(halves):
    rows = halves[0][0].shape[0]
    lane = lax.broadcasted_iota(jnp.int32, (rows, LANES), 1)
    turned = []
    for c, (low, high) in enumerate(halves):
        if c >= 8:
            low, high = high, low
        shift = c % 8
        if shift:
            low, high = roll(low, shift), roll(high, shift)
            wrapped = lane < shift * GROUP
            low, high = jnp.where(wrapped, high, low), jnp.where(wrapped, low, high)
        turned.append((low, high))
    for bit in range(3):
        mask = lane_bit(rows, bit)
        turned = [
            tuple(jnp.where(mask, turned[(i + (1 << bit)) % 16][h], turned[i][h]) for h in range(2))
            for i in range(16)
        ]
    turned = [(turned[i][0], turned[(i + 8) % 16][1]) for i in range(16)]
    return [turned[(-j) % 16] for j in range(16)]


def transpose_groups(values):
    rows = values[0].shape[0]
    turned = [roll(value, a) for a, value in enumerate(values)]
    for bit in range(3):
        mask = lane_bit(rows, bit)
        turned = [jnp.where(mask, turned[(i + (1 << bit)) % 8], turned[i]) for i in range(8)]
    return [roll(turned[(-b) % 8], -b) for b in range(8)]


def spread_half(value, half):
    rows = value.shape[0]
    turned = pltpu.roll(value, 4 * GROUP, 1)
    low = ~lane_bit(rows, 2)
    values = [jnp.where(low == (half == 0), value, turned)]
    for bit in (1, 0):
        low = ~lane_bit(rows, bit)
        spread = []
        for value in values:
            turned = pltpu.roll(value, GROUP << bit, 1)
            spread += [jnp.where(low, value, turned), jnp.where(low, turned, value)]
        values = spread
    return values


def sum_four(values):
    rows = values[0].shape[0]
    for bit in range(2):
        low = ~lane_bit(rows, bit)
        values = [
            jnp.where(low, a, b) + pltpu.roll(jnp.where(low, b, a), GROUP << bit, 1)
            for a, b in zip(values[::2], values[1::2])
        ]
    return values[0] + pltpu.roll(values[0], 4 * GROUP, 1)


def fold_phase(value, phase):
    group = lane_group(FOLD)
    out = None
    for i in range(8):
        piece = roll(value[i * FOLD : (i + 1) * FOLD], i - phase)
        out = piece if out is None else jnp.where(group == i, piece, out)
    return out


def unfold_phase(value, phase, i):
    return roll(value, phase - i)


def split(value):
    high = value.astype(BF16)
    return high, (value - high.astype(F32)).astype(BF16)


def dot(a, b):
    return jnp.dot(a, b, preferred_element_type=F32)


def dot3(table, value):
    return dot(table[0], value[0]) + (dot(table[0], value[1]) + dot(table[1], value[0]))


def wide(value):
    return jnp.concatenate([value, value], 1)


def images_of(maps_ref, at, real, imag):
    maps_real, maps_imag = maps_at(maps_ref, at)
    real, imag = wide(real), wide(imag)
    return maps_real * real - maps_imag * imag, maps_real * imag + maps_imag * real


def maps_at(maps_ref, at):
    return maps_ref[0, at], maps_ref[1, at]


def combine(maps_real, maps_imag, real, imag):
    out_real = maps_real * real + maps_imag * imag
    out_imag = maps_real * imag - maps_imag * real
    return out_real[:, :LANES] + out_real[:, LANES:], out_imag[:, :LANES] + out_imag[:, LANES:]


def row_pairs(step):
    half = SIZE // 2
    return [
        (slice(row, row + step), slice(half + row, half + row + step)) for row in range(0, half, step)
    ]


def store_split(ref, which, at, value):
    ref[which, at], ref[which + 1, at] = split(value)


def expand(vector_ref, maps_ref, pieces):
    half = pl.program_id(0)
    for near, far in row_pairs(16):
        values = [
            [spread_half(vector_ref[part, at], half) for part in range(2)] for at in (near, far)
        ]
        for t in range(4):
            real, imag = images_of(maps_ref, near, values[0][0][t], values[0][1][t])
            far_real, far_imag = images_of(maps_ref, far, values[1][0][t], values[1][1][t])
            store_split(pieces[t], 0, near, real + far_real)
            store_split(pieces[t], 0, far, imag - far_imag)
            store_split(pieces[t], 2, near, imag + far_imag)
            store_split(pieces[t], 2, far, far_real - real)


def reduce(maps_ref, backs, finish):
    for near, far in row_pairs(32):
        near_maps, far_maps = maps_at(maps_ref, near), maps_at(maps_ref, far)
        near_terms, far_terms = [], []
        for t in range(4):
            p_even, p_odd, q_even, q_odd = (
                backs[t][which, at] for which in range(2) for at in (near, far)
            )
            near_terms.append(combine(*near_maps, p_even - q_odd, q_even + p_odd))
            far_terms.append(combine(*far_maps, p_even + q_odd, q_even - p_odd))
        for at, terms in ((near, near_terms), (far, far_terms)):
            finish(at, *(sum_four([term[part] for term in terms]) for part in range(2)))


def products(tables_ref, pieces, backs):
    for t in range(4):
        high, low = tables_ref[t, 0], tables_ref[t, 1]
        for which in range(2):
            value_high, value_low = pieces[t][2 * which], pieces[t][2 * which + 1]
            backs[t][which] = dot(high, value_high) + dot(high, value_low) + dot(low, value_high)


def in_step(rows):
    return lane_bit(rows, 2) == (pl.program_id(0) == 1)


def split_three(value):
    high = value.astype(BF16)
    value = value - high.astype(F32)
    middle = value.astype(BF16)
    return high, middle, (value - middle.astype(F32)).astype(BF16)


def compact(weight_ref, turn_ref, in_ref, lines_ref, base, at_step):
    count = lines_ref.shape[2]
    weight = jnp.broadcast_to(weight_ref[...], (8, LINES))
    row = lax.broadcasted_iota(jnp.int32, (LINES, LINES), 0)
    col = lax.broadcasted_iota(jnp.int32, (LINES, LINES), 1)
    upto = jnp.where(row <= col, 1.0, 0.0).astype(BF16)
    number = dot(weight.astype(BF16), upto).astype(jnp.int32)
    number = jnp.broadcast_to(number[:1], (count, LINES))
    acquired = jnp.broadcast_to(weight_ref[...], (count, LINES)) > 0.5
    line = lax.broadcasted_iota(jnp.int32, (count, LINES), 0) + (base + 1)
    select = jnp.where((number == line) & acquired, 1.0, 0.0).astype(BF16)
    step = in_ref.shape[0]
    cos, sin = (jnp.concatenate([turn_ref[i]] * 2, 1) for i in range(2))
    for c in range(step):
        real, imag = in_ref[c, 0], in_ref[c, 1]
        for part, value in enumerate((real * cos - imag * sin, real * sin + imag * cos)):
            high, middle, low = split_three(value)
            lines_ref[part, at_step * step + c] = (
                dot(select, high) + dot(select, middle) + dot(select, low)
            )


def pack_lines(lines_ref, out_ref):
    count = lines_ref.shape[2]
    for part in range(2):
        for row in range(0, count, 8):
            at = slice(row, row + 8)
            to = slice(part * count + row, part * count + row + 8)
            halves = [
                (lines_ref[part, c, at, :LANES], lines_ref[part, c, at, LANES:]) for c in range(COILS)
            ]
            for j, (low, high) in enumerate(gather_coils(halves)):
                out_ref[j, to, :LANES] = low
                out_ref[j, to, LANES:] = high


def pack_image_kernel(maps_ref, frames_ref, aux_ref, dual_ref, out_ref):
    for part in range(2):
        to = slice(part * 8, (part + 1) * 8)
        halves = [(maps_ref[c, part, :, :LANES], maps_ref[c, part, :, LANES:]) for c in range(COILS)]
        for j, (low, high) in enumerate(gather_coils(halves)):
            out_ref[j, to, :LANES] = low
            out_ref[j, to, LANES:] = high
        for half in range(2):
            cols = slice(half * LANES, (half + 1) * LANES)
            frames = [frames_ref[part, t, :, cols] for t in range(PHASES)]
            splits = [aux_ref[part, t, :, cols] - dual_ref[part, t, :, cols] for t in range(PHASES)]
            lanes = slice(part * LANES, (part + 1) * LANES)
            for which, values in ((2, frames), (3, splits)):
                to_rows = slice(which * 8, (which + 1) * 8)
                for jj, value in enumerate(transpose_groups(values)):
                    out_ref[half * 8 + jj, to_rows, lanes] = value


def whole_spec(value):
    return pl.BlockSpec(value.shape, lambda *_: (0,) * len(value.shape))


def pack_image(coil_maps, *images):
    rows = pl.BlockSpec((2, PHASES, 8, SIZE), lambda i: (0, 0, i, 0))
    return pl.pallas_call(
        pack_image_kernel,
        grid=(ROWS // 8,),
        in_specs=[pl.BlockSpec((COILS, 2, 8, SIZE), lambda i: (0, 0, i, 0))] + [rows] * 3,
        out_specs=pl.BlockSpec((ROW_SHARDS, 32, SIZE), lambda i: (0, i, 0)),
        out_shape=jax.ShapeDtypeStruct((ROW_SHARDS, IMAGE, SIZE), F32),
        compiler_params=params(),
        name="pack_image",
    )(coil_maps, *images)


PACK_STEPS = 4


def pack_measured_kernel(base, weight_ref, turn_ref, in_ref, out_ref, zero_ref, lines_ref):
    step = pl.program_id(0)
    compact(weight_ref, turn_ref, in_ref, lines_ref, base, step)

    @pl.when(step == PACK_STEPS - 1)
    def _():
        pack_lines(lines_ref, out_ref)
        zero_ref[...] = jnp.zeros_like(zero_ref)


def pack_measured(weight, turn, measured, base, count):
    return pl.pallas_call(
        functools.partial(pack_measured_kernel, base),
        grid=(PACK_STEPS,),
        in_specs=[
            whole_spec(weight),
            whole_spec(turn),
            pl.BlockSpec((COILS // PACK_STEPS, 2, LINES, SIZE), lambda i: (i, 0, 0, 0)),
        ],
        out_specs=[pl.BlockSpec((ROW_SHARDS, 2 * count, SIZE), lambda i: (0, 0, 0)), VECTOR_SPEC],
        out_shape=[jax.ShapeDtypeStruct((ROW_SHARDS, 2 * count, SIZE), F32), VECTOR],
        scratch_shapes=[pltpu.VMEM((2, COILS, count, SIZE), F32)],
        compiler_params=params(),
        name=f"pack_measured_{base}",
    )(weight, turn, measured)


def line_table_kernel(index_ref, tables_ref, out_ref):
    row = lax.broadcasted_iota(jnp.int32, (SIZE, SIZE), 0)
    select = jnp.where(row == index_ref[0], 1.0, 0.0).astype(BF16)
    for i in range(2):
        out_ref[0, i] = dot(tables_ref[i], select).astype(BF16)


def line_tables(index, tables):
    return pl.pallas_call(
        line_table_kernel,
        grid=(PHASES,),
        in_specs=[pl.BlockSpec((1, 1, SIZE), lambda t: (t, 0, 0)), whole_spec(tables)],
        out_specs=pl.BlockSpec((1, 2, SIZE, SIZE), lambda t: (t, 0, 0, 0)),
        out_shape=jax.ShapeDtypeStruct((PHASES, 2, SIZE, SIZE), BF16),
        compiler_params=params(),
        name="line_tables",
    )(index, tables)


def reverse_eight(value):
    row = lax.broadcasted_iota(jnp.int32, value.shape, 0)
    value = pltpu.roll(value, 4, 0)
    for bit in (2, 1):
        value = jnp.where((row & bit) != 0, pltpu.roll(value, bit, 0), pltpu.roll(value, 8 - bit, 0))
    return value


def receive_kernel(image_ref, maps_ref, frames_ref, splits_ref, first_ref, last_ref):
    for part in range(2):
        lanes = slice(part * LANES, (part + 1) * LANES)
        for block in range(ROW_SHARDS):
            turned = block >= ROW_SHARDS // 2
            source = ROW_SHARDS + ROW_SHARDS // 2 - 1 - block if turned else block
            for half in range(2):
                row = block * ROWS + half * 8
                at = slice(row, row + 8)
                start = 32 * (1 - half if turned else half)
                maps, frames, splits = (
                    image_ref[source, start + which * 8 : start + (which + 1) * 8, columns]
                    for which, columns in ((part, slice(0, SIZE)), (2, lanes), (3, lanes))
                )
                if turned:
                    maps, frames, splits = (reverse_eight(v) for v in (maps, frames, splits))
                maps_ref[part, at] = maps
                frames_ref[part, at] = frames
                splits_ref[part, at] = splits
        first_ref[part] = fold_phase(frames_ref[part], 0)
        last_ref[part] = fold_phase(frames_ref[part] + splits_ref[part], PHASES - 1)


def receive(image):
    return pl.pallas_call(
        receive_kernel,
        grid=(1,),
        in_specs=[IMAGE_SPEC],
        out_specs=[MAPS_SPEC, VECTOR_SPEC, VECTOR_SPEC, FOLDED_SPEC, FOLDED_SPEC],
        out_shape=[jax.ShapeDtypeStruct((2, SIZE, SIZE), F32), VECTOR, VECTOR, FOLDED, FOLDED],
        compiler_params=params(),
        name="receive",
    )(image)


def gram_table_kernel(weight_ref, tables_ref, out_ref):
    weight = weight_ref[0]
    left = tuple((tables_ref[i].astype(F32) * weight).astype(BF16) for i in range(2))
    right = tables_ref[2], tables_ref[3]
    out_ref[0, 0], out_ref[0, 1] = split(dot3(left, right))


def gram_tables(weight, tables):
    return pl.pallas_call(
        gram_table_kernel,
        grid=(PHASES,),
        in_specs=[
            pl.BlockSpec((1, 1, SIZE), lambda t: (t, 0, 0)),
            pl.BlockSpec((4, SIZE, SIZE), lambda t: (0, 0, 0)),
        ],
        out_specs=pl.BlockSpec((1, 2, SIZE, SIZE), lambda t: (t, 0, 0, 0)),
        out_shape=jax.ShapeDtypeStruct((PHASES, 2, SIZE, SIZE), BF16),
        compiler_params=params(),
        name="gram_tables",
    )(weight, tables)


GRAM_SPEC = pl.BlockSpec((4, 2, SIZE, SIZE), lambda i, *_: (i, 0, 0, 0))
IMAGE_SPEC = pl.BlockSpec((ROW_SHARDS, IMAGE, SIZE), lambda *_: (0, 0, 0))
MAPS_SPEC = pl.BlockSpec((2, SIZE, SIZE), lambda *_: (0, 0, 0))
VECTOR_SPEC = pl.BlockSpec((2, SIZE, LANES), lambda *_: (0, 0, 0))
VECTOR = jax.ShapeDtypeStruct((2, SIZE, LANES), F32)
FOLDED_SPEC = pl.BlockSpec((2, FOLD, LANES), lambda *_: (0, 0, 0))
FOLDED = jax.ShapeDtypeStruct((2, FOLD, LANES), F32)
SUMS_SPEC = pl.BlockSpec((4, 8, LANES), lambda i: (0, 0, 0))
PIECES = [pltpu.VMEM((4, SIZE, SIZE), BF16)] * 4
BACKS = [pltpu.VMEM((2, SIZE, SIZE), F32)] * 4


def params():
    return pltpu.CompilerParams(vmem_limit_bytes=16 << 20)


def start_kernel(gram_ref, maps_ref, frames_ref, splits_ref, in_ref, out_ref, *scratch):
    pieces, backs = scratch[:4], scratch[4:]

    @pl.when(pl.program_id(0) == 0)
    def _():
        group = lane_group(FOLD)
        for row in range(0, SIZE, FOLD):
            at = slice(row, row + FOLD)
            for part in range(2):
                frames, splits = frames_ref[part, at], splits_ref[part, at]
                ahead = pltpu.roll(frames, LANES - GROUP, 1)
                behind = pltpu.roll(frames + splits, GROUP, 1)
                gap = splits - (jnp.where(group == PHASES - 1, 0.0, ahead) - frames)
                gap_behind = jnp.where(group == 0, 0.0, behind) - frames
                out_ref[part, at] = in_ref[part, at] + PENALTY * (gap_behind - gap) - DAMPING * frames

    expand(frames_ref, maps_ref, pieces)
    products(gram_ref, pieces, backs)

    def finish(at, real, imag):
        keep = in_step(at.stop - at.start)
        for part, value in enumerate((real, imag)):
            out_ref[part, at] -= jnp.where(keep, value, 0.0)

    reduce(maps_ref, backs, finish)


def start(grams, maps, frames, splits, so_far):
    return pl.pallas_call(
        start_kernel,
        grid=(2,),
        in_specs=[GRAM_SPEC] + [IN_VMEM] * 4,
        out_specs=VECTOR_SPEC,
        out_shape=VECTOR,
        scratch_shapes=PIECES + BACKS,
        compiler_params=params(),
        name="start",
    )(grams, maps, frames, splits, so_far)


def add_edges(before_ref, after_ref, in_ref, out_ref):
    group = lane_group(FOLD)
    for i in range(8):
        at = slice(i * FOLD, (i + 1) * FOLD)
        for part in range(2):
            before = unfold_phase(before_ref[part], 0, i)
            after = unfold_phase(after_ref[part], PHASES - 1, i)
            edge = jnp.where(group == 0, before, jnp.where(group == PHASES - 1, after, 0.0))
            out_ref[part, at] = in_ref[part, at] + PENALTY * edge


def adjoint_kernel(edges, window_ref, tables_ref, maps_ref, lines_ref, in_ref, *refs):
    edges_in, refs = refs[:edges], refs[edges:]
    out_ref, first_ref, last_ref = refs[:3]
    pieces, backs = refs[3:7], refs[7:]
    half = pl.program_id(0)
    count = lines_ref.shape[1] // 2

    @pl.when(half == 0)
    def _():
        if edges:
            add_edges(*edges_in, in_ref, out_ref)
        else:
            out_ref[...] = in_ref[...]

    for t in range(4):
        for block in range(ROW_SHARDS):
            at = slice(block * ROWS, (block + 1) * ROWS)
            start = window_ref[(half * 4 + t) * ROW_SHARDS + block]
            aligned = jnp.minimum(start // 8, (count - ROWS) // 8 - 1) * 8
            turn = lax.rem(ROWS + 8 - (start - aligned), ROWS + 8)
            for part in range(2):
                rows = pl.ds(pl.multiple_of(part * count + aligned, 8), ROWS + 8)
                rows = pltpu.roll(lines_ref[block, rows], turn, 0)
                store_split(pieces[t], 2 * part, at, rows[:ROWS])
    products(tables_ref, pieces, backs)

    def finish(at, real, imag):
        keep = in_step(at.stop - at.start)
        for which, value in enumerate((real, imag)):
            out_ref[which, at] += jnp.where(keep, value, 0.0)

    reduce(maps_ref, backs, finish)

    @pl.when(half == 1)
    def _():
        for which in range(2):
            value = out_ref[which]
            first_ref[which] = fold_phase(value, 0)
            last_ref[which] = fold_phase(value, PHASES - 1)


def adjoint(window, tables, maps, lines, so_far, *edges):
    return pl.pallas_call(
        functools.partial(adjoint_kernel, len(edges)),
        grid_spec=pltpu.PrefetchScalarGridSpec(
            num_scalar_prefetch=1,
            grid=(2,),
            in_specs=[GRAM_SPEC] + [IN_VMEM] * (3 + len(edges)),
            out_specs=[IN_VMEM] * 3,
            scratch_shapes=PIECES + BACKS,
        ),
        out_shape=[VECTOR, FOLDED, FOLDED],
        compiler_params=params(),
        name="adjoint",
    )(window, tables, maps, lines, so_far, *edges)


def gram_kernel(gram_ref, maps_ref, in_ref, out_ref, *scratch):
    pieces, backs = scratch[:4], scratch[4:]
    expand(in_ref, maps_ref, pieces)
    products(gram_ref, pieces, backs)

    def finish(at, real, imag):
        keep = in_step(at.stop - at.start)
        for part, value in enumerate((real, imag)):
            out_ref[part, at] = jnp.where(keep, value, out_ref[part, at])

    reduce(maps_ref, backs, finish)


def gram_apply(grams, maps, vector):
    return pl.pallas_call(
        gram_kernel,
        grid=(2,),
        in_specs=[GRAM_SPEC, IN_VMEM, IN_VMEM],
        out_specs=IN_VMEM,
        out_shape=VECTOR,
        scratch_shapes=PIECES + BACKS,
        compiler_params=params(),
        name="gram_apply",
    )(grams, maps, vector)


def fold(value):
    return jnp.sum(value.reshape(-1, 8, LANES), 0)


def normal_kernel(
    first_ref, gram_ref, before_ref, after_ref, image_ref, first_edge_ref, last_edge_ref, sums_ref
):
    rr = rw = ww = dd = 0.0
    group = lane_group(FOLD)
    for part in range(2):
        for i in range(8):
            at = slice(i * FOLD, (i + 1) * FOLD)
            value = first_ref[part, at]
            behind = jnp.where(
                group == 0, unfold_phase(before_ref[part], 0, i), pltpu.roll(value, GROUP, 1)
            )
            ahead = jnp.where(
                group == PHASES - 1,
                unfold_phase(after_ref[part], PHASES - 1, i),
                pltpu.roll(value, LANES - GROUP, 1),
            )
            image = (
                gram_ref[part, at]
                + PENALTY * ((value - behind) - (ahead - value))
                + DAMPING * value
            )
            image_ref[part, at] = image
            rr += fold(value * value)
            rw += fold(value * image)
            ww += fold(image * image)
            step = pltpu.roll(image, LANES - GROUP, 1) - image
            dd += fold(jnp.where(group == PHASES - 1, 0.0, step * step))
        whole = image_ref[part]
        first_edge_ref[part] = fold_phase(whole, 0)
        last_edge_ref[part] = fold_phase(whole, PHASES - 1)
    for i, value in enumerate((rr, rw, ww, dd)):
        sums_ref[i] = value


def normal(first, grams_first, before, after):
    return pl.pallas_call(
        normal_kernel,
        grid=(1,),
        in_specs=[IN_VMEM] * 4,
        out_specs=[IN_VMEM] * 4,
        out_shape=[
            VECTOR,
            FOLDED,
            FOLDED,
            jax.ShapeDtypeStruct((4, 8, LANES), F32),
        ],
        compiler_params=params(),
        name="normal",
    )(first, grams_first, before, after)


def curvature_kernel(gram_ref, maps_ref, in_ref, out_ref, *scratch):
    pieces, backs = scratch[:4], scratch[4:]

    @pl.when(pl.program_id(0) == 0)
    def _():
        out_ref[...] = jnp.zeros_like(out_ref)

    expand(in_ref, maps_ref, pieces)
    products(gram_ref, pieces, backs)
    total = 0.0
    for row in range(0, SIZE, 32):
        at = slice(row, row + 32)
        for t in range(4):
            p_high, p_low, q_high, q_low = (pieces[t][i, at].astype(F32) for i in range(4))
            both = (p_high + p_low) * backs[t][0, at] + (q_high + q_low) * backs[t][1, at]
            total += fold(both[:, :LANES] + both[:, LANES:])
    out_ref[...] += total


def curvature(grams, maps, vector):
    return pl.pallas_call(
        curvature_kernel,
        grid=(2,),
        in_specs=[GRAM_SPEC, IN_VMEM, IN_VMEM],
        out_specs=IN_VMEM,
        out_shape=jax.ShapeDtypeStruct((8, LANES), F32),
        scratch_shapes=PIECES + BACKS,
        compiler_params=params(),
        name="curvature",
    )(grams, maps, vector)


def lane_row(values):
    lane = lax.broadcasted_iota(jnp.int32, (1, LANES), 1)
    row = jnp.zeros((1, LANES), F32)
    for i, value in enumerate(values):
        row = jnp.where(lane == i, value, row)
    return row


def whole_sum(value):
    return jnp.sum(jnp.sum(value, 0, keepdims=True), 1, keepdims=True)


def share_kernel(sums_ref, curve_ref, last_ref, after_ref, out_ref):
    rr, rw, ww, dd = (whole_sum(sums_ref[i]) for i in range(4))
    edge = 0.0
    for part in range(2):
        step = after_ref[part] - last_ref[part]
        edge = edge + fold(step * step)
    curve = whole_sum(curve_ref[...]) + PENALTY * (dd + whole_sum(edge)) + DAMPING * ww
    row = lane_row((rr, rw, ww, curve))
    out_ref[...] = jnp.broadcast_to(row[None], out_ref.shape)


def share(sums, curve, last, after):
    return pl.pallas_call(
        share_kernel,
        grid=(1,),
        in_specs=[IN_VMEM] * 4,
        out_specs=pl.BlockSpec((ALL, 1, LANES), lambda i: (0, 0, 0)),
        out_shape=jax.ShapeDtypeStruct((ALL, 1, LANES), F32),
        compiler_params=params(),
        name="share",
    )(sums, curve, last, after)


def solve_kernel(
    shared_ref, frames_ref, residual_ref, product_ref, frames_after_ref, residual_after_ref, product_after_ref, out_ref
):
    row = jnp.sum(shared_ref[...], 0)
    rr, rw, ww, curve = (row[:, i : i + 1] for i in range(4))
    alpha = rr / rw
    fresh = rr - 2.0 * alpha * rw + alpha * alpha * ww
    beta = fresh / rr
    gamma = 1.0 + beta
    bend = gamma * gamma * rw - 2.0 * gamma * alpha * ww + alpha * alpha * curve
    second = fresh / bend
    by_first = alpha + second * gamma
    by_image = -second * alpha
    group = lane_group(8)
    for j in range(ROW_SHARDS):
        turned = j >= ROW_SHARDS // 2
        block = ROW_SHARDS + ROW_SHARDS // 2 - 1 - j if turned else j
        for row in range(0, ROWS, 8):
            at = slice(block * ROWS + row, block * ROWS + row + 8)
            piece, start = divmod(at.start, FOLD)
            folded = slice(start, start + 8)
            values = [
                frames_ref[part, at]
                + by_first * residual_ref[part, at]
                + by_image * product_ref[part, at]
                for part in range(2)
            ]
            edge = [
                roll(
                    frames_after_ref[part, folded]
                    + by_first * residual_after_ref[part, folded]
                    + by_image * product_after_ref[part, folded],
                    part - piece,
                )
                for part in range(2)
            ]
            values.append(jnp.where(group == 0, edge[0], edge[1]))
            to = slice(ROWS - 8 - row, ROWS - row) if turned else slice(row, row + 8)
            for which, value in enumerate(values):
                out_ref[j, which, to] = reverse_eight(value) if turned else value


def solve(shared, frames, residual, product, frames_after, residual_after, product_after):
    return pl.pallas_call(
        solve_kernel,
        grid=(1,),
        in_specs=[IN_VMEM] * 7,
        out_specs=pl.BlockSpec((ROW_SHARDS, 3, ROWS, LANES), lambda i: (0, 0, 0, 0)),
        out_shape=jax.ShapeDtypeStruct((ROW_SHARDS, 3, ROWS, LANES), F32),
        compiler_params=params(),
        name="solve",
    )(shared, frames, residual, product, frames_after, residual_after, product_after)


def finish_kernel(in_ref, aux_ref, dual_ref, x_ref, new_aux_ref, new_dual_ref, out_ref):
    primal = dual_sum = 0.0
    group = lane_group(8)
    for row in range(0, ROWS, 8):
        at = slice(row, row + 8)
        for half in range(2):
            cols = slice(half * LANES, (half + 1) * LANES)
            parts = []
            for part in range(2):
                blocks = [in_ref[half * 8 + jj, part, at] for jj in range(8)]
                values = transpose_groups(blocks)
                after = None
                for jj in range(8):
                    piece = roll(in_ref[half * 8 + jj, 2, at], jj - part)
                    after = piece if after is None else jnp.where(group == jj, piece, after)
                for t in range(PHASES):
                    x_ref[part, t, at, cols] = values[t]
                parts.append(values + [after])
            for t in range(PHASES):
                dual = [dual_ref[part, t, at, cols] for part in range(2)]
                shifted = [parts[part][t + 1] - parts[part][t] + dual[part] for part in range(2)]
                magnitude = jnp.sqrt(shifted[0] * shifted[0] + shifted[1] * shifted[1])
                factor = jnp.maximum(magnitude - THRESHOLD, 0.0) / jnp.maximum(magnitude, THRESHOLD)
                for part in range(2):
                    new_aux = shifted[part] * factor
                    new_dual = shifted[part] - new_aux
                    new_aux_ref[part, t, at, cols] = new_aux
                    new_dual_ref[part, t, at, cols] = new_dual
                    gap = new_dual - dual[part]
                    primal += gap * gap
                    gap = new_aux - aux_ref[part, t, at, cols]
                    dual_sum += gap * gap
    sums = lane_row((whole_sum(primal), whole_sum(dual_sum)))
    out_ref[...] = jnp.broadcast_to(sums[None], out_ref.shape)


def finish(back, auxiliary, scaled_dual):
    image = jax.ShapeDtypeStruct(auxiliary.shape, F32)
    return pl.pallas_call(
        finish_kernel,
        grid=(1,),
        in_specs=[whole_spec(value) for value in (back, auxiliary, scaled_dual)],
        out_specs=[whole_spec(image)] * 3 + [pl.BlockSpec((ALL, 1, LANES), lambda i: (0, 0, 0))],
        out_shape=[image, image, image, jax.ShapeDtypeStruct((ALL, 1, LANES), F32)],
        compiler_params=params(),
        name="finish",
    )(back, auxiliary, scaled_dual)


def tables():
    k = np.arange(SIZE)
    x = np.arange(SIZE // 2)
    unit = 2.0 * math.pi / (2 * SIZE)
    angle = (k[None, :] * (2 * x[:, None] - (SIZE - 1)) % (2 * SIZE)) * unit
    table = (np.concatenate([np.cos(angle), np.sin(angle)]) / math.sqrt(SIZE)).astype(np.float32)
    high = table.astype(BF16)
    low = (table - high.astype(np.float32)).astype(BF16)
    turn = (k * (SIZE - 1) % (2 * SIZE)) * unit
    turn = np.stack([np.cos(turn), np.sin(turn)]).astype(np.float32)
    return np.stack([high, low, high.T, low.T]), turn


def shift(value, steps):
    pairs = [(i, (i + steps) % PHASE_SHARDS) for i in range(PHASE_SHARDS)]
    return lax.ppermute(value, "phase", pairs)


def exchange(value, axes):
    return lax.all_to_all(value, axes, 0, 0, tiled=True)


def windows(number, acquired, base, count):
    before = number[:, :, :1] - acquired[:, :, :1] - base
    window = jnp.clip(before, 0, count - ROWS)
    place = lax.broadcasted_iota(jnp.int32, (1, 1, 1, ROWS), 3)
    match = (acquired > 0)[..., None] & (number[..., None] - (1 + base) == window[..., None] + place)
    match = match & (number[..., None] > base) & (number[..., None] <= base + count)
    k = lax.broadcasted_iota(jnp.int32, (1, ROW_SHARDS, ROWS, 1), 1) * ROWS
    k = k + lax.broadcasted_iota(jnp.int32, (1, ROW_SHARDS, ROWS, 1), 2)
    index = jnp.sum(jnp.where(match, k + 1, 0), 2) - 1
    return window.reshape(PHASES * ROW_SHARDS), index.reshape(PHASES, 1, SIZE)


def in_hbm(value):
    return pltpu.with_memory_space_constraint(value, pltpu.HBM)


def local(frames, auxiliary, scaled_dual, coil_maps, measured, sampling):
    table, turn = (jnp.asarray(value) for value in tables())
    lines = measured.reshape(COILS, 2, LINES, SIZE)
    own = lax.dynamic_slice_in_dim(sampling, lax.axis_index("row") * ROWS, ROWS, 1)
    own = own.astype(F32).reshape(1, LINES)

    packed = pack_image(*(in_hbm(v) for v in (coil_maps, frames, auxiliary, scaled_dual)))
    image = exchange(packed, "row")
    lines, own, turn, packed = lax.optimization_barrier((lines, own, turn, packed))
    turn = lax.dynamic_slice_in_dim(turn, lax.axis_index("row") * ROWS, ROWS, 1)
    turn = jnp.broadcast_to(turn[:, None, :, None], (2, PHASES, ROWS, LANES)).reshape(2, LINES, LANES)
    packed, residual = pack_measured(own, turn, lines, 0, MAIN)
    packed, late_sampling = lax.optimization_barrier((packed, sampling))
    acquired = late_sampling.reshape(PHASES, ROW_SHARDS, ROWS)
    by_phase = jnp.sum(acquired, 2, keepdims=True)
    number = jnp.cumsum(acquired, 2) + jnp.cumsum(by_phase, 0) - by_phase
    overflow = jnp.max(number) > MAIN

    def more(carry):
        window, index = windows(number, acquired, MAIN, EXTRA)
        maps = receive(image)[0]
        extra = exchange(pack_measured(own, turn, lines, MAIN, EXTRA)[0], "row")
        residual, _, _ = adjoint(window, line_tables(index, table), maps, extra, carry[1])
        return jnp.array(False), residual

    _, residual = lax.while_loop(lambda carry: carry[0], more, (overflow, residual))
    packed, residual = lax.optimization_barrier((packed, residual))
    received = exchange(packed, "row")

    grams = in_hbm(gram_tables(late_sampling.astype(F32)[:, None, :], table))
    maps, frames_cols, splits, first, last = receive(image)
    frames_before, frames_after = shift(last, 1), shift(first, -1)
    residual = in_hbm(start(grams, maps, frames_cols, splits, residual))

    window, index = windows(number, acquired, 0, MAIN)
    line_table = in_hbm(line_tables(index, table))
    residual, first, last = adjoint(
        window, line_table, maps, received, residual, frames_before, frames_after
    )

    residual_before = shift(last, 1)
    residual_after = shift(first, -1)
    grams_residual = gram_apply(grams, maps, residual)
    product, first, last, sums = normal(residual, grams_residual, residual_before, residual_after)
    product_after = shift(first, -1)
    shared = share(sums, curvature(grams, maps, product), last, product_after)
    shared = exchange(shared, ("phase", "row"))
    back = solve(shared, frames_cols, residual, product, frames_after, residual_after, product_after)
    new_frames, new_aux, new_dual, gaps = finish(exchange(back, "row"), auxiliary, scaled_dual)
    gaps = jnp.sum(exchange(gaps, ("phase", "row"))[:, 0, :2], 0)
    residual_norms = jnp.sqrt(gaps) * jnp.array([1.0, PENALTY], F32)
    return new_frames, new_aux, new_dual, residual_norms


def solution(mesh):
    image = P(None, "phase", "row", None)
    in_specs = (
        image,
        image,
        image,
        P(None, None, "row", None),
        P(None, None, "phase", "row", None),
        P("phase", None),
    )
    return jax.shard_map(
        local, mesh=mesh, in_specs=in_specs, out_specs=(image, image, image, P()), check_vma=False
    )
```

```python
import functools
import math

import jax
import jax.numpy as jnp
import numpy as np
from jax import lax
from jax.experimental import pallas as pl
from jax.experimental.pallas import tpu as pltpu
from jax.sharding import PartitionSpec as P

PENALTY = 0.5
DAMPING = 0.1
THRESHOLD = 1.0

COILS = 16
PHASES = 8
ROWS = 16
SIZE = 256
LANES = 128
GROUP = 16
FOLD = 32
LINES = PHASES * ROWS
MAIN = 88
EXTRA = LINES - MAIN
IMAGE = 4 * ROWS
ROW_SHARDS = 16
PHASE_SHARDS = 8
ALL = ROW_SHARDS * PHASE_SHARDS

IN_VMEM = pl.BlockSpec(memory_space=pltpu.VMEM)

F32 = jnp.float32
BF16 = jnp.bfloat16


def lane_bit(rows, bit):
    lane = lax.broadcasted_iota(jnp.int32, (rows, LANES), 1)
    return (lane & (GROUP << bit)) != 0


def lane_group(rows):
    return lax.broadcasted_iota(jnp.int32, (rows, LANES), 1) // GROUP


def roll(value, groups):
    groups %= 8
    if groups == 0:
        return value
    return pltpu.roll(value, groups * GROUP, 1)


def gather_coils(halves):
    rows = halves[0][0].shape[0]
    lane = lax.broadcasted_iota(jnp.int32, (rows, LANES), 1)
    turned = []
    for c, (low, high) in enumerate(halves):
        if c >= 8:
            low, high = high, low
        shift = c % 8
        if shift:
            low, high = roll(low, shift), roll(high, shift)
            wrapped = lane < shift * GROUP
            low, high = jnp.where(wrapped, high, low), jnp.where(wrapped, low, high)
        turned.append((low, high))
    for bit in range(3):
        mask = lane_bit(rows, bit)
        turned = [
            tuple(jnp.where(mask, turned[(i + (1 << bit)) % 16][h], turned[i][h]) for h in range(2))
            for i in range(16)
        ]
    turned = [(turned[i][0], turned[(i + 8) % 16][1]) for i in range(16)]
    return [turned[(-j) % 16] for j in range(16)]


def transpose_groups(values):
    rows = values[0].shape[0]
    turned = [roll(value, a) for a, value in enumerate(values)]
    for bit in range(3):
        mask = lane_bit(rows, bit)
        turned = [jnp.where(mask, turned[(i + (1 << bit)) % 8], turned[i]) for i in range(8)]
    return [roll(turned[(-b) % 8], -b) for b in range(8)]


def spread_half(value, half):
    rows = value.shape[0]
    turned = pltpu.roll(value, 4 * GROUP, 1)
    low = ~lane_bit(rows, 2)
    values = [jnp.where(low == (half == 0), value, turned)]
    for bit in (1, 0):
        low = ~lane_bit(rows, bit)
        spread = []
        for value in values:
            turned = pltpu.roll(value, GROUP << bit, 1)
            spread += [jnp.where(low, value, turned), jnp.where(low, turned, value)]
        values = spread
    return values


def sum_four(values):
    rows = values[0].shape[0]
    for bit in range(2):
        low = ~lane_bit(rows, bit)
        values = [
            jnp.where(low, a, b) + pltpu.roll(jnp.where(low, b, a), GROUP << bit, 1)
            for a, b in zip(values[::2], values[1::2])
        ]
    return values[0] + pltpu.roll(values[0], 4 * GROUP, 1)


def fold_phase(value, phase):
    group = lane_group(FOLD)
    out = None
    for i in range(8):
        piece = roll(value[i * FOLD : (i + 1) * FOLD], i - phase)
        out = piece if out is None else jnp.where(group == i, piece, out)
    return out


def unfold_phase(value, phase, i):
    return roll(value, phase - i)


def split(value):
    high = value.astype(BF16)
    return high, (value - high.astype(F32)).astype(BF16)


def dot(a, b):
    return jnp.dot(a, b, preferred_element_type=F32)


def dot3(table, value):
    return dot(table[0], value[0]) + (dot(table[0], value[1]) + dot(table[1], value[0]))


def wide(value):
    return jnp.concatenate([value, value], 1)


def images_of(maps_ref, at, real, imag):
    maps_real, maps_imag = maps_at(maps_ref, at)
    real, imag = wide(real), wide(imag)
    return maps_real * real - maps_imag * imag, maps_real * imag + maps_imag * real


def maps_at(maps_ref, at):
    return maps_ref[0, at], maps_ref[1, at]


def combine(maps_real, maps_imag, real, imag):
    out_real = maps_real * real + maps_imag * imag
    out_imag = maps_real * imag - maps_imag * real
    return out_real[:, :LANES] + out_real[:, LANES:], out_imag[:, :LANES] + out_imag[:, LANES:]


def row_pairs(step):
    half = SIZE // 2
    return [
        (slice(row, row + step), slice(half + row, half + row + step)) for row in range(0, half, step)
    ]


def store_split(ref, which, at, value):
    ref[which, at], ref[which + 1, at] = split(value)


def expand(vector_ref, maps_ref, pieces):
    half = pl.program_id(0)
    for near, far in row_pairs(32):
        values = [
            [spread_half(vector_ref[part, at], half) for part in range(2)] for at in (near, far)
        ]
        for t in range(4):
            real, imag = images_of(maps_ref, near, values[0][0][t], values[0][1][t])
            far_real, far_imag = images_of(maps_ref, far, values[1][0][t], values[1][1][t])
            store_split(pieces[t], 0, near, real + far_real)
            store_split(pieces[t], 0, far, imag - far_imag)
            store_split(pieces[t], 2, near, imag + far_imag)
            store_split(pieces[t], 2, far, far_real - real)


def reduce(maps_ref, backs, finish):
    for near, far in row_pairs(32):
        near_maps, far_maps = maps_at(maps_ref, near), maps_at(maps_ref, far)
        near_terms, far_terms = [], []
        for t in range(4):
            p_even, p_odd, q_even, q_odd = (
                backs[t][which, at] for which in range(2) for at in (near, far)
            )
            near_terms.append(combine(*near_maps, p_even - q_odd, q_even + p_odd))
            far_terms.append(combine(*far_maps, p_even + q_odd, q_even - p_odd))
        for at, terms in ((near, near_terms), (far, far_terms)):
            finish(at, *(sum_four([term[part] for term in terms]) for part in range(2)))


def products(tables_ref, pieces, backs):
    for t in range(4):
        high, low = tables_ref[t, 0], tables_ref[t, 1]
        for which in range(2):
            value_high, value_low = pieces[t][2 * which], pieces[t][2 * which + 1]
            backs[t][which] = dot(high, value_high) + dot(high, value_low) + dot(low, value_high)


def in_step(rows):
    return lane_bit(rows, 2) == (pl.program_id(0) == 1)


def split_three(value):
    high = value.astype(BF16)
    value = value - high.astype(F32)
    middle = value.astype(BF16)
    return high, middle, (value - middle.astype(F32)).astype(BF16)


def compact(weight_ref, turn_ref, in_ref, lines_ref, base, at_step):
    count = lines_ref.shape[2]
    weight = jnp.broadcast_to(weight_ref[...], (8, LINES))
    row = lax.broadcasted_iota(jnp.int32, (LINES, LINES), 0)
    col = lax.broadcasted_iota(jnp.int32, (LINES, LINES), 1)
    upto = jnp.where(row <= col, 1.0, 0.0).astype(BF16)
    number = dot(weight.astype(BF16), upto).astype(jnp.int32)
    number = jnp.broadcast_to(number[:1], (count, LINES))
    acquired = jnp.broadcast_to(weight_ref[...], (count, LINES)) > 0.5
    line = lax.broadcasted_iota(jnp.int32, (count, LINES), 0) + (base + 1)
    select = jnp.where((number == line) & acquired, 1.0, 0.0).astype(BF16)
    step = in_ref.shape[0]
    cos, sin = (jnp.concatenate([turn_ref[i]] * 2, 1) for i in range(2))
    for c in range(step):
        real, imag = in_ref[c, 0], in_ref[c, 1]
        for part, value in enumerate((real * cos - imag * sin, real * sin + imag * cos)):
            high, middle, low = split_three(value)
            lines_ref[part, at_step * step + c] = (
                dot(select, high) + dot(select, middle) + dot(select, low)
            )


def pack_lines(lines_ref, out_ref):
    count = lines_ref.shape[2]
    for part in range(2):
        for row in range(0, count, 8):
            at = slice(row, row + 8)
            to = slice(part * count + row, part * count + row + 8)
            halves = [
                (lines_ref[part, c, at, :LANES], lines_ref[part, c, at, LANES:]) for c in range(COILS)
            ]
            for j, (low, high) in enumerate(gather_coils(halves)):
                out_ref[j, to, :LANES] = low
                out_ref[j, to, LANES:] = high


def pack_image_kernel(maps_ref, frames_ref, aux_ref, dual_ref, out_ref):
    for part in range(2):
        to = slice(part * 8, (part + 1) * 8)
        halves = [(maps_ref[c, part, :, :LANES], maps_ref[c, part, :, LANES:]) for c in range(COILS)]
        for j, (low, high) in enumerate(gather_coils(halves)):
            out_ref[j, to, :LANES] = low
            out_ref[j, to, LANES:] = high
        for half in range(2):
            cols = slice(half * LANES, (half + 1) * LANES)
            frames = [frames_ref[part, t, :, cols] for t in range(PHASES)]
            splits = [aux_ref[part, t, :, cols] - dual_ref[part, t, :, cols] for t in range(PHASES)]
            lanes = slice(part * LANES, (part + 1) * LANES)
            for which, values in ((2, frames), (3, splits)):
                to_rows = slice(which * 8, (which + 1) * 8)
                for jj, value in enumerate(transpose_groups(values)):
                    out_ref[half * 8 + jj, to_rows, lanes] = value


def whole_spec(value):
    return pl.BlockSpec(value.shape, lambda *_: (0,) * len(value.shape))


def pack_image(coil_maps, *images):
    rows = pl.BlockSpec((2, PHASES, 8, SIZE), lambda i: (0, 0, i, 0))
    return pl.pallas_call(
        pack_image_kernel,
        grid=(ROWS // 8,),
        in_specs=[pl.BlockSpec((COILS, 2, 8, SIZE), lambda i: (0, 0, i, 0))] + [rows] * 3,
        out_specs=pl.BlockSpec((ROW_SHARDS, 32, SIZE), lambda i: (0, i, 0)),
        out_shape=jax.ShapeDtypeStruct((ROW_SHARDS, IMAGE, SIZE), F32),
        compiler_params=params(),
        name="pack_image",
    )(coil_maps, *images)


PACK_STEPS = 4


def pack_measured_kernel(base, weight_ref, turn_ref, in_ref, out_ref, zero_ref, lines_ref):
    step = pl.program_id(0)
    compact(weight_ref, turn_ref, in_ref, lines_ref, base, step)

    @pl.when(step == PACK_STEPS - 1)
    def _():
        pack_lines(lines_ref, out_ref)
        zero_ref[...] = jnp.zeros_like(zero_ref)


def pack_measured(weight, turn, measured, base, count):
    return pl.pallas_call(
        functools.partial(pack_measured_kernel, base),
        grid=(PACK_STEPS,),
        in_specs=[
            whole_spec(weight),
            whole_spec(turn),
            pl.BlockSpec((COILS // PACK_STEPS, 2, LINES, SIZE), lambda i: (i, 0, 0, 0)),
        ],
        out_specs=[pl.BlockSpec((ROW_SHARDS, 2 * count, SIZE), lambda i: (0, 0, 0)), VECTOR_SPEC],
        out_shape=[jax.ShapeDtypeStruct((ROW_SHARDS, 2 * count, SIZE), F32), VECTOR],
        scratch_shapes=[pltpu.VMEM((2, COILS, count, SIZE), F32)],
        compiler_params=params(),
        name=f"pack_measured_{base}",
    )(weight, turn, measured)


def line_table_kernel(index_ref, tables_ref, out_ref):
    row = lax.broadcasted_iota(jnp.int32, (SIZE, SIZE), 0)
    select = jnp.where(row == index_ref[0], 1.0, 0.0).astype(BF16)
    for i in range(2):
        out_ref[0, i] = dot(tables_ref[i], select).astype(BF16)


def line_tables(index, tables):
    return pl.pallas_call(
        line_table_kernel,
        grid=(PHASES,),
        in_specs=[pl.BlockSpec((1, 1, SIZE), lambda t: (t, 0, 0)), whole_spec(tables)],
        out_specs=pl.BlockSpec((1, 2, SIZE, SIZE), lambda t: (t, 0, 0, 0)),
        out_shape=jax.ShapeDtypeStruct((PHASES, 2, SIZE, SIZE), BF16),
        compiler_params=params(),
        name="line_tables",
    )(index, tables)


def reverse_eight(value):
    row = lax.broadcasted_iota(jnp.int32, value.shape, 0)
    value = pltpu.roll(value, 4, 0)
    for bit in (2, 1):
        value = jnp.where((row & bit) != 0, pltpu.roll(value, bit, 0), pltpu.roll(value, 8 - bit, 0))
    return value


def receive_kernel(image_ref, maps_ref, frames_ref, splits_ref, first_ref, last_ref):
    for part in range(2):
        lanes = slice(part * LANES, (part + 1) * LANES)
        for block in range(ROW_SHARDS):
            turned = block >= ROW_SHARDS // 2
            source = ROW_SHARDS + ROW_SHARDS // 2 - 1 - block if turned else block
            for half in range(2):
                row = block * ROWS + half * 8
                at = slice(row, row + 8)
                start = 32 * (1 - half if turned else half)
                maps, frames, splits = (
                    image_ref[source, start + which * 8 : start + (which + 1) * 8, columns]
                    for which, columns in ((part, slice(0, SIZE)), (2, lanes), (3, lanes))
                )
                if turned:
                    maps, frames, splits = (reverse_eight(v) for v in (maps, frames, splits))
                maps_ref[part, at] = maps
                frames_ref[part, at] = frames
                splits_ref[part, at] = splits
        first_ref[part] = fold_phase(frames_ref[part], 0)
        last_ref[part] = fold_phase(frames_ref[part] + splits_ref[part], PHASES - 1)


def receive(image):
    return pl.pallas_call(
        receive_kernel,
        grid=(1,),
        in_specs=[IMAGE_SPEC],
        out_specs=[MAPS_SPEC, VECTOR_SPEC, VECTOR_SPEC, FOLDED_SPEC, FOLDED_SPEC],
        out_shape=[jax.ShapeDtypeStruct((2, SIZE, SIZE), F32), VECTOR, VECTOR, FOLDED, FOLDED],
        compiler_params=params(),
        name="receive",
    )(image)


def gram_table_kernel(weight_ref, tables_ref, out_ref):
    weight = weight_ref[0]
    left = tuple((tables_ref[i].astype(F32) * weight).astype(BF16) for i in range(2))
    right = tables_ref[2], tables_ref[3]
    out_ref[0, 0], out_ref[0, 1] = split(dot3(left, right))


def gram_tables(weight, tables):
    return pl.pallas_call(
        gram_table_kernel,
        grid=(PHASES,),
        in_specs=[
            pl.BlockSpec((1, 1, SIZE), lambda t: (t, 0, 0)),
            pl.BlockSpec((4, SIZE, SIZE), lambda t: (0, 0, 0)),
        ],
        out_specs=pl.BlockSpec((1, 2, SIZE, SIZE), lambda t: (t, 0, 0, 0)),
        out_shape=jax.ShapeDtypeStruct((PHASES, 2, SIZE, SIZE), BF16),
        compiler_params=params(),
        name="gram_tables",
    )(weight, tables)


GRAM_SPEC = pl.BlockSpec((4, 2, SIZE, SIZE), lambda i, *_: (i, 0, 0, 0))
IMAGE_SPEC = pl.BlockSpec((ROW_SHARDS, IMAGE, SIZE), lambda *_: (0, 0, 0))
MAPS_SPEC = pl.BlockSpec((2, SIZE, SIZE), lambda *_: (0, 0, 0))
VECTOR_SPEC = pl.BlockSpec((2, SIZE, LANES), lambda *_: (0, 0, 0))
VECTOR = jax.ShapeDtypeStruct((2, SIZE, LANES), F32)
FOLDED_SPEC = pl.BlockSpec((2, FOLD, LANES), lambda *_: (0, 0, 0))
FOLDED = jax.ShapeDtypeStruct((2, FOLD, LANES), F32)
SUMS_SPEC = pl.BlockSpec((4, 8, LANES), lambda i: (0, 0, 0))
PIECES = [pltpu.VMEM((4, SIZE, SIZE), BF16)] * 4
BACKS = [pltpu.VMEM((2, SIZE, SIZE), F32)] * 4


def params():
    return pltpu.CompilerParams(vmem_limit_bytes=16 << 20)


def start_kernel(gram_ref, maps_ref, frames_ref, splits_ref, in_ref, out_ref, *scratch):
    pieces, backs = scratch[:4], scratch[4:]

    @pl.when(pl.program_id(0) == 0)
    def _():
        group = lane_group(FOLD)
        for row in range(0, SIZE, FOLD):
            at = slice(row, row + FOLD)
            for part in range(2):
                frames, splits = frames_ref[part, at], splits_ref[part, at]
                ahead = pltpu.roll(frames, LANES - GROUP, 1)
                behind = pltpu.roll(frames + splits, GROUP, 1)
                gap = splits - (jnp.where(group == PHASES - 1, 0.0, ahead) - frames)
                gap_behind = jnp.where(group == 0, 0.0, behind) - frames
                out_ref[part, at] = in_ref[part, at] + PENALTY * (gap_behind - gap) - DAMPING * frames

    expand(frames_ref, maps_ref, pieces)
    products(gram_ref, pieces, backs)

    def finish(at, real, imag):
        keep = in_step(at.stop - at.start)
        for part, value in enumerate((real, imag)):
            out_ref[part, at] -= jnp.where(keep, value, 0.0)

    reduce(maps_ref, backs, finish)


def start(grams, maps, frames, splits, so_far):
    return pl.pallas_call(
        start_kernel,
        grid=(2,),
        in_specs=[GRAM_SPEC] + [IN_VMEM] * 4,
        out_specs=VECTOR_SPEC,
        out_shape=VECTOR,
        scratch_shapes=PIECES + BACKS,
        compiler_params=params(),
        name="start",
    )(grams, maps, frames, splits, so_far)


def add_edges(before_ref, after_ref, in_ref, out_ref):
    group = lane_group(FOLD)
    for i in range(8):
        at = slice(i * FOLD, (i + 1) * FOLD)
        for part in range(2):
            before = unfold_phase(before_ref[part], 0, i)
            after = unfold_phase(after_ref[part], PHASES - 1, i)
            edge = jnp.where(group == 0, before, jnp.where(group == PHASES - 1, after, 0.0))
            out_ref[part, at] = in_ref[part, at] + PENALTY * edge


def adjoint_kernel(edges, window_ref, tables_ref, maps_ref, lines_ref, in_ref, *refs):
    edges_in, refs = refs[:edges], refs[edges:]
    out_ref, first_ref, last_ref = refs[:3]
    pieces, backs = refs[3:7], refs[7:]
    half = pl.program_id(0)
    count = lines_ref.shape[1] // 2

    @pl.when(half == 0)
    def _():
        if edges:
            add_edges(*edges_in, in_ref, out_ref)
        else:
            out_ref[...] = in_ref[...]

    for t in range(4):
        for block in range(ROW_SHARDS):
            at = slice(block * ROWS, (block + 1) * ROWS)
            start = window_ref[(half * 4 + t) * ROW_SHARDS + block]
            aligned = jnp.minimum(start // 8, (count - ROWS) // 8 - 1) * 8
            turn = lax.rem(ROWS + 8 - (start - aligned), ROWS + 8)
            for part in range(2):
                rows = pl.ds(pl.multiple_of(part * count + aligned, 8), ROWS + 8)
                rows = pltpu.roll(lines_ref[block, rows], turn, 0)
                store_split(pieces[t], 2 * part, at, rows[:ROWS])
    products(tables_ref, pieces, backs)

    def finish(at, real, imag):
        keep = in_step(at.stop - at.start)
        for which, value in enumerate((real, imag)):
            out_ref[which, at] += jnp.where(keep, value, 0.0)

    reduce(maps_ref, backs, finish)

    @pl.when(half == 1)
    def _():
        for which in range(2):
            value = out_ref[which]
            first_ref[which] = fold_phase(value, 0)
            last_ref[which] = fold_phase(value, PHASES - 1)


def adjoint(window, tables, maps, lines, so_far, *edges):
    return pl.pallas_call(
        functools.partial(adjoint_kernel, len(edges)),
        grid_spec=pltpu.PrefetchScalarGridSpec(
            num_scalar_prefetch=1,
            grid=(2,),
            in_specs=[GRAM_SPEC] + [IN_VMEM] * (3 + len(edges)),
            out_specs=[IN_VMEM] * 3,
            scratch_shapes=PIECES + BACKS,
        ),
        out_shape=[VECTOR, FOLDED, FOLDED],
        compiler_params=params(),
        name="adjoint",
    )(window, tables, maps, lines, so_far, *edges)


def gram_kernel(gram_ref, maps_ref, in_ref, out_ref, *scratch):
    pieces, backs = scratch[:4], scratch[4:]
    expand(in_ref, maps_ref, pieces)
    products(gram_ref, pieces, backs)

    def finish(at, real, imag):
        keep = in_step(at.stop - at.start)
        for part, value in enumerate((real, imag)):
            out_ref[part, at] = jnp.where(keep, value, out_ref[part, at])

    reduce(maps_ref, backs, finish)


def gram_apply(grams, maps, vector):
    return pl.pallas_call(
        gram_kernel,
        grid=(2,),
        in_specs=[GRAM_SPEC, IN_VMEM, IN_VMEM],
        out_specs=IN_VMEM,
        out_shape=VECTOR,
        scratch_shapes=PIECES + BACKS,
        compiler_params=params(),
        name="gram_apply",
    )(grams, maps, vector)


def fold(value):
    return jnp.sum(value.reshape(-1, 8, LANES), 0)


def normal_kernel(
    first_ref, gram_ref, before_ref, after_ref, image_ref, first_edge_ref, last_edge_ref, sums_ref
):
    rr = rw = ww = dd = 0.0
    group = lane_group(FOLD)
    for part in range(2):
        for i in range(8):
            at = slice(i * FOLD, (i + 1) * FOLD)
            value = first_ref[part, at]
            behind = jnp.where(
                group == 0, unfold_phase(before_ref[part], 0, i), pltpu.roll(value, GROUP, 1)
            )
            ahead = jnp.where(
                group == PHASES - 1,
                unfold_phase(after_ref[part], PHASES - 1, i),
                pltpu.roll(value, LANES - GROUP, 1),
            )
            image = (
                gram_ref[part, at]
                + PENALTY * ((value - behind) - (ahead - value))
                + DAMPING * value
            )
            image_ref[part, at] = image
            rr += fold(value * value)
            rw += fold(value * image)
            ww += fold(image * image)
            step = pltpu.roll(image, LANES - GROUP, 1) - image
            dd += fold(jnp.where(group == PHASES - 1, 0.0, step * step))
        whole = image_ref[part]
        first_edge_ref[part] = fold_phase(whole, 0)
        last_edge_ref[part] = fold_phase(whole, PHASES - 1)
    for i, value in enumerate((rr, rw, ww, dd)):
        sums_ref[i] = value


def normal(first, grams_first, before, after):
    return pl.pallas_call(
        normal_kernel,
        grid=(1,),
        in_specs=[IN_VMEM] * 4,
        out_specs=[IN_VMEM] * 4,
        out_shape=[
            VECTOR,
            FOLDED,
            FOLDED,
            jax.ShapeDtypeStruct((4, 8, LANES), F32),
        ],
        compiler_params=params(),
        name="normal",
    )(first, grams_first, before, after)


def curvature_kernel(gram_ref, maps_ref, in_ref, out_ref, *scratch):
    pieces, backs = scratch[:4], scratch[4:]

    @pl.when(pl.program_id(0) == 0)
    def _():
        out_ref[...] = jnp.zeros_like(out_ref)

    expand(in_ref, maps_ref, pieces)
    products(gram_ref, pieces, backs)
    total = 0.0
    for row in range(0, SIZE, 32):
        at = slice(row, row + 32)
        for t in range(4):
            p_high, p_low, q_high, q_low = (pieces[t][i, at].astype(F32) for i in range(4))
            both = (p_high + p_low) * backs[t][0, at] + (q_high + q_low) * backs[t][1, at]
            total += fold(both[:, :LANES] + both[:, LANES:])
    out_ref[...] += total


def curvature(grams, maps, vector):
    return pl.pallas_call(
        curvature_kernel,
        grid=(2,),
        in_specs=[GRAM_SPEC, IN_VMEM, IN_VMEM],
        out_specs=IN_VMEM,
        out_shape=jax.ShapeDtypeStruct((8, LANES), F32),
        scratch_shapes=PIECES + BACKS,
        compiler_params=params(),
        name="curvature",
    )(grams, maps, vector)


def lane_row(values):
    lane = lax.broadcasted_iota(jnp.int32, (1, LANES), 1)
    row = jnp.zeros((1, LANES), F32)
    for i, value in enumerate(values):
        row = jnp.where(lane == i, value, row)
    return row


def whole_sum(value):
    return jnp.sum(jnp.sum(value, 0, keepdims=True), 1, keepdims=True)


def share_kernel(sums_ref, curve_ref, last_ref, after_ref, out_ref):
    rr, rw, ww, dd = (whole_sum(sums_ref[i]) for i in range(4))
    edge = 0.0
    for part in range(2):
        step = after_ref[part] - last_ref[part]
        edge = edge + fold(step * step)
    curve = whole_sum(curve_ref[...]) + PENALTY * (dd + whole_sum(edge)) + DAMPING * ww
    row = lane_row((rr, rw, ww, curve))
    out_ref[...] = jnp.broadcast_to(row[None], out_ref.shape)


def share(sums, curve, last, after):
    return pl.pallas_call(
        share_kernel,
        grid=(1,),
        in_specs=[IN_VMEM] * 4,
        out_specs=pl.BlockSpec((ALL, 1, LANES), lambda i: (0, 0, 0)),
        out_shape=jax.ShapeDtypeStruct((ALL, 1, LANES), F32),
        compiler_params=params(),
        name="share",
    )(sums, curve, last, after)


def solve_kernel(
    shared_ref, frames_ref, residual_ref, product_ref, frames_after_ref, residual_after_ref, product_after_ref, out_ref
):
    row = jnp.sum(shared_ref[...], 0)
    rr, rw, ww, curve = (row[:, i : i + 1] for i in range(4))
    alpha = rr / rw
    fresh = rr - 2.0 * alpha * rw + alpha * alpha * ww
    beta = fresh / rr
    gamma = 1.0 + beta
    bend = gamma * gamma * rw - 2.0 * gamma * alpha * ww + alpha * alpha * curve
    second = fresh / bend
    by_first = alpha + second * gamma
    by_image = -second * alpha
    group = lane_group(8)
    for j in range(ROW_SHARDS):
        turned = j >= ROW_SHARDS // 2
        block = ROW_SHARDS + ROW_SHARDS // 2 - 1 - j if turned else j
        edges = jnp.zeros((8, LANES), F32)
        for row in range(0, ROWS, 8):
            at = slice(block * ROWS + row, block * ROWS + row + 8)
            piece, start = divmod(at.start, FOLD)
            folded = slice(start, start + 8)
            to = ROWS - 8 - row if turned else row
            for part in range(2):
                value = (
                    frames_ref[part, at]
                    + by_first * residual_ref[part, at]
                    + by_image * product_ref[part, at]
                )
                place = 2 * part + to // 8
                edge = roll(
                    frames_after_ref[part, folded]
                    + by_first * residual_after_ref[part, folded]
                    + by_image * product_after_ref[part, folded],
                    place - piece,
                )
                if turned:
                    value, edge = reverse_eight(value), reverse_eight(edge)
                out_ref[j, part * ROWS + to : part * ROWS + to + 8] = value
                edges = jnp.where(group == place, edge, edges)
        out_ref[j, 2 * ROWS : 2 * ROWS + 8] = edges


def solve(shared, frames, residual, product, frames_after, residual_after, product_after):
    return pl.pallas_call(
        solve_kernel,
        grid=(1,),
        in_specs=[IN_VMEM] * 7,
        out_specs=pl.BlockSpec((ROW_SHARDS, 2 * ROWS + 8, LANES), lambda i: (0, 0, 0)),
        out_shape=jax.ShapeDtypeStruct((ROW_SHARDS, 2 * ROWS + 8, LANES), F32),
        compiler_params=params(),
        name="solve",
    )(shared, frames, residual, product, frames_after, residual_after, product_after)


def finish_kernel(in_ref, aux_ref, dual_ref, x_ref, new_aux_ref, new_dual_ref, out_ref):
    primal = dual_sum = 0.0
    group = lane_group(8)
    for row in range(0, ROWS, 8):
        at = slice(row, row + 8)
        for half in range(2):
            cols = slice(half * LANES, (half + 1) * LANES)
            parts = []
            for part in range(2):
                rows = slice(part * ROWS + row, part * ROWS + row + 8)
                blocks = [in_ref[half * 8 + jj, rows] for jj in range(8)]
                values = transpose_groups(blocks)
                after = None
                for jj in range(8):
                    place = 2 * part + row // 8
                    piece = roll(in_ref[half * 8 + jj, 2 * ROWS : 2 * ROWS + 8], jj - place)
                    after = piece if after is None else jnp.where(group == jj, piece, after)
                for t in range(PHASES):
                    x_ref[part, t, at, cols] = values[t]
                parts.append(values + [after])
            for t in range(PHASES):
                dual = [dual_ref[part, t, at, cols] for part in range(2)]
                shifted = [parts[part][t + 1] - parts[part][t] + dual[part] for part in range(2)]
                magnitude = jnp.sqrt(shifted[0] * shifted[0] + shifted[1] * shifted[1])
                factor = jnp.maximum(magnitude - THRESHOLD, 0.0) / jnp.maximum(magnitude, THRESHOLD)
                for part in range(2):
                    new_aux = shifted[part] * factor
                    new_dual = shifted[part] - new_aux
                    new_aux_ref[part, t, at, cols] = new_aux
                    new_dual_ref[part, t, at, cols] = new_dual
                    gap = new_dual - dual[part]
                    primal += gap * gap
                    gap = new_aux - aux_ref[part, t, at, cols]
                    dual_sum += gap * gap
    sums = lane_row((whole_sum(primal), whole_sum(dual_sum)))
    out_ref[...] = jnp.broadcast_to(sums[None], out_ref.shape)


def finish(back, auxiliary, scaled_dual):
    image = jax.ShapeDtypeStruct(auxiliary.shape, F32)
    return pl.pallas_call(
        finish_kernel,
        grid=(1,),
        in_specs=[whole_spec(value) for value in (back, auxiliary, scaled_dual)],
        out_specs=[whole_spec(image)] * 3 + [pl.BlockSpec((ALL, 1, LANES), lambda i: (0, 0, 0))],
        out_shape=[image, image, image, jax.ShapeDtypeStruct((ALL, 1, LANES), F32)],
        compiler_params=params(),
        name="finish",
    )(back, auxiliary, scaled_dual)


def tables():
    k = np.arange(SIZE)
    x = np.arange(SIZE // 2)
    unit = 2.0 * math.pi / (2 * SIZE)
    angle = (k[None, :] * (2 * x[:, None] - (SIZE - 1)) % (2 * SIZE)) * unit
    table = (np.concatenate([np.cos(angle), np.sin(angle)]) / math.sqrt(SIZE)).astype(np.float32)
    high = table.astype(BF16)
    low = (table - high.astype(np.float32)).astype(BF16)
    turn = (k * (SIZE - 1) % (2 * SIZE)) * unit
    turn = np.stack([np.cos(turn), np.sin(turn)]).astype(np.float32)
    return np.stack([high, low, high.T, low.T]), turn


def shift(value, steps):
    pairs = [(i, (i + steps) % PHASE_SHARDS) for i in range(PHASE_SHARDS)]
    return lax.ppermute(value, "phase", pairs)


def exchange(value, axes):
    return lax.all_to_all(value, axes, 0, 0, tiled=True)


def windows(number, acquired, base, count):
    before = number[:, :, :1] - acquired[:, :, :1] - base
    window = jnp.clip(before, 0, count - ROWS)
    place = lax.broadcasted_iota(jnp.int32, (1, 1, 1, ROWS), 3)
    match = (acquired > 0)[..., None] & (number[..., None] - (1 + base) == window[..., None] + place)
    match = match & (number[..., None] > base) & (number[..., None] <= base + count)
    k = lax.broadcasted_iota(jnp.int32, (1, ROW_SHARDS, ROWS, 1), 1) * ROWS
    k = k + lax.broadcasted_iota(jnp.int32, (1, ROW_SHARDS, ROWS, 1), 2)
    index = jnp.sum(jnp.where(match, k + 1, 0), 2) - 1
    return window.reshape(PHASES * ROW_SHARDS), index.reshape(PHASES, 1, SIZE)


def in_hbm(value):
    return pltpu.with_memory_space_constraint(value, pltpu.HBM)


def local(frames, auxiliary, scaled_dual, coil_maps, measured, sampling):
    table, turn = (jnp.asarray(value) for value in tables())
    lines = measured.reshape(COILS, 2, LINES, SIZE)
    own = lax.dynamic_slice_in_dim(sampling, lax.axis_index("row") * ROWS, ROWS, 1)
    own = own.astype(F32).reshape(1, LINES)

    packed = pack_image(*(in_hbm(v) for v in (coil_maps, frames, auxiliary, scaled_dual)))
    image = exchange(packed, "row")
    lines, own, turn, packed = lax.optimization_barrier((lines, own, turn, packed))
    turn = lax.dynamic_slice_in_dim(turn, lax.axis_index("row") * ROWS, ROWS, 1)
    turn = jnp.broadcast_to(turn[:, None, :, None], (2, PHASES, ROWS, LANES)).reshape(2, LINES, LANES)
    packed, residual = pack_measured(own, turn, lines, 0, MAIN)
    packed, late_sampling = lax.optimization_barrier((packed, sampling))
    acquired = late_sampling.reshape(PHASES, ROW_SHARDS, ROWS)
    by_phase = jnp.sum(acquired, 2, keepdims=True)
    number = jnp.cumsum(acquired, 2) + jnp.cumsum(by_phase, 0) - by_phase
    overflow = jnp.max(number) > MAIN

    def more(carry):
        window, index = windows(number, acquired, MAIN, EXTRA)
        maps = receive(image)[0]
        extra = exchange(pack_measured(own, turn, lines, MAIN, EXTRA)[0], "row")
        residual, _, _ = adjoint(window, line_tables(index, table), maps, extra, carry[1])
        return jnp.array(False), residual

    _, residual = lax.while_loop(lambda carry: carry[0], more, (overflow, residual))
    packed, residual = lax.optimization_barrier((packed, residual))
    received = exchange(packed, "row")

    grams = in_hbm(gram_tables(late_sampling.astype(F32)[:, None, :], table))
    maps, frames_cols, splits, first, last = receive(image)
    frames_before, frames_after = shift(last, 1), shift(first, -1)
    residual = in_hbm(start(grams, maps, frames_cols, splits, residual))

    window, index = windows(number, acquired, 0, MAIN)
    line_table = in_hbm(line_tables(index, table))
    residual, first, last = adjoint(
        window, line_table, maps, received, residual, frames_before, frames_after
    )

    residual_before = shift(last, 1)
    residual_after = shift(first, -1)
    grams_residual = gram_apply(grams, maps, residual)
    product, first, last, sums = normal(residual, grams_residual, residual_before, residual_after)
    product_after = shift(first, -1)
    shared = share(sums, curvature(grams, maps, product), last, product_after)
    shared = exchange(shared, ("phase", "row"))
    back = solve(shared, frames_cols, residual, product, frames_after, residual_after, product_after)
    new_frames, new_aux, new_dual, gaps = finish(exchange(back, "row"), auxiliary, scaled_dual)
    gaps = jnp.sum(exchange(gaps, ("phase", "row"))[:, 0, :2], 0)
    residual_norms = jnp.sqrt(gaps) * jnp.array([1.0, PENALTY], F32)
    return new_frames, new_aux, new_dual, residual_norms


def solution(mesh):
    image = P(None, "phase", "row", None)
    in_specs = (
        image,
        image,
        image,
        P(None, None, "row", None),
        P(None, None, "phase", "row", None),
        P("phase", None),
    )
    return jax.shard_map(
        local, mesh=mesh, in_specs=in_specs, out_specs=(image, image, image, P()), check_vma=False
    )
```

```python
import functools
import math

import jax
import jax.numpy as jnp
import numpy as np
from jax import lax
from jax.experimental import pallas as pl
from jax.experimental.pallas import tpu as pltpu
from jax.sharding import PartitionSpec as P

PENALTY = 0.5
DAMPING = 0.1
THRESHOLD = 1.0

COILS = 16
PHASES = 8
ROWS = 16
SIZE = 256
LANES = 128
GROUP = 16
FOLD = 32
LINES = PHASES * ROWS
MAIN = 88
EXTRA = LINES - MAIN
IMAGE = 4 * ROWS
ROW_SHARDS = 16
PHASE_SHARDS = 8
ALL = ROW_SHARDS * PHASE_SHARDS

IN_VMEM = pl.BlockSpec(memory_space=pltpu.VMEM)

F32 = jnp.float32
BF16 = jnp.bfloat16


def lane_bit(rows, bit):
    lane = lax.broadcasted_iota(jnp.int32, (rows, LANES), 1)
    return (lane & (GROUP << bit)) != 0


def lane_group(rows):
    return lax.broadcasted_iota(jnp.int32, (rows, LANES), 1) // GROUP


def roll(value, groups):
    groups %= 8
    if groups == 0:
        return value
    return pltpu.roll(value, groups * GROUP, 1)


def gather_coils(halves):
    rows = halves[0][0].shape[0]
    lane = lax.broadcasted_iota(jnp.int32, (rows, LANES), 1)
    turned = []
    for c, (low, high) in enumerate(halves):
        if c >= 8:
            low, high = high, low
        shift = c % 8
        if shift:
            low, high = roll(low, shift), roll(high, shift)
            wrapped = lane < shift * GROUP
            low, high = jnp.where(wrapped, high, low), jnp.where(wrapped, low, high)
        turned.append((low, high))
    for bit in range(3):
        mask = lane_bit(rows, bit)
        turned = [
            tuple(jnp.where(mask, turned[(i + (1 << bit)) % 16][h], turned[i][h]) for h in range(2))
            for i in range(16)
        ]
    turned = [(turned[i][0], turned[(i + 8) % 16][1]) for i in range(16)]
    return [turned[(-j) % 16] for j in range(16)]


def transpose_groups(values):
    rows = values[0].shape[0]
    turned = [roll(value, a) for a, value in enumerate(values)]
    for bit in range(3):
        mask = lane_bit(rows, bit)
        turned = [jnp.where(mask, turned[(i + (1 << bit)) % 8], turned[i]) for i in range(8)]
    return [roll(turned[(-b) % 8], -b) for b in range(8)]


def spread_half(value, half):
    rows = value.shape[0]
    turned = pltpu.roll(value, 4 * GROUP, 1)
    low = ~lane_bit(rows, 2)
    values = [jnp.where(low == (half == 0), value, turned)]
    for bit in (1, 0):
        low = ~lane_bit(rows, bit)
        spread = []
        for value in values:
            turned = pltpu.roll(value, GROUP << bit, 1)
            spread += [jnp.where(low, value, turned), jnp.where(low, turned, value)]
        values = spread
    return values


def sum_four(values):
    rows = values[0].shape[0]
    for bit in range(2):
        low = ~lane_bit(rows, bit)
        values = [
            jnp.where(low, a, b) + pltpu.roll(jnp.where(low, b, a), GROUP << bit, 1)
            for a, b in zip(values[::2], values[1::2])
        ]
    return values[0] + pltpu.roll(values[0], 4 * GROUP, 1)


def fold_phase(value, phase):
    group = lane_group(FOLD)
    out = None
    for i in range(8):
        piece = roll(value[i * FOLD : (i + 1) * FOLD], i - phase)
        out = piece if out is None else jnp.where(group == i, piece, out)
    return out


def unfold_phase(value, phase, i):
    return roll(value, phase - i)


def split(value):
    high = value.astype(BF16)
    return high, (value - high.astype(F32)).astype(BF16)


def dot(a, b):
    return jnp.dot(a, b, preferred_element_type=F32)


def dot3(table, value):
    return dot(table[0], value[0]) + (dot(table[0], value[1]) + dot(table[1], value[0]))


def wide(value):
    return jnp.concatenate([value, value], 1)


def images_of(maps_ref, at, real, imag):
    maps_real, maps_imag = maps_at(maps_ref, at)
    real, imag = wide(real), wide(imag)
    return maps_real * real - maps_imag * imag, maps_real * imag + maps_imag * real


def maps_at(maps_ref, at):
    return maps_ref[0, at], maps_ref[1, at]


def combine(maps_real, maps_imag, real, imag):
    out_real = maps_real * real + maps_imag * imag
    out_imag = maps_real * imag - maps_imag * real
    return out_real[:, :LANES] + out_real[:, LANES:], out_imag[:, :LANES] + out_imag[:, LANES:]


def row_pairs(step):
    half = SIZE // 2
    return [
        (slice(row, row + step), slice(half + row, half + row + step)) for row in range(0, half, step)
    ]


def store_split(ref, which, at, value):
    ref[which, at], ref[which + 1, at] = split(value)


def expand(vector_ref, maps_ref, pieces):
    half = pl.program_id(0)
    for near, far in row_pairs(32):
        values = [
            [spread_half(vector_ref[part, at], half) for part in range(2)] for at in (near, far)
        ]
        for t in range(4):
            real, imag = images_of(maps_ref, near, values[0][0][t], values[0][1][t])
            far_real, far_imag = images_of(maps_ref, far, values[1][0][t], values[1][1][t])
            store_split(pieces[t], 0, near, real + far_real)
            store_split(pieces[t], 0, far, imag - far_imag)
            store_split(pieces[t], 2, near, imag + far_imag)
            store_split(pieces[t], 2, far, far_real - real)


def reduce(maps_ref, backs, finish):
    for near, far in row_pairs(32):
        near_maps, far_maps = maps_at(maps_ref, near), maps_at(maps_ref, far)
        near_terms, far_terms = [], []
        for t in range(4):
            p_even, p_odd, q_even, q_odd = (
                backs[t][which, at] for which in range(2) for at in (near, far)
            )
            near_terms.append(combine(*near_maps, p_even - q_odd, q_even + p_odd))
            far_terms.append(combine(*far_maps, p_even + q_odd, q_even - p_odd))
        for at, terms in ((near, near_terms), (far, far_terms)):
            finish(at, *(sum_four([term[part] for term in terms]) for part in range(2)))


def products(tables_ref, pieces, backs):
    for t in range(4):
        high, low = tables_ref[t, 0], tables_ref[t, 1]
        for which in range(2):
            value_high, value_low = pieces[t][2 * which], pieces[t][2 * which + 1]
            backs[t][which] = dot(high, value_high) + dot(high, value_low) + dot(low, value_high)


def in_step(rows):
    return lane_bit(rows, 2) == (pl.program_id(0) == 1)


def split_three(value):
    high = value.astype(BF16)
    value = value - high.astype(F32)
    middle = value.astype(BF16)
    return high, middle, (value - middle.astype(F32)).astype(BF16)


def compact(weight_ref, turn_ref, in_ref, lines_ref, base, at_step):
    count = lines_ref.shape[2]
    weight = jnp.broadcast_to(weight_ref[...], (8, LINES))
    row = lax.broadcasted_iota(jnp.int32, (LINES, LINES), 0)
    col = lax.broadcasted_iota(jnp.int32, (LINES, LINES), 1)
    upto = jnp.where(row <= col, 1.0, 0.0).astype(BF16)
    number = dot(weight.astype(BF16), upto).astype(jnp.int32)
    number = jnp.broadcast_to(number[:1], (count, LINES))
    acquired = jnp.broadcast_to(weight_ref[...], (count, LINES)) > 0.5
    line = lax.broadcasted_iota(jnp.int32, (count, LINES), 0) + (base + 1)
    select = jnp.where((number == line) & acquired, 1.0, 0.0).astype(BF16)
    step = in_ref.shape[0]
    cos, sin = (jnp.concatenate([turn_ref[i]] * 2, 1) for i in range(2))
    for c in range(step):
        real, imag = in_ref[c, 0], in_ref[c, 1]
        for part, value in enumerate((real * cos - imag * sin, real * sin + imag * cos)):
            high, middle, low = split_three(value)
            lines_ref[part, at_step * step + c] = (
                dot(select, high) + dot(select, middle) + dot(select, low)
            )


def pack_lines(lines_ref, out_ref):
    count = lines_ref.shape[2]
    for part in range(2):
        for row in range(0, count, 8):
            at = slice(row, row + 8)
            to = slice(part * count + row, part * count + row + 8)
            halves = [
                (lines_ref[part, c, at, :LANES], lines_ref[part, c, at, LANES:]) for c in range(COILS)
            ]
            for j, (low, high) in enumerate(gather_coils(halves)):
                out_ref[j, to, :LANES] = low
                out_ref[j, to, LANES:] = high


def pack_image_kernel(maps_ref, frames_ref, aux_ref, dual_ref, out_ref):
    for part in range(2):
        to = slice(part * 8, (part + 1) * 8)
        halves = [(maps_ref[c, part, :, :LANES], maps_ref[c, part, :, LANES:]) for c in range(COILS)]
        for j, (low, high) in enumerate(gather_coils(halves)):
            out_ref[j, to, :LANES] = low
            out_ref[j, to, LANES:] = high
        for half in range(2):
            cols = slice(half * LANES, (half + 1) * LANES)
            frames = [frames_ref[part, t, :, cols] for t in range(PHASES)]
            splits = [aux_ref[part, t, :, cols] - dual_ref[part, t, :, cols] for t in range(PHASES)]
            lanes = slice(part * LANES, (part + 1) * LANES)
            for which, values in ((2, frames), (3, splits)):
                to_rows = slice(which * 8, (which + 1) * 8)
                for jj, value in enumerate(transpose_groups(values)):
                    out_ref[half * 8 + jj, to_rows, lanes] = value


def whole_spec(value):
    return pl.BlockSpec(value.shape, lambda *_: (0,) * len(value.shape))


def pack_image(coil_maps, *images):
    rows = pl.BlockSpec((2, PHASES, 8, SIZE), lambda i: (0, 0, i, 0))
    return pl.pallas_call(
        pack_image_kernel,
        grid=(ROWS // 8,),
        in_specs=[pl.BlockSpec((COILS, 2, 8, SIZE), lambda i: (0, 0, i, 0))] + [rows] * 3,
        out_specs=pl.BlockSpec((ROW_SHARDS, 32, SIZE), lambda i: (0, i, 0)),
        out_shape=jax.ShapeDtypeStruct((ROW_SHARDS, IMAGE, SIZE), F32),
        compiler_params=params(),
        name="pack_image",
    )(coil_maps, *images)


PACK_STEPS = 4


def pack_measured_kernel(base, weight_ref, turn_ref, in_ref, out_ref, zero_ref, lines_ref):
    step = pl.program_id(0)
    compact(weight_ref, turn_ref, in_ref, lines_ref, base, step)

    @pl.when(step == PACK_STEPS - 1)
    def _():
        pack_lines(lines_ref, out_ref)
        zero_ref[...] = jnp.zeros_like(zero_ref)


def pack_measured(weight, turn, measured, base, count):
    return pl.pallas_call(
        functools.partial(pack_measured_kernel, base),
        grid=(PACK_STEPS,),
        in_specs=[
            whole_spec(weight),
            whole_spec(turn),
            pl.BlockSpec((COILS // PACK_STEPS, 2, LINES, SIZE), lambda i: (i, 0, 0, 0)),
        ],
        out_specs=[pl.BlockSpec((ROW_SHARDS, 2 * count, SIZE), lambda i: (0, 0, 0)), VECTOR_SPEC],
        out_shape=[jax.ShapeDtypeStruct((ROW_SHARDS, 2 * count, SIZE), F32), VECTOR],
        scratch_shapes=[pltpu.VMEM((2, COILS, count, SIZE), F32)],
        compiler_params=params(),
        name=f"pack_measured_{base}",
    )(weight, turn, measured)


def line_table_kernel(index_ref, tables_ref, out_ref):
    row = lax.broadcasted_iota(jnp.int32, (SIZE, SIZE), 0)
    select = jnp.where(row == index_ref[0], 1.0, 0.0).astype(BF16)
    for i in range(2):
        out_ref[0, i] = dot(tables_ref[i], select).astype(BF16)


def line_tables(index, tables):
    return pl.pallas_call(
        line_table_kernel,
        grid=(PHASES,),
        in_specs=[pl.BlockSpec((1, 1, SIZE), lambda t: (t, 0, 0)), whole_spec(tables)],
        out_specs=pl.BlockSpec((1, 2, SIZE, SIZE), lambda t: (t, 0, 0, 0)),
        out_shape=jax.ShapeDtypeStruct((PHASES, 2, SIZE, SIZE), BF16),
        compiler_params=params(),
        name="line_tables",
    )(index, tables)


def reverse_eight(value):
    row = lax.broadcasted_iota(jnp.int32, value.shape, 0)
    value = pltpu.roll(value, 4, 0)
    for bit in (2, 1):
        value = jnp.where((row & bit) != 0, pltpu.roll(value, bit, 0), pltpu.roll(value, 8 - bit, 0))
    return value


def receive_kernel(image_ref, maps_ref, frames_ref, splits_ref, first_ref, last_ref):
    for part in range(2):
        lanes = slice(part * LANES, (part + 1) * LANES)
        for block in range(ROW_SHARDS):
            turned = block >= ROW_SHARDS // 2
            source = ROW_SHARDS + ROW_SHARDS // 2 - 1 - block if turned else block
            for half in range(2):
                row = block * ROWS + half * 8
                at = slice(row, row + 8)
                start = 32 * (1 - half if turned else half)
                maps, frames, splits = (
                    image_ref[source, start + which * 8 : start + (which + 1) * 8, columns]
                    for which, columns in ((part, slice(0, SIZE)), (2, lanes), (3, lanes))
                )
                if turned:
                    maps, frames, splits = (reverse_eight(v) for v in (maps, frames, splits))
                maps_ref[part, at] = maps
                frames_ref[part, at] = frames
                splits_ref[part, at] = splits
        first_ref[part] = fold_phase(frames_ref[part], 0)
        last_ref[part] = fold_phase(frames_ref[part] + splits_ref[part], PHASES - 1)


def receive(image):
    return pl.pallas_call(
        receive_kernel,
        grid=(1,),
        in_specs=[IMAGE_SPEC],
        out_specs=[MAPS_SPEC, VECTOR_SPEC, VECTOR_SPEC, FOLDED_SPEC, FOLDED_SPEC],
        out_shape=[jax.ShapeDtypeStruct((2, SIZE, SIZE), F32), VECTOR, VECTOR, FOLDED, FOLDED],
        compiler_params=params(),
        name="receive",
    )(image)


def gram_table_kernel(weight_ref, tables_ref, out_ref):
    weight = weight_ref[0]
    left = tuple((tables_ref[i].astype(F32) * weight).astype(BF16) for i in range(2))
    right = tables_ref[2], tables_ref[3]
    out_ref[0, 0], out_ref[0, 1] = split(dot3(left, right))


def gram_tables(weight, tables):
    return pl.pallas_call(
        gram_table_kernel,
        grid=(PHASES,),
        in_specs=[
            pl.BlockSpec((1, 1, SIZE), lambda t: (t, 0, 0)),
            pl.BlockSpec((4, SIZE, SIZE), lambda t: (0, 0, 0)),
        ],
        out_specs=pl.BlockSpec((1, 2, SIZE, SIZE), lambda t: (t, 0, 0, 0)),
        out_shape=jax.ShapeDtypeStruct((PHASES, 2, SIZE, SIZE), BF16),
        compiler_params=params(),
        name="gram_tables",
    )(weight, tables)


GRAM_SPEC = pl.BlockSpec((4, 2, SIZE, SIZE), lambda i, *_: (i, 0, 0, 0))
IMAGE_SPEC = pl.BlockSpec((ROW_SHARDS, IMAGE, SIZE), lambda *_: (0, 0, 0))
MAPS_SPEC = pl.BlockSpec((2, SIZE, SIZE), lambda *_: (0, 0, 0))
VECTOR_SPEC = pl.BlockSpec((2, SIZE, LANES), lambda *_: (0, 0, 0))
VECTOR = jax.ShapeDtypeStruct((2, SIZE, LANES), F32)
FOLDED_SPEC = pl.BlockSpec((2, FOLD, LANES), lambda *_: (0, 0, 0))
FOLDED = jax.ShapeDtypeStruct((2, FOLD, LANES), F32)
SUMS_SPEC = pl.BlockSpec((4, 8, LANES), lambda i: (0, 0, 0))
PIECES = [pltpu.VMEM((4, SIZE, SIZE), BF16)] * 4
BACKS = [pltpu.VMEM((2, SIZE, SIZE), F32)] * 4


def params():
    return pltpu.CompilerParams(vmem_limit_bytes=16 << 20)


def start_kernel(gram_ref, maps_ref, frames_ref, splits_ref, in_ref, out_ref, *scratch):
    pieces, backs = scratch[:4], scratch[4:]

    @pl.when(pl.program_id(0) == 0)
    def _():
        group = lane_group(FOLD)
        for row in range(0, SIZE, FOLD):
            at = slice(row, row + FOLD)
            for part in range(2):
                frames, splits = frames_ref[part, at], splits_ref[part, at]
                ahead = pltpu.roll(frames, LANES - GROUP, 1)
                behind = pltpu.roll(frames + splits, GROUP, 1)
                gap = splits - (jnp.where(group == PHASES - 1, 0.0, ahead) - frames)
                gap_behind = jnp.where(group == 0, 0.0, behind) - frames
                out_ref[part, at] = in_ref[part, at] + PENALTY * (gap_behind - gap) - DAMPING * frames

    expand(frames_ref, maps_ref, pieces)
    products(gram_ref, pieces, backs)

    def finish(at, real, imag):
        keep = in_step(at.stop - at.start)
        for part, value in enumerate((real, imag)):
            out_ref[part, at] -= jnp.where(keep, value, 0.0)

    reduce(maps_ref, backs, finish)


def start(grams, maps, frames, splits, so_far):
    return pl.pallas_call(
        start_kernel,
        grid=(2,),
        in_specs=[GRAM_SPEC] + [IN_VMEM] * 4,
        out_specs=VECTOR_SPEC,
        out_shape=VECTOR,
        scratch_shapes=PIECES + BACKS,
        compiler_params=params(),
        name="start",
    )(grams, maps, frames, splits, so_far)


def add_edges(before_ref, after_ref, in_ref, out_ref):
    group = lane_group(FOLD)
    for i in range(8):
        at = slice(i * FOLD, (i + 1) * FOLD)
        for part in range(2):
            before = unfold_phase(before_ref[part], 0, i)
            after = unfold_phase(after_ref[part], PHASES - 1, i)
            edge = jnp.where(group == 0, before, jnp.where(group == PHASES - 1, after, 0.0))
            out_ref[part, at] = in_ref[part, at] + PENALTY * edge


def adjoint_kernel(edges, window_ref, tables_ref, maps_ref, lines_ref, in_ref, *refs):
    edges_in, refs = refs[:edges], refs[edges:]
    out_ref, first_ref, last_ref = refs[:3]
    pieces, backs = refs[3:7], refs[7:]
    half = pl.program_id(0)
    count = lines_ref.shape[1] // 2

    @pl.when(half == 0)
    def _():
        if edges:
            add_edges(*edges_in, in_ref, out_ref)
        else:
            out_ref[...] = in_ref[...]

    for t in range(4):
        for block in range(ROW_SHARDS):
            at = slice(block * ROWS, (block + 1) * ROWS)
            start = window_ref[(half * 4 + t) * ROW_SHARDS + block]
            aligned = jnp.minimum(start // 8, (count - ROWS) // 8 - 1) * 8
            turn = lax.rem(ROWS + 8 - (start - aligned), ROWS + 8)
            for part in range(2):
                rows = pl.ds(pl.multiple_of(part * count + aligned, 8), ROWS + 8)
                rows = pltpu.roll(lines_ref[block, rows], turn, 0)
                store_split(pieces[t], 2 * part, at, rows[:ROWS])
    products(tables_ref, pieces, backs)

    def finish(at, real, imag):
        keep = in_step(at.stop - at.start)
        for which, value in enumerate((real, imag)):
            out_ref[which, at] += jnp.where(keep, value, 0.0)

    reduce(maps_ref, backs, finish)

    @pl.when(half == 1)
    def _():
        for which in range(2):
            value = out_ref[which]
            first_ref[which] = fold_phase(value, 0)
            last_ref[which] = fold_phase(value, PHASES - 1)


def adjoint(window, tables, maps, lines, so_far, *edges):
    return pl.pallas_call(
        functools.partial(adjoint_kernel, len(edges)),
        grid_spec=pltpu.PrefetchScalarGridSpec(
            num_scalar_prefetch=1,
            grid=(2,),
            in_specs=[GRAM_SPEC] + [IN_VMEM] * (3 + len(edges)),
            out_specs=[IN_VMEM] * 3,
            scratch_shapes=PIECES + BACKS,
        ),
        out_shape=[VECTOR, FOLDED, FOLDED],
        compiler_params=params(),
        name="adjoint",
    )(window, tables, maps, lines, so_far, *edges)


def gram_kernel(gram_ref, maps_ref, in_ref, out_ref, *scratch):
    pieces, backs = scratch[:4], scratch[4:]
    expand(in_ref, maps_ref, pieces)
    products(gram_ref, pieces, backs)

    def finish(at, real, imag):
        keep = in_step(at.stop - at.start)
        for part, value in enumerate((real, imag)):
            out_ref[part, at] = jnp.where(keep, value, out_ref[part, at])

    reduce(maps_ref, backs, finish)


def gram_apply(grams, maps, vector):
    return pl.pallas_call(
        gram_kernel,
        grid=(2,),
        in_specs=[GRAM_SPEC, IN_VMEM, IN_VMEM],
        out_specs=IN_VMEM,
        out_shape=VECTOR,
        scratch_shapes=PIECES + BACKS,
        compiler_params=params(),
        name="gram_apply",
    )(grams, maps, vector)


def fold(value):
    return jnp.sum(value.reshape(-1, 8, LANES), 0)


def normal_kernel(
    first_ref, gram_ref, before_ref, after_ref, image_ref, first_edge_ref, last_edge_ref, sums_ref
):
    rr = rw = ww = dd = 0.0
    group = lane_group(FOLD)
    for part in range(2):
        for i in range(8):
            at = slice(i * FOLD, (i + 1) * FOLD)
            value = first_ref[part, at]
            behind = jnp.where(
                group == 0, unfold_phase(before_ref[part], 0, i), pltpu.roll(value, GROUP, 1)
            )
            ahead = jnp.where(
                group == PHASES - 1,
                unfold_phase(after_ref[part], PHASES - 1, i),
                pltpu.roll(value, LANES - GROUP, 1),
            )
            image = (
                gram_ref[part, at]
                + PENALTY * ((value - behind) - (ahead - value))
                + DAMPING * value
            )
            image_ref[part, at] = image
            rr += fold(value * value)
            rw += fold(value * image)
            ww += fold(image * image)
            step = pltpu.roll(image, LANES - GROUP, 1) - image
            dd += fold(jnp.where(group == PHASES - 1, 0.0, step * step))
        whole = image_ref[part]
        first_edge_ref[part] = fold_phase(whole, 0)
        last_edge_ref[part] = fold_phase(whole, PHASES - 1)
    for i, value in enumerate((rr, rw, ww, dd)):
        sums_ref[i] = value


def normal(first, grams_first, before, after):
    return pl.pallas_call(
        normal_kernel,
        grid=(1,),
        in_specs=[IN_VMEM] * 4,
        out_specs=[IN_VMEM] * 4,
        out_shape=[
            VECTOR,
            FOLDED,
            FOLDED,
            jax.ShapeDtypeStruct((4, 8, LANES), F32),
        ],
        compiler_params=params(),
        name="normal",
    )(first, grams_first, before, after)


def curvature_kernel(gram_ref, maps_ref, in_ref, out_ref, *scratch):
    pieces, backs = scratch[:4], scratch[4:]

    @pl.when(pl.program_id(0) == 0)
    def _():
        out_ref[...] = jnp.zeros_like(out_ref)

    expand(in_ref, maps_ref, pieces)
    products(gram_ref, pieces, backs)
    total = 0.0
    for row in range(0, SIZE, 32):
        at = slice(row, row + 32)
        for t in range(4):
            p_high, p_low, q_high, q_low = (pieces[t][i, at].astype(F32) for i in range(4))
            both = (p_high + p_low) * backs[t][0, at] + (q_high + q_low) * backs[t][1, at]
            total += fold(both[:, :LANES] + both[:, LANES:])
    out_ref[...] += total


def curvature(grams, maps, vector):
    return pl.pallas_call(
        curvature_kernel,
        grid=(2,),
        in_specs=[GRAM_SPEC, IN_VMEM, IN_VMEM],
        out_specs=IN_VMEM,
        out_shape=jax.ShapeDtypeStruct((8, LANES), F32),
        scratch_shapes=PIECES + BACKS,
        compiler_params=params(),
        name="curvature",
    )(grams, maps, vector)


def lane_row(values):
    lane = lax.broadcasted_iota(jnp.int32, (1, LANES), 1)
    row = jnp.zeros((1, LANES), F32)
    for i, value in enumerate(values):
        row = jnp.where(lane == i, value, row)
    return row


def whole_sum(value):
    return jnp.sum(jnp.sum(value, 0, keepdims=True), 1, keepdims=True)


def share_kernel(sums_ref, curve_ref, last_ref, after_ref, out_ref):
    rr, rw, ww, dd = (whole_sum(sums_ref[i]) for i in range(4))
    edge = 0.0
    for part in range(2):
        step = after_ref[part] - last_ref[part]
        edge = edge + fold(step * step)
    curve = whole_sum(curve_ref[...]) + PENALTY * (dd + whole_sum(edge)) + DAMPING * ww
    row = lane_row((rr, rw, ww, curve))
    out_ref[...] = jnp.broadcast_to(row[None], out_ref.shape)


def share(sums, curve, last, after):
    return pl.pallas_call(
        share_kernel,
        grid=(1,),
        in_specs=[IN_VMEM] * 4,
        out_specs=pl.BlockSpec((ALL, 1, LANES), lambda i: (0, 0, 0)),
        out_shape=jax.ShapeDtypeStruct((ALL, 1, LANES), F32),
        compiler_params=params(),
        name="share",
    )(sums, curve, last, after)


def solve_kernel(
    shared_ref, frames_ref, residual_ref, product_ref, frames_after_ref, residual_after_ref, product_after_ref, out_ref
):
    row = jnp.sum(shared_ref[...], 0)
    rr, rw, ww, curve = (row[:, i : i + 1] for i in range(4))
    alpha = rr / rw
    fresh = rr - 2.0 * alpha * rw + alpha * alpha * ww
    beta = fresh / rr
    gamma = 1.0 + beta
    bend = gamma * gamma * rw - 2.0 * gamma * alpha * ww + alpha * alpha * curve
    second = fresh / bend
    by_first = alpha + second * gamma
    by_image = -second * alpha
    group = lane_group(8)
    for j in range(ROW_SHARDS):
        turned = j >= ROW_SHARDS // 2
        block = ROW_SHARDS + ROW_SHARDS // 2 - 1 - j if turned else j
        edges = jnp.zeros((8, LANES), F32)
        for row in range(0, ROWS, 8):
            at = slice(block * ROWS + row, block * ROWS + row + 8)
            piece, start = divmod(at.start, FOLD)
            folded = slice(start, start + 8)
            to = ROWS - 8 - row if turned else row
            for part in range(2):
                value = (
                    frames_ref[part, at]
                    + by_first * residual_ref[part, at]
                    + by_image * product_ref[part, at]
                )
                place = 2 * part + to // 8
                edge = roll(
                    frames_after_ref[part, folded]
                    + by_first * residual_after_ref[part, folded]
                    + by_image * product_after_ref[part, folded],
                    place - piece,
                )
                if turned:
                    value, edge = reverse_eight(value), reverse_eight(edge)
                out_ref[j, part * ROWS + to : part * ROWS + to + 8] = value
                edges = jnp.where(group == place, edge, edges)
        out_ref[j, 2 * ROWS : 2 * ROWS + 8] = edges


def solve(shared, frames, residual, product, frames_after, residual_after, product_after):
    return pl.pallas_call(
        solve_kernel,
        grid=(1,),
        in_specs=[IN_VMEM] * 7,
        out_specs=pl.BlockSpec((ROW_SHARDS, 2 * ROWS + 8, LANES), lambda i: (0, 0, 0)),
        out_shape=jax.ShapeDtypeStruct((ROW_SHARDS, 2 * ROWS + 8, LANES), F32),
        compiler_params=params(),
        name="solve",
    )(shared, frames, residual, product, frames_after, residual_after, product_after)


def finish_kernel(in_ref, aux_ref, dual_ref, x_ref, new_aux_ref, new_dual_ref, out_ref):
    primal = dual_sum = 0.0
    group = lane_group(8)
    for row in range(0, ROWS, 8):
        at = slice(row, row + 8)
        for half in range(2):
            cols = slice(half * LANES, (half + 1) * LANES)
            parts = []
            for part in range(2):
                rows = slice(part * ROWS + row, part * ROWS + row + 8)
                blocks = [in_ref[half * 8 + jj, rows] for jj in range(8)]
                values = transpose_groups(blocks)
                after = None
                for jj in range(8):
                    place = 2 * part + row // 8
                    piece = roll(in_ref[half * 8 + jj, 2 * ROWS : 2 * ROWS + 8], jj - place)
                    after = piece if after is None else jnp.where(group == jj, piece, after)
                for t in range(PHASES):
                    x_ref[part, t, at, cols] = values[t]
                parts.append(values + [after])
            for t in range(PHASES):
                dual = [dual_ref[part, t, at, cols] for part in range(2)]
                shifted = [parts[part][t + 1] - parts[part][t] + dual[part] for part in range(2)]
                magnitude = jnp.sqrt(shifted[0] * shifted[0] + shifted[1] * shifted[1])
                factor = jnp.maximum(magnitude - THRESHOLD, 0.0) / jnp.maximum(magnitude, THRESHOLD)
                for part in range(2):
                    new_aux = shifted[part] * factor
                    new_dual = shifted[part] - new_aux
                    new_aux_ref[part, t, at, cols] = new_aux
                    new_dual_ref[part, t, at, cols] = new_dual
                    gap = new_dual - dual[part]
                    primal += gap * gap
                    gap = new_aux - aux_ref[part, t, at, cols]
                    dual_sum += gap * gap
    sums = lane_row((whole_sum(primal), whole_sum(dual_sum)))
    out_ref[...] = jnp.broadcast_to(sums[None], out_ref.shape)


def finish(back, auxiliary, scaled_dual):
    image = jax.ShapeDtypeStruct(auxiliary.shape, F32)
    return pl.pallas_call(
        finish_kernel,
        grid=(1,),
        in_specs=[whole_spec(value) for value in (back, auxiliary, scaled_dual)],
        out_specs=[whole_spec(image)] * 3 + [pl.BlockSpec((ALL, 1, LANES), lambda i: (0, 0, 0))],
        out_shape=[image, image, image, jax.ShapeDtypeStruct((ALL, 1, LANES), F32)],
        compiler_params=params(),
        name="finish",
    )(back, auxiliary, scaled_dual)


def tables():
    k = np.arange(SIZE)
    x = np.arange(SIZE // 2)
    unit = 2.0 * math.pi / (2 * SIZE)
    angle = (k[None, :] * (2 * x[:, None] - (SIZE - 1)) % (2 * SIZE)) * unit
    table = (np.concatenate([np.cos(angle), np.sin(angle)]) / math.sqrt(SIZE)).astype(np.float32)
    high = table.astype(BF16)
    low = (table - high.astype(np.float32)).astype(BF16)
    turn = (k * (SIZE - 1) % (2 * SIZE)) * unit
    turn = np.stack([np.cos(turn), np.sin(turn)]).astype(np.float32)
    return np.stack([high, low, high.T, low.T]), turn


def shift(value, steps):
    pairs = [(i, (i + steps) % PHASE_SHARDS) for i in range(PHASE_SHARDS)]
    return lax.ppermute(value, "phase", pairs)


def exchange(value, axes):
    return lax.all_to_all(value, axes, 0, 0, tiled=True)


def windows(number, acquired, base, count):
    before = number[:, :, :1] - acquired[:, :, :1] - base
    window = jnp.clip(before, 0, count - ROWS)
    place = lax.broadcasted_iota(jnp.int32, (1, 1, 1, ROWS), 3)
    match = (acquired > 0)[..., None] & (number[..., None] - (1 + base) == window[..., None] + place)
    match = match & (number[..., None] > base) & (number[..., None] <= base + count)
    k = lax.broadcasted_iota(jnp.int32, (1, ROW_SHARDS, ROWS, 1), 1) * ROWS
    k = k + lax.broadcasted_iota(jnp.int32, (1, ROW_SHARDS, ROWS, 1), 2)
    index = jnp.sum(jnp.where(match, k + 1, 0), 2) - 1
    return window.reshape(PHASES * ROW_SHARDS), index.reshape(PHASES, 1, SIZE)


def in_hbm(value):
    return pltpu.with_memory_space_constraint(value, pltpu.HBM)


def local(frames, auxiliary, scaled_dual, coil_maps, measured, sampling):
    table, turn = (jnp.asarray(value) for value in tables())
    lines = measured.reshape(COILS, 2, LINES, SIZE)
    own = lax.dynamic_slice_in_dim(sampling, lax.axis_index("row") * ROWS, ROWS, 1)
    own = own.astype(F32).reshape(1, LINES)

    packed = pack_image(*(in_hbm(v) for v in (coil_maps, frames, auxiliary, scaled_dual)))
    image = exchange(packed, "row")
    lines, own, turn, packed = lax.optimization_barrier((lines, own, turn, packed))
    turn = lax.dynamic_slice_in_dim(turn, lax.axis_index("row") * ROWS, ROWS, 1)
    turn = jnp.broadcast_to(turn[:, None, :, None], (2, PHASES, ROWS, LANES)).reshape(2, LINES, LANES)
    packed, residual = pack_measured(own, turn, lines, 0, MAIN)
    packed, late_sampling = lax.optimization_barrier((packed, sampling))
    acquired = late_sampling.reshape(PHASES, ROW_SHARDS, ROWS)
    by_phase = jnp.sum(acquired, 2, keepdims=True)
    number = jnp.cumsum(acquired, 2) + jnp.cumsum(by_phase, 0) - by_phase
    overflow = jnp.max(number) > MAIN

    def more(carry):
        window, index = windows(number, acquired, MAIN, EXTRA)
        maps = receive(image)[0]
        extra = exchange(pack_measured(own, turn, lines, MAIN, EXTRA)[0], "row")
        residual, _, _ = adjoint(window, line_tables(index, table), maps, extra, carry[1])
        return jnp.array(False), residual

    _, residual = lax.while_loop(lambda carry: carry[0], more, (overflow, residual))
    packed, residual = lax.optimization_barrier((packed, residual))
    received = exchange(packed, "row")

    grams = gram_tables(late_sampling.astype(F32)[:, None, :], table)
    maps, frames_cols, splits, first, last = receive(image)
    frames_before, frames_after = shift(last, 1), shift(first, -1)
    residual = in_hbm(start(grams, maps, frames_cols, splits, residual))

    window, index = windows(number, acquired, 0, MAIN)
    line_table = in_hbm(line_tables(index, table))
    residual, first, last = adjoint(
        window, line_table, maps, received, residual, frames_before, frames_after
    )

    residual_before = shift(last, 1)
    residual_after = shift(first, -1)
    grams_residual = gram_apply(grams, maps, residual)
    product, first, last, sums = normal(residual, grams_residual, residual_before, residual_after)
    product_after = shift(first, -1)
    shared = share(sums, curvature(grams, maps, product), last, product_after)
    shared = exchange(shared, ("phase", "row"))
    back = solve(shared, frames_cols, residual, product, frames_after, residual_after, product_after)
    new_frames, new_aux, new_dual, gaps = finish(exchange(back, "row"), auxiliary, scaled_dual)
    gaps = jnp.sum(exchange(gaps, ("phase", "row"))[:, 0, :2], 0)
    residual_norms = jnp.sqrt(gaps) * jnp.array([1.0, PENALTY], F32)
    return new_frames, new_aux, new_dual, residual_norms


def solution(mesh):
    image = P(None, "phase", "row", None)
    in_specs = (
        image,
        image,
        image,
        P(None, None, "row", None),
        P(None, None, "phase", "row", None),
        P("phase", None),
    )
    return jax.shard_map(
        local, mesh=mesh, in_specs=in_specs, out_specs=(image, image, image, P()), check_vma=False
    )
```
